512 devices in a mesh: replica: 16 (over x, z_lo), expert: 32 (over y, z_hi, core).
Axes of the slice: x: 4, y: 8, z: 8 (z_hi: 2, z_lo: 4; z = z_hi * 4 + z_lo), core: 2. Of those that a mesh axis runs over, the one named last changes fastest.
Arguments:
- moe_input: bfloat16 [8192, 2048], P(('replica', 'expert')), may hold values from -6 to 6
- expert_ids: int32 [8192, 8], P(('replica', 'expert')), may hold values from 0 to 127, all different within a row; in each aligned block of 16 rows (0 to 15, 16 to 31, ...) at most 2 rows name the same one
- route_weight: float32 [8192, 8], P(('replica', 'expert')), may hold values from 0.05 to 0.5
- expert_slot: int32 [128], replicated, may hold values from 0 to 127, each once
- w_gate_up: bfloat16 [2048, 196608], P(None, ('replica', 'expert')), may hold values from -0.125 to 0.125
- w_down: bfloat16 [98304, 2048], P(('replica', 'expert')), may hold values from -0.21875 to 0.21875
- queries: bfloat16 [1024, 8192], P(('replica', 'expert')), may hold values from -80 to 80
- incoming_key_value: bfloat16 [1024, 1024], P(('replica', 'expert')), may hold values from -4 to 4
- key_value_pool: bfloat16 [8192, 64, 1024], P(('replica', 'expert')), may hold values from -4 to 4
- block_owner: int32 [8192], P(('replica', 'expert')), may hold values from 0 to 31, as said below
- block_tokens: int32 [8192], P(('replica', 'expert')), may hold values from 1 to 64
Outputs:
- moe_out: bfloat16 [8192, 2048], P(('replica', 'expert'))
- attn_out: bfloat16 [1024, 8192], P(('replica', 'expert'))
The draws below stay inside these ranges and needn't reach their ends.
Inputs may be any that keep to these rules, and one draw needn't show every extreme that they name: `expert_ids`: in the rows of one device no expert is named by more than 2 rows, a bound that some block reaches. `expert_slot`: each slot hosts one expert. `block_owner`: on every device at most 2 blocks are owned by requests of any one other replica, and exactly 2 for some other replica.
All inputs are finite; a program needn't handle non-finite values.
Results may differ from the reference program's by a relative error of at most 0.0058.
Values may be sent and summed in bfloat16 or wider, within the bound.
No kernel may reach another device: no remote copies, remote signals or barrier semaphores. Data moves between devices by JAX's collectives and lax.ppermute only.
A program may use at most 64 MiB of HBM per device.

```python
import math
import jax
import jax.numpy as jnp
import numpy as np
from jax import lax

D = 2048
FFE = 768
QUART = 4
EXPERTS = 128
TOP = 8
TOK_DEV = 16
CAP = 2
TOKENS = 8192
QUERY_HEADS = 64
KEY_VALUE_HEADS = 4
HEAD_DIMENSION = 128
DEVICE_REQUESTS = 2
TOTAL_REQUESTS = 1024
DEVICE_BLOCKS = 16
BLOCK_SLOTS = 64
MIG = 2
TOTAL_BLOCKS = 8192
N_REPLICA = 16
N_EXPERT = 32


def owner_helper(key):
    devices = N_REPLICA * N_EXPERT
    replica_of = jnp.arange(devices, dtype=jnp.int32) // N_EXPERT
    device_keys = jax.random.split(jax.random.fold_in(key, 11), devices)

    def per_device(device_key, replica):
        first, second, third, fourth = jax.random.split(device_key, 4)
        offsets = jax.random.permutation(first, N_REPLICA - 1).astype(jnp.int32) + 1
        query_group = jnp.arange(DEVICE_BLOCKS, dtype=jnp.int32) // MIG
        coin = jax.random.randint(second, (DEVICE_BLOCKS,), 0, 2)
        picked = offsets[jnp.minimum(query_group, N_REPLICA - 2)]
        offset = jnp.where(query_group == 0, offsets[0], jnp.where((query_group < N_REPLICA - 1) & (coin == 1), picked, 0))
        target = (replica + offset) % N_REPLICA
        tail = jax.random.randint(third, (DEVICE_BLOCKS,), 0, 3)
        request = jnp.where(tail == 0, 0, jax.random.randint(fourth, (DEVICE_BLOCKS,), 0, DEVICE_REQUESTS))
        return (target * DEVICE_REQUESTS + request).astype(jnp.int32)
    return jax.vmap(per_device)(device_keys, replica_of).reshape(-1)


def draw_block_owner(key, part):
    return owner_helper(key)


def draw_block_tokens(key, part):
    cached_value_rows = jax.random.randint(jax.random.fold_in(key, 23), (TOTAL_BLOCKS,), 1, BLOCK_SLOTS + 1)
    local = jnp.arange(TOTAL_BLOCKS, dtype=jnp.int32) % DEVICE_BLOCKS
    return jnp.where(local == 0, BLOCK_SLOTS, cached_value_rows).astype(jnp.int32)


def draw_queries(key, part):
    base_offset = jnp.clip(jax.random.normal(jax.random.fold_in(key, 41), (TOTAL_REQUESTS, QUERY_HEADS * HEAD_DIMENSION), jnp.float32), -4.0, 4.0)
    return base_offset.astype(jnp.bfloat16)


def draw_incoming_key_value(key, part):
    base_offset = jnp.clip(jax.random.normal(jax.random.fold_in(key, 43), (TOTAL_REQUESTS, 2 * KEY_VALUE_HEADS * HEAD_DIMENSION), jnp.float32), -4.0, 4.0)
    return base_offset.astype(jnp.bfloat16)


def draw_key_value_pool(key, part):
    base_offset = jnp.clip(jax.random.normal(jax.random.fold_in(key, 47), (TOTAL_BLOCKS, BLOCK_SLOTS, 2 * KEY_VALUE_HEADS * HEAD_DIMENSION), jnp.float32), -4.0, 4.0)
    return base_offset.astype(jnp.bfloat16)


def steps_of(stream_key, extent, shards, low, largest):
    level, own = 1.0, jax.random.fold_in(stream_key, 6)
    for dim, parts in shards:
        draws = jnp.exp(jax.random.uniform(jax.random.fold_in(own, dim), (parts,), jnp.float32, low / len(shards), largest / len(shards)))
        level = level * jnp.repeat(draws, extent[dim] // parts).reshape([-1 if axis == dim else 1 for axis in range(len(extent))])
    return level


def shared_out(stream_key, own, number, rows, number_of, top, bound, lean):
    sequence = jax.random.permutation(stream_key, number_of)
    heavy_load, common = shares(number_of, rows * top, bound, lean, True), shares(number_of, rows * top, bound, lean, False)
    places = jnp.arange(number_of)

    def named(tallies, offset_by):
        used = int((tallies > 0).sum())
        fixed = max(1, used // 4)
        shifted = fixed + (places - fixed + offset_by * (used - fixed)) % max(1, number_of - fixed)
        return jnp.zeros((number_of,), jnp.int32).at[sequence[jnp.where(places < fixed, places, shifted)]].set(jnp.asarray(tallies, jnp.int32))

    tallies = jnp.where(number % 4 == 0, named(heavy_load, number // 4), named(common, number - number // 4 - 1))
    mixed = jax.random.permutation(jax.random.fold_in(own, 3), number_of)
    source_of, taker = mixed[0:number_of // 2 * 2:2], mixed[1:number_of // 2 * 2:2]
    margin = jnp.minimum(tallies[source_of] - 1, bound - tallies[taker]) // 2
    margin = jnp.where((source_of == sequence[0]) | (taker == sequence[0]) | (tallies[taker] == 0), 0, jnp.maximum(margin, 0))
    shifted = jax.random.randint(jax.random.fold_in(own, 4), (number_of // 2,), 0, 1 << 20) % (margin + 1)
    tallies = tallies.at[source_of].add(-shifted).at[taker].add(shifted)
    members = jnp.searchsorted(jnp.cumsum(tallies), jnp.arange(rows * top), side="right").astype(jnp.int32)
    grid = members.reshape(top, rows).T
    grid = grid[jax.random.permutation(jax.random.fold_in(own, 1), rows)]
    offset_by = jax.random.randint(jax.random.fold_in(own, 2), (rows, 1), 0, top)
    return jnp.take_along_axis(grid, (jnp.arange(top)[None, :] + offset_by) % top, axis=1)


def shares(amount, total, limit, lean, full):
    weights = [(1 << 20) // math.isqrt(grade ** lean) + 1 for grade in range(1, amount + 1)]
    largest = limit if full else min(limit, max(-(-total // amount), total * weights[0] // sum(weights)))
    least = 1 if total - largest >= amount - 1 else 0
    holding, spare = [largest] + [least] * (amount - 1), total - largest - least * (amount - 1)
    while spare > 0:
        movable = [i for i in range(1, amount) if holding[i] < largest] or [i for i in range(1, amount) if holding[i] < limit]
        pool, left = sum([weights[i] for i in movable]), spare
        for i in movable:
            extra = min(limit - holding[i], max(1, left * weights[i] // pool), spare)
            holding[i] = holding[i] + extra
            spare = spare - extra
    return np.array(holding)


def normal_values(rng, shape, deviation, most, pieces=(), kind=jnp.bfloat16):
    level = steps_of(rng, shape, pieces, -0.22, 0.18) if pieces else 1.0
    array = jax.random.normal(rng, shape, jnp.float32) * deviation * level
    return jnp.minimum(jnp.maximum(array, -most), most).astype(kind)


def setup_inputs(seed: int = 0) -> dict:
    streams_of = jax.random.split(jax.random.key(seed), 12)
    moe_input = normal_values(streams_of[0], (TOKENS, D), 1.0, 6.0, ((0, 512),))
    expert_ids_keys = jax.random.split(jax.random.fold_in(streams_of[1], 1), TOKENS // TOK_DEV)
    expert_ids_turns = jax.random.permutation(jax.random.fold_in(streams_of[1], 3), TOKENS // TOK_DEV)
    expert_ids = jax.vmap(lambda own, number: shared_out(jax.random.fold_in(streams_of[1], 2), own, number, TOK_DEV, EXPERTS, TOP, CAP, 2))(expert_ids_keys, expert_ids_turns).reshape((TOKENS, TOP))
    route_weight = jnp.clip(jnp.exp(math.log(0.5) - 2.3025851 * jax.random.uniform(streams_of[2], (TOKENS, TOP), jnp.float32) ** steps_of(streams_of[2], (TOKENS, TOP), ((0, 512),), -0.2, 0.2)), 0.05, 0.5)
    expert_slot = jax.random.permutation(streams_of[3], EXPERTS).astype(jnp.int32)
    w_gate_up = normal_values(streams_of[4], (D, 2 * EXPERTS * FFE), D ** -0.5, 0.125, ((1, 512),))
    w_down = normal_values(streams_of[5], (EXPERTS * FFE, D), FFE ** -0.5, 0.21875, ((0, 512),))
    queries = draw_queries(jax.random.fold_in(streams_of[11], 71), 0)
    incoming_key_value = draw_incoming_key_value(jax.random.fold_in(streams_of[11], 71), 0)
    key_value_pool = draw_key_value_pool(jax.random.fold_in(streams_of[11], 71), 0)
    block_owner = draw_block_owner(jax.random.fold_in(streams_of[11], 71), 0)
    block_tokens = draw_block_tokens(jax.random.fold_in(streams_of[11], 71), 0)
    return dict(moe_input=moe_input, expert_ids=expert_ids, route_weight=route_weight, expert_slot=expert_slot, w_gate_up=w_gate_up, w_down=w_down, queries=queries, incoming_key_value=incoming_key_value, key_value_pool=key_value_pool, block_owner=block_owner, block_tokens=block_tokens)


HIGHEST = lax.Precision.HIGHEST

def mixture_reference(moe_input, expert_ids, route_weight, expert_slot, w_gate_up, w_down):
    devices = N_REPLICA * N_EXPERT
    quarter = FFE // QUART
    token_count = moe_input.shape[0]
    ids_by_device = expert_ids.reshape(devices, TOK_DEV * TOP)
    onehot = (ids_by_device[:, :, None] == jnp.arange(EXPERTS, dtype=jnp.int32)[None, None, :]).astype(jnp.int32)
    rank_before = jnp.cumsum(onehot, axis=1) - onehot
    position = lax.optimization_barrier(jnp.sum(rank_before * onehot, axis=2)).astype(jnp.int32)
    source = jnp.broadcast_to(jnp.arange(devices, dtype=jnp.int32)[:, None], ids_by_device.shape)
    token_index = source * TOK_DEV + jnp.arange(TOK_DEV * TOP, dtype=jnp.int32)[None, :] // TOP
    token_table = jnp.full((EXPERTS, devices, CAP), token_count, dtype=jnp.int32)
    token_table = token_table.at[ids_by_device, source, position].set(token_index)
    weight_table = jnp.zeros((EXPERTS, devices, CAP), jnp.float32)
    weight_table = weight_table.at[ids_by_device, source, position].set(route_weight.reshape(devices, TOK_DEV * TOP).astype(jnp.float32))
    hosted = jnp.zeros((EXPERTS,), jnp.int32).at[expert_slot].set(jnp.arange(EXPERTS, dtype=jnp.int32))
    padded = jnp.concatenate([moe_input, jnp.zeros((1, D), moe_input.dtype)], axis=0)
    gate_up_slots = w_gate_up.reshape(D, EXPERTS, QUART * 2 * quarter)
    down_slots = w_down.reshape(EXPERTS, QUART * quarter, D)

    def one_slot(running, slot_index):
        expert = hosted[slot_index]
        row_index = token_table[expert].reshape(-1)
        gathered = padded[row_index]
        halves = jnp.dot(gathered, gate_up_slots[:, slot_index, :], preferred_element_type=jnp.float32)
        halves = halves.reshape(-1, QUART, 2, quarter)
        activation = (jax.nn.silu(halves[:, :, 0]) * halves[:, :, 1]).astype(jnp.bfloat16)
        down_slot = down_slots[slot_index]
        output_sum = jnp.zeros((gathered.shape[0], D), jnp.float32)
        for quarter_id in range(QUART):
            quarter_part = jnp.dot(activation[:, quarter_id], down_slot[quarter_id * quarter:(quarter_id + 1) * quarter], preferred_element_type=jnp.float32).astype(jnp.bfloat16)
            output_sum = output_sum + quarter_part.astype(jnp.float32)
        scaled = output_sum * weight_table[expert].reshape(-1)[:, None]
        return (running.at[row_index].add(scaled), None)
    running = jnp.zeros((token_count + 1, D), jnp.float32)
    running, _ = lax.scan(one_slot, running, jnp.arange(EXPERTS, dtype=jnp.int32))
    return running[:token_count].astype(jnp.bfloat16)

def attention_reference(queries, incoming_key_value, key_value_pool, block_owner, block_tokens):
    query_group = QUERY_HEADS // KEY_VALUE_HEADS
    scale = 1.0 / math.sqrt(HEAD_DIMENSION)
    requests_per_column = N_REPLICA * DEVICE_REQUESTS
    block_pool = key_value_pool.reshape(N_REPLICA, N_EXPERT, DEVICE_BLOCKS, BLOCK_SLOTS, 2 * KEY_VALUE_HEADS * HEAD_DIMENSION)
    block_pool = jnp.transpose(block_pool, (1, 0, 2, 3, 4)).reshape(N_EXPERT, N_REPLICA * DEVICE_BLOCKS, BLOCK_SLOTS, 2 * KEY_VALUE_HEADS * HEAD_DIMENSION)
    owners = jnp.transpose(block_owner.reshape(N_REPLICA, N_EXPERT, DEVICE_BLOCKS), (1, 0, 2)).reshape(N_EXPERT, N_REPLICA * DEVICE_BLOCKS)
    counts = jnp.transpose(block_tokens.reshape(N_REPLICA, N_EXPERT, DEVICE_BLOCKS), (1, 0, 2)).reshape(N_EXPERT, N_REPLICA * DEVICE_BLOCKS)
    query_rows = jnp.transpose(queries.reshape(N_REPLICA, N_EXPERT, DEVICE_REQUESTS, QUERY_HEADS * HEAD_DIMENSION), (1, 0, 2, 3)).reshape(N_EXPERT, requests_per_column, KEY_VALUE_HEADS, query_group, HEAD_DIMENSION)
    latest_entry = jnp.transpose(incoming_key_value.reshape(N_REPLICA, N_EXPERT, DEVICE_REQUESTS, 2 * KEY_VALUE_HEADS * HEAD_DIMENSION), (1, 0, 2, 3)).reshape(N_EXPERT, requests_per_column, 2 * KEY_VALUE_HEADS * HEAD_DIMENSION)

    def one_column(inputs):
        block_pool_column, owner_column, count_column, query_column, latest_column = inputs
        cached_key_rows = block_pool_column[:, :, :KEY_VALUE_HEADS * HEAD_DIMENSION].reshape(-1, BLOCK_SLOTS, KEY_VALUE_HEADS, HEAD_DIMENSION).astype(jnp.float32)
        cached_value_rows = block_pool_column[:, :, KEY_VALUE_HEADS * HEAD_DIMENSION:].reshape(-1, BLOCK_SLOTS, KEY_VALUE_HEADS, HEAD_DIMENSION).astype(jnp.float32)
        query_f = query_column.astype(jnp.float32)
        incoming_keys = latest_column[:, :KEY_VALUE_HEADS * HEAD_DIMENSION].reshape(-1, KEY_VALUE_HEADS, HEAD_DIMENSION).astype(jnp.float32)
        incoming_values = latest_column[:, KEY_VALUE_HEADS * HEAD_DIMENSION:].reshape(-1, KEY_VALUE_HEADS, HEAD_DIMENSION).astype(jnp.float32)
        new_score = jnp.einsum('rgjd,rgd->rgj', query_f, incoming_keys, precision=HIGHEST) * scale
        block_query = query_f[owner_column]
        scores = jnp.einsum('bgjd,btgd->bgjt', block_query, cached_key_rows, precision=HIGHEST) * scale
        valid = jnp.arange(BLOCK_SLOTS, dtype=jnp.int32)[None, :] < count_column[:, None]
        block_top = lax.optimization_barrier(jnp.max(jnp.where(valid[:, None, None, :], scores, -jnp.inf), axis=3))
        member = owner_column[:, None] == jnp.arange(requests_per_column, dtype=jnp.int32)[None, :]
        request_top = lax.optimization_barrier(jnp.max(jnp.where(member[:, :, None, None], block_top[:, None, :, :], -jnp.inf), axis=0))
        best = jnp.maximum(request_top, new_score)
        weights = jnp.where(valid[:, None, None, :], jnp.exp(scores - best[owner_column][..., None]), 0.0)
        block_denom = lax.optimization_barrier(jnp.sum(weights, axis=3))
        block_sum = jnp.einsum('bgjt,btgd->bgjd', weights, cached_value_rows, precision=HIGHEST)
        member_f = member.astype(jnp.float32)
        own_weight = jnp.exp(new_score - best)
        denom = jnp.einsum('br,bgj->rgj', member_f, block_denom, precision=HIGHEST) + own_weight
        mixed = jnp.einsum('br,bgjd->rgjd', member_f, block_sum, precision=HIGHEST) + own_weight[..., None] * incoming_values[:, :, None, :]
        return (mixed / denom[..., None]).reshape(requests_per_column, QUERY_HEADS * HEAD_DIMENSION).astype(jnp.bfloat16)
    result = lax.map(one_column, (block_pool, owners, counts, query_rows, latest_entry))
    result = jnp.transpose(result.reshape(N_EXPERT, N_REPLICA, DEVICE_REQUESTS, QUERY_HEADS * HEAD_DIMENSION), (1, 0, 2, 3))
    return result.reshape(N_REPLICA * N_EXPERT * DEVICE_REQUESTS, QUERY_HEADS * HEAD_DIMENSION)

def reference(moe_input, expert_ids, route_weight, expert_slot, w_gate_up, w_down, queries, incoming_key_value, key_value_pool, block_owner, block_tokens):
    moe_out = mixture_reference(moe_input, expert_ids, route_weight, expert_slot, w_gate_up, w_down)
    attn_out = attention_reference(queries, incoming_key_value, key_value_pool, block_owner, block_tokens)
    return (moe_out, attn_out)
```

```python
import functools
import math

import jax
import jax.numpy as jnp
from jax import lax
from jax.experimental import pallas as pl
from jax.experimental.pallas import tpu as pltpu
from jax.sharding import Mesh
from jax.sharding import PartitionSpec as P

D = 2048
TOK = 16
TOP = 8
SLOTS = 128
CAP = 2
PIECES = 8
WIDE = D // PIECES
HALF = 192
HEADS = 64
GROUPS = 4
HEAD = 128
REPLICAS = 16
REQUESTS = 2
BLOCKS = 16
LEN = 64
KV = GROUPS * HEAD
NEG = -1e30
STAT = 16
MESSAGE = REQUESTS * HEADS + STAT

F32 = jnp.float32
BF16 = jnp.bfloat16
VMEM_LIMIT = 56 * 1024 * 1024

AXES = ("x", "zl", "y", "zh", "c")
CHIPS = ("x", "zl", "y", "zh")
REPLICA = ("x", "zl")


def iota(shape, dim):
    return lax.broadcasted_iota(jnp.int32, shape, dim)


def whole(count):
    return [pl.BlockSpec(memory_space=pltpu.VMEM)] * count


def params():
    return pltpu.CompilerParams(vmem_limit_bytes=VMEM_LIMIT)


def routing(ids, weight, slot_row):
    lane = iota((TOK, SLOTS), 1)
    chosen = jnp.zeros((TOK, SLOTS), F32)
    scale = jnp.zeros((TOK, SLOTS), F32)
    slots = slot_row.astype(F32)
    for k in range(TOP):
        slot = jnp.sum(jnp.where(ids[:, k : k + 1] == lane, slots, 0.0), axis=1, keepdims=True)
        hit = slot == lane.astype(F32)
        chosen = chosen + jnp.where(hit, 1.0, 0.0)
        scale = scale + jnp.where(hit, weight[:, k : k + 1], 0.0)
    earlier = jnp.where(iota((TOK, TOK), 1) < iota((TOK, TOK), 0), 1.0, 0.0).astype(BF16)
    rank = jnp.dot(earlier, chosen.astype(BF16), preferred_element_type=F32)
    taken = [jnp.where(rank == float(j), chosen, 0.0) for j in range(CAP)]
    return taken, scale


def dispatch_kernel(ids_ref, weight_ref, slot_ref, rows_ref, send_ref):
    taken, _ = routing(ids_ref[...], weight_ref[...], slot_ref[...])
    spread = jnp.where(iota((TOK, TOK * PIECES), 1) // PIECES == iota((TOK, TOK * PIECES), 0), 1.0, 0.0)
    same = (
        iota((1, PIECES, TOK * PIECES), 2) % PIECES == iota((1, PIECES, TOK * PIECES), 1)
    )
    picks = []
    for j in range(CAP):
        wide = lax.dot_general(
            taken[j].astype(BF16),
            spread.astype(BF16),
            (((0,), (0,)), ((), ())),
            preferred_element_type=F32,
        )
        picks.append(jnp.where(same, wide[:, None, :], 0.0))
    pick = jnp.concatenate(picks, axis=1).reshape(SLOTS * CAP * PIECES, TOK * PIECES)
    rows = jnp.dot(pick.astype(BF16), rows_ref[...], preferred_element_type=F32).astype(BF16)
    rows = rows.reshape(SLOTS, CAP * PIECES, WIDE)
    send_ref[:, 0] = rows
    send_ref[:, 1] = rows


def dispatch(ids, weight, slot_row, rows):
    return pl.pallas_call(
        dispatch_kernel,
        name="dispatch",
        out_shape=jax.ShapeDtypeStruct((SLOTS, 2, CAP * PIECES, WIDE), BF16),
        in_specs=whole(4),
        out_specs=whole(1)[0],
        compiler_params=params(),
    )(ids, weight, slot_row, rows)


MIX_CHUNK = 512
MIX_WIDTH = SLOTS * 2 * CAP * PIECES


def mixing_kernel(ids_ref, weight_ref, slot_ref, mix_ref):
    taken, scale = routing(ids_ref[...], weight_ref[...], slot_ref[...])
    parts = []
    for j in range(CAP):
        exact = taken[j] * scale
        high = exact.astype(BF16)
        low = (exact - high.astype(F32)).astype(BF16)
        parts.append(jnp.concatenate([high, low], axis=0))
    for start in range(0, MIX_WIDTH, MIX_CHUNK):
        place = iota((SLOTS, MIX_CHUNK), 1) + start
        mine = place // (2 * CAP * PIECES) == iota((SLOTS, MIX_CHUNK), 0)
        total = jnp.zeros((2 * TOK, MIX_CHUNK), F32)
        for j in range(CAP):
            use = mine & ((place // PIECES) % CAP == j)
            total = total + jnp.dot(
                parts[j], jnp.where(use, 1.0, 0.0).astype(BF16), preferred_element_type=F32
            )
        same = iota((1, PIECES, MIX_CHUNK), 2) % PIECES == iota((1, PIECES, MIX_CHUNK), 1)
        spread = jnp.where(same, total[:, None, :], 0.0)
        mix_ref[:, start : start + MIX_CHUNK] = spread.reshape(
            2 * TOK * PIECES, MIX_CHUNK
        ).astype(BF16)


def mixing(ids, weight, slot_row):
    return pl.pallas_call(
        mixing_kernel,
        name="mixing",
        out_shape=jax.ShapeDtypeStruct((2 * TOK * PIECES, MIX_WIDTH), BF16),
        in_specs=whole(3),
        out_specs=whole(1)[0],
        compiler_params=params(),
    )(ids, weight, slot_row)


def combine_kernel(mix_ref, rows_ref, out_ref):
    both = jnp.dot(mix_ref[...], rows_ref[...], preferred_element_type=F32)
    half = TOK * PIECES
    out_ref[...] = (both[:half] + both[half:]).astype(BF16)


def combine(mix, rows):
    return pl.pallas_call(
        combine_kernel,
        name="combine",
        out_shape=jax.ShapeDtypeStruct((TOK * PIECES, WIDE), BF16),
        in_specs=whole(2),
        out_specs=whole(1)[0],
        compiler_params=params(),
    )(mix, rows)


ROW_STEP = 128
PERM = 128


def expert_kernel(rows_ref, gate_ref, up_ref, down_ref, out_ref):
    near = PERM // PIECES
    one, two = iota((PERM, PERM), 0), iota((PERM, PERM), 1)
    apart = jnp.where(two == (one % near) * PIECES + one // near, 1.0, 0.0).astype(BF16)
    back = jnp.where(two == (one % PIECES) * near + one // PIECES, 1.0, 0.0).astype(BF16)
    tall = []
    for block in range(ROW_STEP // near):
        turned = jnp.dot(
            apart, rows_ref[block * PERM : (block + 1) * PERM], preferred_element_type=F32
        ).astype(BF16)
        tall.append(
            jnp.concatenate([turned[p * near : (p + 1) * near] for p in range(PIECES)], axis=1)
        )
    x = jnp.concatenate(tall, axis=0)
    gate = jnp.dot(x, gate_ref[...], preferred_element_type=F32)
    up = jnp.dot(x, up_ref[...], preferred_element_type=F32)
    act = (gate / (1.0 + jnp.exp(-gate)) * up).astype(BF16)
    y = jnp.dot(act, down_ref[...], preferred_element_type=F32).astype(BF16)
    for block in range(ROW_STEP // near):
        rows = y[block * near : (block + 1) * near]
        stacked = jnp.concatenate(
            [rows[:, p * WIDE : (p + 1) * WIDE] for p in range(PIECES)], axis=0
        )
        out_ref[block * PERM : (block + 1) * PERM] = jnp.dot(
            back, stacked, preferred_element_type=F32
        ).astype(BF16)


def expert(rows, gate, up, down):
    step = ROW_STEP * PIECES
    return pl.pallas_call(
        expert_kernel,
        name="expert",
        grid=(rows.shape[0] // step,),
        out_shape=jax.ShapeDtypeStruct(rows.shape, BF16),
        in_specs=[
            pl.BlockSpec((step, WIDE), lambda i: (i, 0)),
            pl.BlockSpec(gate.shape, lambda i: (0, 0)),
            pl.BlockSpec(up.shape, lambda i: (0, 0)),
            pl.BlockSpec(down.shape, lambda i: (0, 0)),
        ],
        out_specs=pl.BlockSpec((step, WIDE), lambda i: (i, 0)),
        compiler_params=params(),
    )(rows, gate, up, down)


def partial_kernel(owner_ref, count_ref, query_ref, pool_ref, send_ref, top_ref, sum_ref, acc_ref):
    scale = 1.0 / math.sqrt(HEAD)
    top_ref[...] = jnp.full(top_ref.shape, NEG, F32)
    sum_ref[...] = jnp.zeros(sum_ref.shape, F32)
    acc_ref[...] = jnp.zeros(acc_ref.shape, F32)
    per = HEADS // GROUPS
    own = iota((HEADS, KV), 1) // HEAD == iota((HEADS, KV), 0) // per
    slot = iota((HEADS, LEN), 1)
    for b in range(BLOCKS):
        owner = owner_ref[b]
        rows = pl.ds(pl.multiple_of(owner * HEADS, HEADS), HEADS)
        query = query_ref[rows, :]
        wide = jnp.where(own, jnp.concatenate([query] * GROUPS, axis=1), jnp.zeros((), BF16))
        score = (
            lax.dot_general(
                wide, pool_ref[b, :, :KV], (((1,), (1,)), ((), ())), preferred_element_type=F32
            )
            * scale
        )
        keep = slot < count_ref[b]
        score = jnp.where(keep, score, NEG)
        top = jnp.max(score, axis=1, keepdims=True)
        weight = jnp.where(keep, jnp.exp(score - top), 0.0)
        total = jnp.sum(weight, axis=1, keepdims=True)
        high = weight.astype(BF16)
        low = (weight - high.astype(F32)).astype(BF16)
        mixed = jnp.dot(
            jnp.concatenate([high, low], axis=0), pool_ref[b, :, KV:], preferred_element_type=F32
        )
        mixed = mixed[:HEADS] + mixed[HEADS:]
        mixed = jnp.concatenate(
            [
                mixed[g * per : (g + 1) * per, g * HEAD : (g + 1) * HEAD]
                for g in range(GROUPS)
            ],
            axis=0,
        )
        old = top_ref[rows, :]
        best = jnp.maximum(old, top)
        keep_old, add_new = jnp.exp(old - best), jnp.exp(top - best)
        top_ref[rows, :] = best
        sum_ref[rows, :] = keep_old * sum_ref[rows, :] + add_new * total
        acc_ref[rows, :] = keep_old * acc_ref[rows, :] + add_new * mixed
    lane, row = iota((HEADS, HEAD), 1), iota((HEADS, HEAD), 0)
    line = iota((STAT, HEAD), 0)
    for r in range(REPLICAS):
        stats = jnp.zeros((STAT, HEAD), F32)
        for i in range(REQUESTS):
            at = (r * REQUESTS + i) * HEADS
            send_ref[r, i * HEADS : (i + 1) * HEADS, :] = acc_ref[at : at + HEADS, :].astype(BF16)
            flat = jnp.where(lane == row, top_ref[at : at + HEADS, :], 0.0) + jnp.where(
                lane == row + HEADS, sum_ref[at : at + HEADS, :], 0.0
            )
            flat = jnp.sum(flat, axis=0, keepdims=True)
            high = flat.astype(BF16).astype(F32)
            middle = (flat - high).astype(BF16).astype(F32)
            for part, value in enumerate((high, middle, flat - high - middle)):
                stats = jnp.where(line == i * 3 + part, value, stats)
        send_ref[r, REQUESTS * HEADS :, :] = stats.astype(BF16)


def partial_attention(owner, count, queries, pool):
    smem = pl.BlockSpec(memory_space=pltpu.SMEM)
    wide = (REPLICAS * REQUESTS * HEADS, HEAD)
    return pl.pallas_call(
        partial_kernel,
        name="partial_attention",
        out_shape=jax.ShapeDtypeStruct((REPLICAS, MESSAGE, HEAD), BF16),
        in_specs=[smem, smem] + whole(2),
        out_specs=whole(1)[0],
        scratch_shapes=[pltpu.VMEM(wide, F32)] * 3,
        compiler_params=params(),
    )(owner, count, queries, pool)


def finish_kernel(got_ref, query_ref, new_ref, out_ref):
    scale = 1.0 / math.sqrt(HEAD)
    per = HEADS // GROUPS
    lane, row = iota((HEADS, HEAD), 1), iota((HEADS, HEAD), 0)

    def by_head(line):
        return jnp.concatenate(
            [
                jnp.broadcast_to(line[:, g * HEAD : (g + 1) * HEAD], (per, HEAD))
                for g in range(GROUPS)
            ],
            axis=0,
        )

    for i in range(REQUESTS):
        query = query_ref[i * HEADS : (i + 1) * HEADS, :].astype(F32)
        key = by_head(new_ref[i : i + 1, :KV].astype(F32))
        value = by_head(new_ref[i : i + 1, KV:].astype(F32))
        own = jnp.sum(query * key, axis=1, keepdims=True) * scale
        tops, sums = [], []
        best = own
        for r in range(REPLICAS):
            stats = got_ref[r, REQUESTS * HEADS :, :].astype(F32)
            flat = stats[i * 3 : i * 3 + 1] + stats[i * 3 + 1 : i * 3 + 2]
            flat = flat + stats[i * 3 + 2 : i * 3 + 3]
            tops.append(jnp.sum(jnp.where(lane == row, flat, 0.0), axis=1, keepdims=True))
            sums.append(jnp.sum(jnp.where(lane == row + HEADS, flat, 0.0), axis=1, keepdims=True))
            best = jnp.maximum(best, tops[-1])
        weight = jnp.exp(own - best)
        total = weight
        mixed = weight * value
        for r in range(REPLICAS):
            factor = jnp.exp(tops[r] - best)
            total = total + factor * sums[r]
            mixed = mixed + factor * got_ref[r, i * HEADS : (i + 1) * HEADS, :].astype(F32)
        out_ref[i * HEADS : (i + 1) * HEADS, :] = (mixed / total).astype(BF16)


def finish(got, queries, incoming):
    return pl.pallas_call(
        finish_kernel,
        name="finish",
        out_shape=jax.ShapeDtypeStruct((REQUESTS * HEADS, HEAD), BF16),
        in_specs=whole(3),
        out_specs=whole(1)[0],
        compiler_params=params(),
    )(got, queries, incoming)


def exchange(array, axes):
    return lax.all_to_all(array, axes, split_axis=0, concat_axis=0, tiled=True)


def swap(array):
    return lax.ppermute(array, "c", [(0, 1), (1, 0)])


def shards(
    moe_input,
    expert_ids,
    route_weight,
    expert_slot,
    w_gate_up,
    w_down,
    queries,
    incoming_key_value,
    key_value_pool,
    block_owner,
    block_tokens,
):
    slot_row = expert_slot.reshape(1, SLOTS)
    query_rows = queries.reshape(REQUESTS * HEADS, HEAD)
    all_queries = lax.all_gather(query_rows, REPLICA, axis=0, tiled=True)

    send = dispatch(
        expert_ids, route_weight, slot_row, moe_input.reshape(TOK * PIECES, WIDE)
    )
    received = exchange(send.reshape(SLOTS * 2, CAP * PIECES, WIDE), CHIPS)

    other_gate_up, other_down = swap(w_gate_up), swap(w_down)
    gate = jnp.concatenate([w_gate_up[:, :HALF], other_gate_up[:, :HALF]], axis=1)
    up = jnp.concatenate([w_gate_up[:, HALF:], other_gate_up[:, HALF:]], axis=1)
    down = jnp.concatenate([w_down, other_down], axis=0)
    mix = mixing(expert_ids, route_weight, slot_row)
    partials = partial_attention(block_owner, block_tokens, all_queries, key_value_pool)

    rows = expert(received.reshape(-1, WIDE), gate, up, down)
    returned = exchange(rows.reshape(SLOTS * 2, CAP * PIECES, WIDE), CHIPS)
    got = exchange(partials, REPLICA)
    moe_out = combine(mix, returned.reshape(-1, WIDE)).reshape(TOK, D)
    attn_out = finish(got, query_rows, incoming_key_value).reshape(REQUESTS, HEADS * HEAD)
    return (moe_out, attn_out)


def solution(mesh):
    fine = Mesh(mesh.devices.reshape(4, 4, 8, 2, 2), AXES)
    rows = P(AXES, None)
    placed = (
        rows,
        rows,
        rows,
        P(),
        P(None, AXES),
        rows,
        rows,
        rows,
        P(AXES, None, None),
        P(AXES),
        P(AXES),
    )
    return jax.shard_map(
        shards, mesh=fine, in_specs=placed, out_specs=(rows, rows), check_vma=False
    )
```

```python
import math

import jax
import jax.numpy as jnp
from jax import lax
from jax.experimental import pallas as pl
from jax.experimental.pallas import tpu as pltpu
from jax.sharding import Mesh
from jax.sharding import PartitionSpec as P

D = 2048
TOK = 16
TOP = 8
SLOTS = 128
RING = 8
REACH = 32
ROWS = 16
NEAR = RING * TOK
EXTRA = 256
HALF = 192
HEADS = 64
GROUPS = 4
HEAD = 128
REQUESTS = 2
SIDE = 4
BLOCKS = 16
LEN = 64
KV = GROUPS * HEAD
NEG = -1e30
STAT = 16
MESSAGE = REQUESTS * HEADS + STAT

F32 = jnp.float32
BF16 = jnp.bfloat16
VMEM_LIMIT = 56 * 1024 * 1024
AXIS = "d"


def number(x, zl, y, zh, c):
    return (x * 4 + zl) * 32 + y * 4 + zh * 2 + c


def position(device):
    return device >> 7, (device >> 5) & 3, (device >> 2) & 7, (device >> 1) & 1, device & 1


RING_GROUPS = [
    [number(x, z % 4, y, z // 4, 0) for z in range(8)] for x in range(4) for y in range(8)
] + [
    [number(x, z % 4, y, z // 4, 1) for y in range(8)] for x in range(4) for z in range(8)
]
REACH_GROUPS = [
    [number(x, z % 4, y, z // 4, 0) for x in range(4) for y in range(8)] for z in range(8)
] + [
    [number(x, z % 4, y, z // 4, 1) for x in range(4) for z in range(8)] for y in range(8)
]


def exchange(array, groups):
    return lax.all_to_all(
        array, AXIS, split_axis=0, concat_axis=0, axis_index_groups=groups, tiled=True
    )


def moved(array, dx=0, dz=0, dc=0):
    pairs = []
    for device in range(512):
        x, zl, y, zh, c = position(device)
        pairs.append((device, number((x + dx) % 4, (zl + dz) % 4, y, zh, (c + dc) % 2)))
    return lax.ppermute(array, AXIS, pairs)


def iota(shape, dim):
    return lax.broadcasted_iota(jnp.int32, shape, dim)


def whole(count):
    return [pl.BlockSpec(memory_space=pltpu.VMEM)] * count


def one(condition):
    return jnp.where(condition, 1.0, 0.0).astype(BF16)


def split(value):
    high = value.astype(BF16)
    rest = value - high.astype(F32)
    middle = rest.astype(BF16)
    return high, middle, (rest - middle.astype(F32)).astype(BF16)


def call(kernel, name, shapes, inputs, **more):
    return pl.pallas_call(
        kernel,
        name=name,
        out_shape=shapes,
        in_specs=more.pop("in_specs", whole(inputs)),
        out_specs=more.pop("out_specs", whole(1)[0]),
        compiler_params=pltpu.CompilerParams(vmem_limit_bytes=VMEM_LIMIT),
        **more,
    )


def shape(dims, kind=BF16):
    return jax.ShapeDtypeStruct(dims, kind)


def pack_kernel(token_ref, ids_ref, weight_ref, out_ref):
    x, zl, y, zh, c = position(lax.axis_index(AXIS))
    mine = jnp.where(c == 0, zh * 4 + zl, y)
    put = one(iota((TOK, NEAR), 1) == iota((TOK, NEAR), 0) + mine * TOK)
    ids = ids_ref[...].astype(F32).astype(BF16)
    parts = [jnp.dot(p, put, preferred_element_type=F32) for p in (ids,) + split(weight_ref[...])]
    left = jnp.concatenate(parts[:2], axis=0).astype(BF16)
    right = jnp.concatenate(parts[2:], axis=0).astype(BF16)
    for u in range(RING):
        out_ref[u, :, :D] = token_ref[...]
        out_ref[u, :, D : D + NEAR] = left
        out_ref[u, :, D + NEAR :] = right


def reached(slot_ref):
    x, zl, y, zh, c = position(lax.axis_index(AXIS))
    d = iota((REACH, SLOTS), 0)
    across, along = d >> 3, d & 7
    at_zl = jnp.where(c == 0, zl, along & 3)
    at_y = jnp.where(c == 0, along, y)
    return one(slot_ref[...] == (across * 4 + at_zl) * 8 + at_y)


def routing(near_ref, slot_ref):
    head = jnp.sum(near_ref[:, :, D:].astype(F32), axis=0)
    ids, weights = head[:TOP, :NEAR], (head[TOP:, :NEAR], head[:TOP, NEAR:], head[TOP:, NEAR:])
    expert = iota((SLOTS, NEAR), 0).astype(F32)
    hits = [ids[k : k + 1] == expert for k in range(TOP)]
    chosen = jnp.zeros((SLOTS, NEAR), F32)
    for hit in hits:
        chosen = chosen + jnp.where(hit, 1.0, 0.0)
    here = reached(slot_ref)
    mine = jnp.dot(here, chosen.astype(BF16), preferred_element_type=F32)
    earlier = one(iota((NEAR, NEAR), 0) < iota((NEAR, NEAR), 1))
    rank = jnp.dot(mine.astype(BF16), earlier, preferred_element_type=F32)
    place = jnp.where(mine > 0.5, rank, -1.0)
    taken = place[:, None, :] == iota((1, ROWS, NEAR), 1).astype(F32)
    return hits, weights, here, taken


def dispatch_kernel(near_ref, slot_ref, out_ref):
    _, _, _, taken = routing(near_ref, slot_ref)
    pick = jnp.where(taken, 1.0, 0.0).reshape(REACH * ROWS, NEAR).astype(BF16)
    tokens = near_ref[:, :, :D].reshape(NEAR, D)
    rows = jnp.dot(pick, tokens, preferred_element_type=F32)
    out_ref[...] = rows.astype(BF16).reshape(REACH, ROWS, D)


def mixing_kernel(near_ref, slot_ref, out_ref):
    hits, weights, here, taken = routing(near_ref, slot_ref)
    total = jnp.zeros((REACH, NEAR), F32)
    for part in weights:
        spread = jnp.zeros((SLOTS, NEAR), F32)
        for k in range(TOP):
            spread = spread + jnp.where(hits[k], part[k : k + 1], 0.0)
        total = total + jnp.dot(here, spread.astype(BF16), preferred_element_type=F32)
    mix = jnp.where(taken, total[:, None, :], 0.0).reshape(REACH * ROWS, NEAR).T
    high, low, _ = split(mix)
    out_ref[:NEAR] = high
    out_ref[NEAR:] = low


def combine_kernel(mix_ref, rows_ref, out_ref):
    rows = rows_ref[...].reshape(REACH * ROWS, D)
    both = jnp.dot(mix_ref[...], rows, preferred_element_type=F32)
    out_ref[...] = (both[:NEAR] + both[NEAR:]).astype(BF16).reshape(RING, TOK, D)


def total_kernel(parts_ref, out_ref):
    out_ref[...] = jnp.sum(parts_ref[...].astype(F32), axis=0).astype(BF16)


ROW_STEP = 128


def expert_kernel(rows_ref, gate_ref, up_ref, down_ref, out_ref):
    x = rows_ref[...]
    gate = jnp.dot(x, gate_ref[...], preferred_element_type=F32)
    up = jnp.dot(x, up_ref[...], preferred_element_type=F32)
    act = (gate / (1.0 + jnp.exp(-gate)) * up).astype(BF16)
    out_ref[...] = jnp.dot(act, down_ref[...], preferred_element_type=F32).astype(BF16)


def expert(rows, gate, up, down):
    step = pl.BlockSpec((ROW_STEP, D), lambda i: (i, 0))
    fixed = [pl.BlockSpec(w.shape, lambda i: (0, 0)) for w in (gate, up, down)]
    return call(
        expert_kernel,
        "expert",
        shape(rows.shape),
        4,
        grid=(rows.shape[0] // ROW_STEP,),
        in_specs=[step] + fixed,
        out_specs=step,
    )(rows, gate, up, down)


def partial_kernel(owner_ref, count_ref, query_ref, pool_ref, send_ref, top_ref, sum_ref, acc_ref):
    scale = 1.0 / math.sqrt(HEAD)
    top_ref[...] = jnp.full(top_ref.shape, NEG, F32)
    sum_ref[...] = jnp.zeros(sum_ref.shape, F32)
    acc_ref[...] = jnp.zeros(acc_ref.shape, F32)
    x, zl, _, _, _ = position(lax.axis_index(AXIS))
    per = HEADS // GROUPS
    own = iota((HEADS, KV), 1) // HEAD == iota((HEADS, KV), 0) // per
    slot = iota((HEADS, LEN), 1)
    for b in range(BLOCKS):
        owner = owner_ref[b]
        ax, az, request = owner >> 3, (owner >> 1) & 3, owner & 1
        asked = ((zl - az) & 3) * 8 + ((x - ax) & 3) * 2 + request
        state = ((az - zl) & 3) * 8 + ((ax - x) & 3) * 2 + request
        rows = pl.ds(pl.multiple_of(state * HEADS, HEADS), HEADS)
        query = query_ref[pl.ds(pl.multiple_of(asked * HEADS, HEADS), HEADS), :]
        wide = jnp.where(own, jnp.concatenate([query] * GROUPS, axis=1), jnp.zeros((), BF16))
        score = (
            lax.dot_general(
                wide, pool_ref[b, :, :KV], (((1,), (1,)), ((), ())), preferred_element_type=F32
            )
            * scale
        )
        keep = slot < count_ref[b]
        score = jnp.where(keep, score, NEG)
        top = jnp.max(score, axis=1, keepdims=True)
        weight = jnp.where(keep, jnp.exp(score - top), 0.0)
        total = jnp.sum(weight, axis=1, keepdims=True)
        high, low, _ = split(weight)
        mixed = jnp.dot(
            jnp.concatenate([high, low], axis=0), pool_ref[b, :, KV:], preferred_element_type=F32
        )
        mixed = mixed[:HEADS] + mixed[HEADS:]
        mixed = jnp.concatenate(
            [mixed[g * per : (g + 1) * per, g * HEAD : (g + 1) * HEAD] for g in range(GROUPS)],
            axis=0,
        )
        old = top_ref[rows, :]
        best = jnp.maximum(old, top)
        keep_old, add_new = jnp.exp(old - best), jnp.exp(top - best)
        top_ref[rows, :] = best
        sum_ref[rows, :] = keep_old * sum_ref[rows, :] + add_new * total
        acc_ref[rows, :] = keep_old * acc_ref[rows, :] + add_new * mixed
    lane, row = iota((HEADS, HEAD), 1), iota((HEADS, HEAD), 0)
    line = iota((STAT, HEAD), 0)
    for r in range(SIDE * SIDE):
        stats = jnp.zeros((STAT, HEAD), F32)
        for i in range(REQUESTS):
            at = (r * REQUESTS + i) * HEADS
            send_ref[r, i * HEADS : (i + 1) * HEADS, :] = acc_ref[at : at + HEADS, :].astype(BF16)
            flat = jnp.where(lane == row, top_ref[at : at + HEADS, :], 0.0) + jnp.where(
                lane == row + HEADS, sum_ref[at : at + HEADS, :], 0.0
            )
            flat = jnp.sum(flat, axis=0, keepdims=True)
            for part, value in enumerate(split(flat)):
                stats = jnp.where(line == i * 3 + part, value.astype(F32), stats)
        send_ref[r, REQUESTS * HEADS :, :] = stats.astype(BF16)


def partial_attention(owner, count, queries, pool):
    smem = pl.BlockSpec(memory_space=pltpu.SMEM)
    return call(
        partial_kernel,
        "partial_attention",
        shape((SIDE * SIDE, MESSAGE, HEAD)),
        4,
        in_specs=[smem, smem] + whole(2),
        scratch_shapes=[pltpu.VMEM((SIDE * SIDE * REQUESTS * HEADS, HEAD), F32)] * 3,
    )(owner, count, queries, pool)


def finish_kernel(got0_ref, got1_ref, got2_ref, got3_ref, query_ref, new_ref, out_ref):
    scale = 1.0 / math.sqrt(HEAD)
    per = HEADS // GROUPS
    lane, row = iota((HEADS, HEAD), 1), iota((HEADS, HEAD), 0)
    parts = [(ref, r) for ref in (got0_ref, got1_ref, got2_ref, got3_ref) for r in range(SIDE)]

    def by_head(line):
        return jnp.concatenate(
            [
                jnp.broadcast_to(line[:, g * HEAD : (g + 1) * HEAD], (per, HEAD))
                for g in range(GROUPS)
            ],
            axis=0,
        )

    for i in range(REQUESTS):
        query = query_ref[i * HEADS : (i + 1) * HEADS, :].astype(F32)
        key = by_head(new_ref[i : i + 1, :KV].astype(F32))
        value = by_head(new_ref[i : i + 1, KV:].astype(F32))
        own = jnp.sum(query * key, axis=1, keepdims=True) * scale
        tops, sums = [], []
        best = own
        for ref, r in parts:
            stats = ref[r, REQUESTS * HEADS :, :].astype(F32)
            flat = stats[i * 3 : i * 3 + 1] + stats[i * 3 + 1 : i * 3 + 2]
            flat = flat + stats[i * 3 + 2 : i * 3 + 3]
            tops.append(jnp.sum(jnp.where(lane == row, flat, 0.0), axis=1, keepdims=True))
            sums.append(jnp.sum(jnp.where(lane == row + HEADS, flat, 0.0), axis=1, keepdims=True))
            best = jnp.maximum(best, tops[-1])
        weight = jnp.exp(own - best)
        total = weight
        mixed = weight * value
        for (ref, r), top, part in zip(parts, tops, sums):
            factor = jnp.exp(top - best)
            total = total + factor * part
            mixed = mixed + factor * ref[r, i * HEADS : (i + 1) * HEADS, :].astype(F32)
        out_ref[i * HEADS : (i + 1) * HEADS, :] = (mixed / total).astype(BF16)


def ask(queries, pool, owner, count):
    own = queries.reshape(REQUESTS * HEADS, HEAD)
    line = jnp.concatenate([own] + [moved(own, dx=k) for k in range(1, SIDE)], axis=0)
    square = jnp.concatenate([line] + [moved(line, dz=k) for k in range(1, SIDE)], axis=0)
    return own, partial_attention(owner, count, square, pool)


def answer(own, partials, incoming):
    partials = partials.reshape(SIDE, SIDE, MESSAGE, HEAD)
    columns = [partials[0]] + [moved(partials[k], dz=k) for k in range(1, SIDE)]
    got = []
    for k in range(SIDE):
        piece = jnp.stack([column[k] for column in columns])
        got.append(moved(piece, dx=k) if k else piece)
    out = call(finish_kernel, "finish", shape((REQUESTS * HEADS, HEAD)), 6)(*got, own, incoming)
    return out.reshape(REQUESTS, HEADS * HEAD)


def shards(
    moe_input,
    expert_ids,
    route_weight,
    expert_slot,
    w_gate_up,
    w_down,
    queries,
    incoming_key_value,
    key_value_pool,
    block_owner,
    block_tokens,
):
    slot_row = expert_slot.reshape(1, SLOTS)
    packed = call(pack_kernel, "pack", shape((RING, TOK, D + EXTRA)), 3)(
        moe_input, expert_ids.T, route_weight.T
    )
    near = exchange(packed, RING_GROUPS)
    send = call(dispatch_kernel, "dispatch", shape((REACH, ROWS, D)), 2)(near, slot_row)
    received = exchange(send, REACH_GROUPS)

    own, partials = ask(queries, key_value_pool, block_owner, block_tokens)
    other_gate_up, other_down = moved(w_gate_up, dc=1), moved(w_down, dc=1)
    gate = jnp.concatenate([w_gate_up[:, :HALF], other_gate_up[:, :HALF]], axis=1)
    up = jnp.concatenate([w_gate_up[:, HALF:], other_gate_up[:, HALF:]], axis=1)
    down = jnp.concatenate([w_down, other_down], axis=0)
    received, partials = lax.optimization_barrier((received, partials))

    rows = expert(received.reshape(REACH * ROWS, D), gate, up, down)
    returned = exchange(rows.reshape(REACH, ROWS, D), REACH_GROUPS)
    attn_out = answer(own, partials, incoming_key_value)
    mix = call(mixing_kernel, "mixing", shape((2 * NEAR, REACH * ROWS)), 2)(near, slot_row)
    parts = call(combine_kernel, "combine", shape((RING, TOK, D)), 2)(mix, returned)
    parts = exchange(parts, RING_GROUPS)
    moe_out = call(total_kernel, "total", shape((TOK, D)), 1)(parts)
    return (moe_out, attn_out)


def solution(mesh):
    flat = Mesh(mesh.devices.reshape(-1), (AXIS,))
    rows = P(AXIS, None)
    placed = (
        rows,
        rows,
        rows,
        P(),
        P(None, AXIS),
        rows,
        rows,
        rows,
        P(AXIS, None, None),
        P(AXIS),
        P(AXIS),
    )
    return jax.shard_map(
        shards, mesh=flat, in_specs=placed, out_specs=(rows, rows), check_vma=False
    )
```

```python
import math

import jax
import jax.numpy as jnp
from jax import lax
from jax.experimental import pallas as pl
from jax.experimental.pallas import tpu as pltpu
from jax.sharding import Mesh
from jax.sharding import PartitionSpec as P

D = 2048
TOK = 16
TOP = 8
SLOTS = 128
RING = 8
REACH = 32
ROWS = 16
NEAR = RING * TOK
EXTRA = 256
HALF = 192
HEADS = 64
GROUPS = 4
HEAD = 128
REQUESTS = 2
SIDE = 4
BLOCKS = 16
LEN = 64
KV = GROUPS * HEAD
NEG = -1e30
STAT = 16
MESSAGE = REQUESTS * HEADS + STAT

F32 = jnp.float32
BF16 = jnp.bfloat16
VMEM_LIMIT = 56 * 1024 * 1024
AXIS = "d"


def number(x, zl, y, zh, c):
    return (x * 4 + zl) * 32 + y * 4 + zh * 2 + c


def position(device):
    return device >> 7, (device >> 5) & 3, (device >> 2) & 7, (device >> 1) & 1, device & 1


RING_GROUPS = [
    [number(x, z % 4, y, z // 4, 0) for z in range(8)] for x in range(4) for y in range(8)
] + [
    [number(x, z % 4, y, z // 4, 1) for y in range(8)] for x in range(4) for z in range(8)
]
REACH_GROUPS = [
    [number(x, z % 4, y, z // 4, 0) for x in range(4) for y in range(8)] for z in range(8)
] + [
    [number(x, z % 4, y, z // 4, 1) for x in range(4) for z in range(8)] for y in range(8)
]


def exchange(array, groups):
    return lax.all_to_all(
        array, AXIS, split_axis=0, concat_axis=0, axis_index_groups=groups, tiled=True
    )


def moved(array, dx=0, dz=0, dc=0):
    pairs = []
    for device in range(512):
        x, zl, y, zh, c = position(device)
        pairs.append((device, number((x + dx) % 4, (zl + dz) % 4, y, zh, (c + dc) % 2)))
    return lax.ppermute(array, AXIS, pairs)


def iota(shape, dim):
    return lax.broadcasted_iota(jnp.int32, shape, dim)


def whole(count):
    return [pl.BlockSpec(memory_space=pltpu.VMEM)] * count


def one(condition):
    return jnp.where(condition, 1.0, 0.0).astype(BF16)


def split(value):
    high = value.astype(BF16)
    rest = value - high.astype(F32)
    middle = rest.astype(BF16)
    return high, middle, (rest - middle.astype(F32)).astype(BF16)


def call(kernel, name, shapes, inputs, **more):
    return pl.pallas_call(
        kernel,
        name=name,
        out_shape=shapes,
        in_specs=more.pop("in_specs", whole(inputs)),
        out_specs=more.pop("out_specs", whole(1)[0]),
        compiler_params=pltpu.CompilerParams(vmem_limit_bytes=VMEM_LIMIT),
        **more,
    )


def shape(dims, kind=BF16):
    return jax.ShapeDtypeStruct(dims, kind)


def pack_kernel(token_ref, ids_ref, weight_ref, out_ref):
    x, zl, y, zh, c = position(lax.axis_index(AXIS))
    mine = jnp.where(c == 0, zh * 4 + zl, y)
    put = one(iota((TOK, NEAR), 1) == iota((TOK, NEAR), 0) + mine * TOK)
    ids = ids_ref[...].astype(F32).astype(BF16)
    parts = [jnp.dot(p, put, preferred_element_type=F32) for p in (ids,) + split(weight_ref[...])]
    left = jnp.concatenate(parts[:2], axis=0).astype(BF16)
    right = jnp.concatenate(parts[2:], axis=0).astype(BF16)
    for u in range(RING):
        out_ref[u, :, :D] = token_ref[...]
        out_ref[u, :, D : D + NEAR] = left
        out_ref[u, :, D + NEAR :] = right


def reached(slot_ref):
    x, zl, y, zh, c = position(lax.axis_index(AXIS))
    d = iota((REACH, SLOTS), 0)
    across, along = d >> 3, d & 7
    at_zl = jnp.where(c == 0, zl, along & 3)
    at_y = jnp.where(c == 0, along, y)
    return one(slot_ref[...] == (across * 4 + at_zl) * 8 + at_y)


def routing(near_ref, slot_ref):
    head = jnp.sum(near_ref[:, :, D:].astype(F32), axis=0)
    ids, weights = head[:TOP, :NEAR], (head[TOP:, :NEAR], head[:TOP, NEAR:], head[TOP:, NEAR:])
    expert = iota((SLOTS, NEAR), 0).astype(F32)
    hits = [ids[k : k + 1] == expert for k in range(TOP)]
    chosen = jnp.zeros((SLOTS, NEAR), F32)
    for hit in hits:
        chosen = chosen + jnp.where(hit, 1.0, 0.0)
    here = reached(slot_ref)
    mine = jnp.dot(here, chosen.astype(BF16), preferred_element_type=F32)
    earlier = one(iota((NEAR, NEAR), 0) < iota((NEAR, NEAR), 1))
    rank = jnp.dot(mine.astype(BF16), earlier, preferred_element_type=F32)
    place = jnp.where(mine > 0.5, rank, -1.0)
    taken = place[:, None, :] == iota((1, ROWS, NEAR), 1).astype(F32)
    return hits, weights, here, taken


def dispatch_kernel(near_ref, slot_ref, out_ref):
    _, _, _, taken = routing(near_ref, slot_ref)
    pick = jnp.where(taken, 1.0, 0.0).reshape(REACH * ROWS, NEAR).astype(BF16)
    tokens = near_ref[:, :, :D].reshape(NEAR, D)
    rows = jnp.dot(pick, tokens, preferred_element_type=F32)
    out_ref[...] = rows.astype(BF16).reshape(REACH, ROWS, D)


def mixing_kernel(near_ref, slot_ref, out_ref):
    hits, weights, here, taken = routing(near_ref, slot_ref)
    total = jnp.zeros((REACH, NEAR), F32)
    for part in weights:
        spread = jnp.zeros((SLOTS, NEAR), F32)
        for k in range(TOP):
            spread = spread + jnp.where(hits[k], part[k : k + 1], 0.0)
        total = total + jnp.dot(here, spread.astype(BF16), preferred_element_type=F32)
    mix = jnp.where(taken, total[:, None, :], 0.0).reshape(REACH * ROWS, NEAR).T
    high, low, _ = split(mix)
    out_ref[:NEAR] = high
    out_ref[NEAR:] = low


def combine_kernel(mix_ref, rows_ref, out_ref):
    rows = rows_ref[...].reshape(REACH * ROWS, D)
    both = jnp.dot(mix_ref[...], rows, preferred_element_type=F32)
    out_ref[...] = (both[:NEAR] + both[NEAR:]).astype(BF16).reshape(RING, TOK, D)


def total_kernel(parts_ref, out_ref):
    out_ref[...] = jnp.sum(parts_ref[...].astype(F32), axis=0).astype(BF16)


ROW_STEP = 256


def expert_kernel(rows_ref, gate_up_ref, other_gate_up_ref, down_ref, other_down_ref, out_ref):
    x = rows_ref[...]
    total = jnp.zeros((ROW_STEP, D), F32)
    for both_ref, back_ref in ((gate_up_ref, down_ref), (other_gate_up_ref, other_down_ref)):
        both = jnp.dot(x, both_ref[...], preferred_element_type=F32)
        gate, up = both[:, :HALF], both[:, HALF:]
        act = (gate / (1.0 + jnp.exp(-gate)) * up).astype(BF16)
        total = total + jnp.dot(act, back_ref[...], preferred_element_type=F32)
    out_ref[...] = total.astype(BF16)


def expert(rows, *weights):
    step = pl.BlockSpec((ROW_STEP, D), lambda i: (i, 0))
    fixed = [pl.BlockSpec(w.shape, lambda i: (0, 0)) for w in weights]
    return call(
        expert_kernel,
        "expert",
        shape(rows.shape),
        5,
        grid=(rows.shape[0] // ROW_STEP,),
        in_specs=[step] + fixed,
        out_specs=step,
    )(rows, *weights)


def partial_kernel(owner_ref, count_ref, query_ref, pool_ref, send_ref, top_ref, sum_ref, acc_ref):
    scale = 1.0 / math.sqrt(HEAD)
    top_ref[...] = jnp.full(top_ref.shape, NEG, F32)
    sum_ref[...] = jnp.zeros(sum_ref.shape, F32)
    acc_ref[...] = jnp.zeros(acc_ref.shape, F32)
    x, zl, _, _, _ = position(lax.axis_index(AXIS))
    per = HEADS // GROUPS
    own = iota((HEADS, KV), 1) // HEAD == iota((HEADS, KV), 0) // per
    slot = iota((HEADS, LEN), 1)
    for b in range(BLOCKS):
        owner = owner_ref[b]
        ax, az, request = owner >> 3, (owner >> 1) & 3, owner & 1
        asked = ((zl - az) & 3) * 8 + ((x - ax) & 3) * 2 + request
        state = ((az - zl) & 3) * 8 + ((ax - x) & 3) * 2 + request
        rows = pl.ds(pl.multiple_of(state * HEADS, HEADS), HEADS)
        query = query_ref[pl.ds(pl.multiple_of(asked * HEADS, HEADS), HEADS), :]
        wide = jnp.where(own, jnp.concatenate([query] * GROUPS, axis=1), jnp.zeros((), BF16))
        score = (
            lax.dot_general(
                wide, pool_ref[b, :, :KV], (((1,), (1,)), ((), ())), preferred_element_type=F32
            )
            * scale
        )
        keep = slot < count_ref[b]
        score = jnp.where(keep, score, NEG)
        top = jnp.max(score, axis=1, keepdims=True)
        weight = jnp.where(keep, jnp.exp(score - top), 0.0)
        total = jnp.sum(weight, axis=1, keepdims=True)
        high, low, _ = split(weight)
        mixed = jnp.dot(
            jnp.concatenate([high, low], axis=0), pool_ref[b, :, KV:], preferred_element_type=F32
        )
        mixed = mixed[:HEADS] + mixed[HEADS:]
        mixed = jnp.concatenate(
            [mixed[g * per : (g + 1) * per, g * HEAD : (g + 1) * HEAD] for g in range(GROUPS)],
            axis=0,
        )
        old = top_ref[rows, :]
        best = jnp.maximum(old, top)
        keep_old, add_new = jnp.exp(old - best), jnp.exp(top - best)
        top_ref[rows, :] = best
        sum_ref[rows, :] = keep_old * sum_ref[rows, :] + add_new * total
        acc_ref[rows, :] = keep_old * acc_ref[rows, :] + add_new * mixed
    lane, row = iota((HEADS, HEAD), 1), iota((HEADS, HEAD), 0)
    line = iota((STAT, HEAD), 0)
    for r in range(SIDE * SIDE):
        stats = jnp.zeros((STAT, HEAD), F32)
        for i in range(REQUESTS):
            at = (r * REQUESTS + i) * HEADS
            send_ref[r, i * HEADS : (i + 1) * HEADS, :] = acc_ref[at : at + HEADS, :].astype(BF16)
            flat = jnp.where(lane == row, top_ref[at : at + HEADS, :], 0.0) + jnp.where(
                lane == row + HEADS, sum_ref[at : at + HEADS, :], 0.0
            )
            flat = jnp.sum(flat, axis=0, keepdims=True)
            for part, value in enumerate(split(flat)):
                stats = jnp.where(line == i * 3 + part, value.astype(F32), stats)
        send_ref[r, REQUESTS * HEADS :, :] = stats.astype(BF16)


def partial_attention(owner, count, queries, pool):
    smem = pl.BlockSpec(memory_space=pltpu.SMEM)
    return call(
        partial_kernel,
        "partial_attention",
        shape((SIDE * SIDE, MESSAGE, HEAD)),
        4,
        in_specs=[smem, smem] + whole(2),
        scratch_shapes=[pltpu.VMEM((SIDE * SIDE * REQUESTS * HEADS, HEAD), F32)] * 3,
    )(owner, count, queries, pool)


def finish_kernel(got0_ref, got1_ref, got2_ref, got3_ref, query_ref, new_ref, out_ref):
    scale = 1.0 / math.sqrt(HEAD)
    per = HEADS // GROUPS
    lane, row = iota((HEADS, HEAD), 1), iota((HEADS, HEAD), 0)
    parts = [(ref, r) for ref in (got0_ref, got1_ref, got2_ref, got3_ref) for r in range(SIDE)]

    def by_head(line):
        return jnp.concatenate(
            [
                jnp.broadcast_to(line[:, g * HEAD : (g + 1) * HEAD], (per, HEAD))
                for g in range(GROUPS)
            ],
            axis=0,
        )

    answers = []
    for i in range(REQUESTS):
        query = query_ref[i * HEADS : (i + 1) * HEADS, :].astype(F32)
        key = by_head(new_ref[i : i + 1, :KV].astype(F32))
        value = by_head(new_ref[i : i + 1, KV:].astype(F32))
        own = jnp.sum(query * key, axis=1, keepdims=True) * scale
        tops, sums = [], []
        best = own
        for ref, r in parts:
            stats = ref[r, REQUESTS * HEADS :, :].astype(F32)
            flat = stats[i * 3 : i * 3 + 1] + stats[i * 3 + 1 : i * 3 + 2]
            flat = flat + stats[i * 3 + 2 : i * 3 + 3]
            tops.append(jnp.sum(jnp.where(lane == row, flat, 0.0), axis=1, keepdims=True))
            sums.append(jnp.sum(jnp.where(lane == row + HEADS, flat, 0.0), axis=1, keepdims=True))
            best = jnp.maximum(best, tops[-1])
        weight = jnp.exp(own - best)
        total = weight
        mixed = weight * value
        for (ref, r), top, part in zip(parts, tops, sums):
            factor = jnp.exp(top - best)
            total = total + factor * part
            mixed = mixed + factor * ref[r, i * HEADS : (i + 1) * HEADS, :].astype(F32)
        answers.append(mixed / total)
    for h in range(HEADS):
        pair = jnp.concatenate([part[h : h + 1] for part in answers], axis=0)
        out_ref[:, h * HEAD : (h + 1) * HEAD] = pair.astype(BF16)


def queries_in_line(queries):
    own = queries.reshape(REQUESTS * HEADS, HEAD)
    return jnp.concatenate([own] + [moved(own, dx=k) for k in range(1, SIDE)], axis=0)


def partials_of(line, pool, owner, count):
    square = jnp.concatenate([line] + [moved(line, dz=k) for k in range(1, SIDE)], axis=0)
    return partial_attention(owner, count, square, pool).reshape(SIDE, SIDE, MESSAGE, HEAD)


def partials_by_column(partials):
    columns = [partials[0]] + [moved(partials[k], dz=k) for k in range(1, SIDE)]
    return [jnp.stack([column[k] for column in columns]) for k in range(SIDE)]


def finish(pieces, own, incoming):
    got = [moved(piece, dx=k) if k else piece for k, piece in enumerate(pieces)]
    return call(finish_kernel, "finish", shape((REQUESTS, HEADS * HEAD)), 6)(*got, own, incoming)


def shards(
    moe_input,
    expert_ids,
    route_weight,
    expert_slot,
    w_gate_up,
    w_down,
    queries,
    incoming_key_value,
    key_value_pool,
    block_owner,
    block_tokens,
):
    slot_row = expert_slot.reshape(1, SLOTS)
    packed = call(pack_kernel, "pack", shape((RING, TOK, D + EXTRA)), 3)(
        moe_input, expert_ids.T, route_weight.T
    )
    near = exchange(packed, RING_GROUPS)
    line = queries_in_line(queries)
    near, line = lax.optimization_barrier((near, line))
    send = call(dispatch_kernel, "dispatch", shape((REACH, ROWS, D)), 2)(near, slot_row)
    received = exchange(send, REACH_GROUPS)

    partials = partials_of(line, key_value_pool, block_owner, block_tokens)
    other_gate_up, other_down = moved(w_gate_up, dc=1), moved(w_down, dc=1)
    received, partials = lax.optimization_barrier((received, partials))

    rows = expert(
        received.reshape(REACH * ROWS, D), w_gate_up, other_gate_up, w_down, other_down
    )
    returned = exchange(rows.reshape(REACH, ROWS, D), REACH_GROUPS)
    mix = call(mixing_kernel, "mixing", shape((2 * NEAR, REACH * ROWS)), 2)(near, slot_row)
    pieces = partials_by_column(partials)
    returned, pieces = lax.optimization_barrier((returned, pieces))

    parts = call(combine_kernel, "combine", shape((RING, TOK, D)), 2)(mix, returned)
    parts = exchange(parts, RING_GROUPS)
    attn_out = finish(pieces, line[: REQUESTS * HEADS], incoming_key_value)
    moe_out = call(total_kernel, "total", shape((TOK, D)), 1)(parts)
    return (moe_out, attn_out)


def solution(mesh):
    flat = Mesh(mesh.devices.reshape(-1), (AXIS,))
    rows = P(AXIS, None)
    placed = (
        rows,
        rows,
        rows,
        P(),
        P(None, AXIS),
        rows,
        rows,
        rows,
        P(AXIS, None, None),
        P(AXIS),
        P(AXIS),
    )
    return jax.shard_map(
        shards, mesh=flat, in_specs=placed, out_specs=(rows, rows), check_vma=False
    )
```

```python
import math

import jax
import jax.numpy as jnp
from jax import lax
from jax.experimental import pallas as pl
from jax.experimental.pallas import tpu as pltpu
from jax.sharding import Mesh
from jax.sharding import PartitionSpec as P

D = 2048
TOK = 16
TOP = 8
SLOTS = 128
RING = 8
REACH = 32
ROWS = 16
NEAR = RING * TOK
EXTRA = 256
HALF = 192
HEADS = 64
GROUPS = 4
HEAD = 128
REQUESTS = 2
SIDE = 4
BLOCKS = 16
LEN = 64
KV = GROUPS * HEAD
NEG = -1e30
STAT = 16
MESSAGE = REQUESTS * HEADS + STAT

F32 = jnp.float32
BF16 = jnp.bfloat16
VMEM_LIMIT = 56 * 1024 * 1024
AXIS = "d"


def number(x, zl, y, zh, c):
    return (x * 4 + zl) * 32 + y * 4 + zh * 2 + c


def position(device):
    return device >> 7, (device >> 5) & 3, (device >> 2) & 7, (device >> 1) & 1, device & 1


RING_GROUPS = [
    [number(x, z % 4, y, z // 4, 0) for z in range(8)] for x in range(4) for y in range(8)
] + [
    [number(x, z % 4, y, z // 4, 1) for y in range(8)] for x in range(4) for z in range(8)
]
REACH_GROUPS = [
    [number(x, z % 4, y, z // 4, 0) for x in range(4) for y in range(8)] for z in range(8)
] + [
    [number(x, z % 4, y, z // 4, 1) for x in range(4) for z in range(8)] for y in range(8)
]


def exchange(array, groups):
    return lax.all_to_all(
        array, AXIS, split_axis=0, concat_axis=0, axis_index_groups=groups, tiled=True
    )


def moved(array, dx=0, dz=0, dc=0):
    pairs = []
    for device in range(512):
        x, zl, y, zh, c = position(device)
        pairs.append((device, number((x + dx) % 4, (zl + dz) % 4, y, zh, (c + dc) % 2)))
    return lax.ppermute(array, AXIS, pairs)


def iota(shape, dim):
    return lax.broadcasted_iota(jnp.int32, shape, dim)


def whole(count):
    return [pl.BlockSpec(memory_space=pltpu.VMEM)] * count


def one(condition):
    return jnp.where(condition, 1.0, 0.0).astype(BF16)


def split(value):
    high = value.astype(BF16)
    rest = value - high.astype(F32)
    middle = rest.astype(BF16)
    return high, middle, (rest - middle.astype(F32)).astype(BF16)


def call(kernel, name, shapes, inputs, **more):
    return pl.pallas_call(
        kernel,
        name=name,
        out_shape=shapes,
        in_specs=more.pop("in_specs", whole(inputs)),
        out_specs=more.pop("out_specs", whole(1)[0]),
        compiler_params=pltpu.CompilerParams(vmem_limit_bytes=VMEM_LIMIT),
        **more,
    )


def shape(dims, kind=BF16):
    return jax.ShapeDtypeStruct(dims, kind)


def pack_kernel(token_ref, ids_ref, weight_ref, out_ref):
    x, zl, y, zh, c = position(lax.axis_index(AXIS))
    mine = jnp.where(c == 0, zh * 4 + zl, y)
    put = one(iota((TOK, NEAR), 1) == iota((TOK, NEAR), 0) + mine * TOK)
    ids = ids_ref[...].astype(F32).astype(BF16)
    parts = [jnp.dot(p, put, preferred_element_type=F32) for p in (ids,) + split(weight_ref[...])]
    left = jnp.concatenate(parts[:2], axis=0).astype(BF16)
    right = jnp.concatenate(parts[2:], axis=0).astype(BF16)
    for u in range(RING):
        out_ref[u, :, :D] = token_ref[...]
        out_ref[u, :, D : D + NEAR] = left
        out_ref[u, :, D + NEAR :] = right


def reached(slot_ref):
    x, zl, y, zh, c = position(lax.axis_index(AXIS))
    d = iota((REACH, SLOTS), 0)
    across, along = d >> 3, d & 7
    at_zl = jnp.where(c == 0, zl, along & 3)
    at_y = jnp.where(c == 0, along, y)
    return one(slot_ref[...] == (across * 4 + at_zl) * 8 + at_y)


def routing(near_ref, slot_ref):
    head = jnp.sum(near_ref[:, :, D:].astype(F32), axis=0)
    ids, weights = head[:TOP, :NEAR], (head[TOP:, :NEAR], head[:TOP, NEAR:], head[TOP:, NEAR:])
    expert = iota((SLOTS, NEAR), 0).astype(F32)
    hits = [ids[k : k + 1] == expert for k in range(TOP)]
    chosen = jnp.zeros((SLOTS, NEAR), F32)
    for hit in hits:
        chosen = chosen + jnp.where(hit, 1.0, 0.0)
    here = reached(slot_ref)
    mine = jnp.dot(here, chosen.astype(BF16), preferred_element_type=F32)
    earlier = one(iota((NEAR, NEAR), 0) < iota((NEAR, NEAR), 1))
    rank = jnp.dot(mine.astype(BF16), earlier, preferred_element_type=F32)
    place = jnp.where(mine > 0.5, rank, -1.0)
    taken = place[:, None, :] == iota((1, ROWS, NEAR), 1).astype(F32)
    return hits, weights, here, taken


def dispatch_kernel(near_ref, slot_ref, out_ref):
    _, _, _, taken = routing(near_ref, slot_ref)
    pick = jnp.where(taken, 1.0, 0.0).reshape(REACH * ROWS, NEAR).astype(BF16)
    tokens = near_ref[:, :, :D].reshape(NEAR, D)
    rows = jnp.dot(pick, tokens, preferred_element_type=F32)
    out_ref[...] = rows.astype(BF16).reshape(REACH, ROWS, D)


def mixing_kernel(near_ref, slot_ref, out_ref):
    hits, weights, here, taken = routing(near_ref, slot_ref)
    total = jnp.zeros((REACH, NEAR), F32)
    for part in weights:
        spread = jnp.zeros((SLOTS, NEAR), F32)
        for k in range(TOP):
            spread = spread + jnp.where(hits[k], part[k : k + 1], 0.0)
        total = total + jnp.dot(here, spread.astype(BF16), preferred_element_type=F32)
    mix = jnp.where(taken, total[:, None, :], 0.0).reshape(REACH * ROWS, NEAR).T
    high, low, _ = split(mix)
    out_ref[:NEAR] = high
    out_ref[NEAR:] = low


def combine_kernel(mix_ref, rows_ref, out_ref):
    rows = rows_ref[...].reshape(REACH * ROWS, D)
    both = jnp.dot(mix_ref[...], rows, preferred_element_type=F32)
    out_ref[...] = (both[:NEAR] + both[NEAR:]).astype(BF16).reshape(RING, TOK, D)


def total_kernel(parts_ref, out_ref):
    out_ref[...] = jnp.sum(parts_ref[...].astype(F32), axis=0).astype(BF16)


ROW_STEP = 256


def expert_kernel(rows_ref, gate_up_ref, other_gate_up_ref, down_ref, other_down_ref, out_ref):
    x = rows_ref[...]
    total = jnp.zeros((ROW_STEP, D), F32)
    for both_ref, back_ref in ((gate_up_ref, down_ref), (other_gate_up_ref, other_down_ref)):
        both = jnp.dot(x, both_ref[...], preferred_element_type=F32)
        gate, up = both[:, :HALF], both[:, HALF:]
        act = (gate / (1.0 + jnp.exp(-gate)) * up).astype(BF16)
        total = total + jnp.dot(act, back_ref[...], preferred_element_type=F32)
    out_ref[...] = total.astype(BF16)


def expert(rows, *weights):
    step = pl.BlockSpec((ROW_STEP, D), lambda i: (i, 0))
    fixed = [pl.BlockSpec(w.shape, lambda i: (0, 0)) for w in weights]
    return call(
        expert_kernel,
        "expert",
        shape(rows.shape),
        5,
        grid=(rows.shape[0] // ROW_STEP,),
        in_specs=[step] + fixed,
        out_specs=step,
    )(rows, *weights)


def partial_kernel(owner_ref, count_ref, query_ref, pool_ref, send_ref, top_ref, sum_ref, acc_ref):
    scale = 1.0 / math.sqrt(HEAD)
    top_ref[...] = jnp.full(top_ref.shape, NEG, F32)
    sum_ref[...] = jnp.zeros(sum_ref.shape, F32)
    acc_ref[...] = jnp.zeros(acc_ref.shape, F32)
    x, zl, _, _, _ = position(lax.axis_index(AXIS))
    per = HEADS // GROUPS
    own = iota((HEADS, KV), 1) // HEAD == iota((HEADS, KV), 0) // per
    slot = iota((HEADS, LEN), 1)
    for b in range(BLOCKS):
        owner = owner_ref[b]
        ax, az, request = owner >> 3, (owner >> 1) & 3, owner & 1
        asked = ((zl - az) & 3) * 8 + ((x - ax) & 3) * 2 + request
        state = ((az - zl) & 3) * 8 + ((ax - x) & 3) * 2 + request
        rows = pl.ds(pl.multiple_of(state * HEADS, HEADS), HEADS)
        query = query_ref[pl.ds(pl.multiple_of(asked * HEADS, HEADS), HEADS), :]
        wide = jnp.where(own, jnp.concatenate([query] * GROUPS, axis=1), jnp.zeros((), BF16))
        score = (
            lax.dot_general(
                wide, pool_ref[b, :, :KV], (((1,), (1,)), ((), ())), preferred_element_type=F32
            )
            * scale
        )
        keep = slot < count_ref[b]
        score = jnp.where(keep, score, NEG)
        top = jnp.max(score, axis=1, keepdims=True)
        weight = jnp.where(keep, jnp.exp(score - top), 0.0)
        total = jnp.sum(weight, axis=1, keepdims=True)
        high, low, _ = split(weight)
        mixed = jnp.dot(
            jnp.concatenate([high, low], axis=0), pool_ref[b, :, KV:], preferred_element_type=F32
        )
        mixed = mixed[:HEADS] + mixed[HEADS:]
        mixed = jnp.concatenate(
            [mixed[g * per : (g + 1) * per, g * HEAD : (g + 1) * HEAD] for g in range(GROUPS)],
            axis=0,
        )
        old = top_ref[rows, :]
        best = jnp.maximum(old, top)
        keep_old, add_new = jnp.exp(old - best), jnp.exp(top - best)
        top_ref[rows, :] = best
        sum_ref[rows, :] = keep_old * sum_ref[rows, :] + add_new * total
        acc_ref[rows, :] = keep_old * acc_ref[rows, :] + add_new * mixed
    lane, row = iota((HEADS, HEAD), 1), iota((HEADS, HEAD), 0)
    line = iota((STAT, HEAD), 0)
    for r in range(SIDE * SIDE):
        stats = jnp.zeros((STAT, HEAD), F32)
        for i in range(REQUESTS):
            at = (r * REQUESTS + i) * HEADS
            send_ref[r, i * HEADS : (i + 1) * HEADS, :] = acc_ref[at : at + HEADS, :].astype(BF16)
            flat = jnp.where(lane == row, top_ref[at : at + HEADS, :], 0.0) + jnp.where(
                lane == row + HEADS, sum_ref[at : at + HEADS, :], 0.0
            )
            flat = jnp.sum(flat, axis=0, keepdims=True)
            for part, value in enumerate(split(flat)):
                stats = jnp.where(line == i * 3 + part, value.astype(F32), stats)
        send_ref[r, REQUESTS * HEADS :, :] = stats.astype(BF16)


def partial_attention(owner, count, queries, pool):
    smem = pl.BlockSpec(memory_space=pltpu.SMEM)
    return call(
        partial_kernel,
        "partial_attention",
        shape((SIDE * SIDE, MESSAGE, HEAD)),
        4,
        in_specs=[smem, smem] + whole(2),
        scratch_shapes=[pltpu.VMEM((SIDE * SIDE * REQUESTS * HEADS, HEAD), F32)] * 3,
    )(owner, count, queries, pool)


def finish_kernel(got0_ref, got1_ref, got2_ref, got3_ref, query_ref, new_ref, out_ref):
    scale = 1.0 / math.sqrt(HEAD)
    per = HEADS // GROUPS
    lane, row = iota((HEADS, HEAD), 1), iota((HEADS, HEAD), 0)
    parts = [(ref, r) for ref in (got0_ref, got1_ref, got2_ref, got3_ref) for r in range(SIDE)]

    def by_head(line):
        return jnp.concatenate(
            [
                jnp.broadcast_to(line[:, g * HEAD : (g + 1) * HEAD], (per, HEAD))
                for g in range(GROUPS)
            ],
            axis=0,
        )

    answers = []
    for i in range(REQUESTS):
        query = query_ref[i * HEADS : (i + 1) * HEADS, :].astype(F32)
        key = by_head(new_ref[i : i + 1, :KV].astype(F32))
        value = by_head(new_ref[i : i + 1, KV:].astype(F32))
        own = jnp.sum(query * key, axis=1, keepdims=True) * scale
        tops, sums = [], []
        best = own
        for ref, r in parts:
            stats = ref[r, REQUESTS * HEADS :, :].astype(F32)
            flat = stats[i * 3 : i * 3 + 1] + stats[i * 3 + 1 : i * 3 + 2]
            flat = flat + stats[i * 3 + 2 : i * 3 + 3]
            tops.append(jnp.sum(jnp.where(lane == row, flat, 0.0), axis=1, keepdims=True))
            sums.append(jnp.sum(jnp.where(lane == row + HEADS, flat, 0.0), axis=1, keepdims=True))
            best = jnp.maximum(best, tops[-1])
        weight = jnp.exp(own - best)
        total = weight
        mixed = weight * value
        for (ref, r), top, part in zip(parts, tops, sums):
            factor = jnp.exp(top - best)
            total = total + factor * part
            mixed = mixed + factor * ref[r, i * HEADS : (i + 1) * HEADS, :].astype(F32)
        answers.append(mixed / total)
    for h in range(HEADS):
        pair = jnp.concatenate([part[h : h + 1] for part in answers], axis=0)
        out_ref[:, h * HEAD : (h + 1) * HEAD] = pair.astype(BF16)


def along(array, axis):
    return [array] + [moved(array, **{axis: k}) for k in range(1, SIDE)]


def shards(
    moe_input,
    expert_ids,
    route_weight,
    expert_slot,
    w_gate_up,
    w_down,
    queries,
    incoming_key_value,
    key_value_pool,
    block_owner,
    block_tokens,
):
    slot_row = expert_slot.reshape(1, SLOTS)
    packed = call(pack_kernel, "pack", shape((RING, TOK, D + EXTRA)), 3)(
        moe_input, expert_ids.T, route_weight.T
    )
    line = along(queries.reshape(REQUESTS * HEADS, HEAD), "dx")
    packed, line[1] = lax.optimization_barrier((packed, line[1]))
    near = exchange(packed, RING_GROUPS)
    square = along(jnp.concatenate(line, axis=0), "dz")
    near, square = lax.optimization_barrier((near, square))
    send = call(dispatch_kernel, "dispatch", shape((REACH, ROWS, D)), 2)(near, slot_row)
    received = exchange(send, REACH_GROUPS)

    other_gate_up, other_down = moved(w_gate_up, dc=1), moved(w_down, dc=1)
    partials = partial_attention(
        block_owner, block_tokens, jnp.concatenate(square, axis=0), key_value_pool
    ).reshape(SIDE, SIDE, MESSAGE, HEAD)
    columns = [partials[0]] + [moved(partials[k], dz=k) for k in range(1, SIDE)]

    rows = expert(
        received.reshape(REACH * ROWS, D), w_gate_up, other_gate_up, w_down, other_down
    )
    rows, columns = lax.optimization_barrier((rows, columns))
    returned = exchange(rows.reshape(REACH, ROWS, D), REACH_GROUPS)
    mix = call(mixing_kernel, "mixing", shape((2 * NEAR, REACH * ROWS)), 2)(near, slot_row)
    pieces = [jnp.stack([column[k] for column in columns]) for k in range(SIDE)]
    got = [moved(piece, dx=k) if k else piece for k, piece in enumerate(pieces)]
    returned, got = lax.optimization_barrier((returned, got))

    parts = call(combine_kernel, "combine", shape((RING, TOK, D)), 2)(mix, returned)
    parts = exchange(parts, RING_GROUPS)
    attn_out = call(finish_kernel, "finish", shape((REQUESTS, HEADS * HEAD)), 6)(
        *got, line[0], incoming_key_value
    )
    moe_out = call(total_kernel, "total", shape((TOK, D)), 1)(parts)
    return (moe_out, attn_out)


def solution(mesh):
    flat = Mesh(mesh.devices.reshape(-1), (AXIS,))
    rows = P(AXIS, None)
    placed = (
        rows,
        rows,
        rows,
        P(),
        P(None, AXIS),
        rows,
        rows,
        rows,
        P(AXIS, None, None),
        P(AXIS),
        P(AXIS),
    )
    return jax.shard_map(
        shards, mesh=flat, in_specs=placed, out_specs=(rows, rows), check_vma=False
    )
```

```python
import math

import jax
import jax.numpy as jnp
from jax import lax
from jax.experimental import pallas as pl
from jax.experimental.pallas import tpu as pltpu
from jax.sharding import Mesh
from jax.sharding import PartitionSpec as P

D = 2048
TOK = 16
TOP = 8
SLOTS = 128
RING = 8
REACH = 32
ROWS = 16
NEAR = RING * TOK
EXTRA = 256
HALF = 192
HEADS = 64
GROUPS = 4
HEAD = 128
REQUESTS = 2
SIDE = 4
BLOCKS = 16
LEN = 64
KV = GROUPS * HEAD
NEG = -1e30
STAT = 16
MESSAGE = REQUESTS * HEADS + STAT

F32 = jnp.float32
BF16 = jnp.bfloat16
VMEM_LIMIT = 56 * 1024 * 1024
AXIS = "d"


def number(x, zl, y, zh, c):
    return (x * 4 + zl) * 32 + y * 4 + zh * 2 + c


def position(device):
    return device >> 7, (device >> 5) & 3, (device >> 2) & 7, (device >> 1) & 1, device & 1


RING_GROUPS = [
    [number(x, z % 4, y, z // 4, 0) for z in range(8)] for x in range(4) for y in range(8)
] + [
    [number(x, z % 4, y, z // 4, 1) for y in range(8)] for x in range(4) for z in range(8)
]
REACH_GROUPS = [
    [number(x, z % 4, y, z // 4, 0) for x in range(4) for y in range(8)] for z in range(8)
] + [
    [number(x, z % 4, y, z // 4, 1) for x in range(4) for z in range(8)] for y in range(8)
]


def exchange(array, groups):
    return lax.all_to_all(
        array, AXIS, split_axis=0, concat_axis=0, axis_index_groups=groups, tiled=True
    )


def moved(array, dx=0, dz=0, dc=0):
    pairs = []
    for device in range(512):
        x, zl, y, zh, c = position(device)
        pairs.append((device, number((x + dx) % 4, (zl + dz) % 4, y, zh, (c + dc) % 2)))
    return lax.ppermute(array, AXIS, pairs)


def iota(shape, dim):
    return lax.broadcasted_iota(jnp.int32, shape, dim)


def whole(count):
    return [pl.BlockSpec(memory_space=pltpu.VMEM)] * count


def one(condition):
    return jnp.where(condition, 1.0, 0.0).astype(BF16)


def split(value):
    high = value.astype(BF16)
    rest = value - high.astype(F32)
    middle = rest.astype(BF16)
    return high, middle, (rest - middle.astype(F32)).astype(BF16)


def call(kernel, name, shapes, inputs, **more):
    return pl.pallas_call(
        kernel,
        name=name,
        out_shape=shapes,
        in_specs=more.pop("in_specs", whole(inputs)),
        out_specs=more.pop("out_specs", whole(1)[0]),
        compiler_params=pltpu.CompilerParams(vmem_limit_bytes=VMEM_LIMIT),
        **more,
    )


def shape(dims, kind=BF16):
    return jax.ShapeDtypeStruct(dims, kind)


def pack_kernel(token_ref, ids_ref, weight_ref, out_ref):
    x, zl, y, zh, c = position(lax.axis_index(AXIS))
    mine = jnp.where(c == 0, zh * 4 + zl, y)
    put = one(iota((TOK, NEAR), 1) == iota((TOK, NEAR), 0) + mine * TOK)
    ids = ids_ref[...].astype(F32).astype(BF16)
    parts = [jnp.dot(p, put, preferred_element_type=F32) for p in (ids,) + split(weight_ref[...])]
    left = jnp.concatenate(parts[:2], axis=0).astype(BF16)
    right = jnp.concatenate(parts[2:], axis=0).astype(BF16)
    for u in range(RING):
        out_ref[u, :, :D] = token_ref[...]
        out_ref[u, :, D : D + NEAR] = left
        out_ref[u, :, D + NEAR :] = right


def reached(slot_ref):
    x, zl, y, zh, c = position(lax.axis_index(AXIS))
    d = iota((REACH, SLOTS), 0)
    across, along = d >> 3, d & 7
    at_zl = jnp.where(c == 0, zl, along & 3)
    at_y = jnp.where(c == 0, along, y)
    return one(slot_ref[...] == (across * 4 + at_zl) * 8 + at_y)


def routing(near_ref, slot_ref):
    head = jnp.sum(near_ref[:, :, D:].astype(F32), axis=0)
    ids, weights = head[:TOP, :NEAR], (head[TOP:, :NEAR], head[:TOP, NEAR:], head[TOP:, NEAR:])
    expert = iota((SLOTS, NEAR), 0).astype(F32)
    hits = [ids[k : k + 1] == expert for k in range(TOP)]
    chosen = jnp.zeros((SLOTS, NEAR), F32)
    for hit in hits:
        chosen = chosen + jnp.where(hit, 1.0, 0.0)
    here = reached(slot_ref)
    mine = jnp.dot(here, chosen.astype(BF16), preferred_element_type=F32)
    earlier = one(iota((NEAR, NEAR), 0) < iota((NEAR, NEAR), 1))
    rank = jnp.dot(mine.astype(BF16), earlier, preferred_element_type=F32)
    place = jnp.where(mine > 0.5, rank, -1.0)
    taken = place[:, None, :] == iota((1, ROWS, NEAR), 1).astype(F32)
    return hits, weights, here, taken


def dispatch_kernel(near_ref, slot_ref, out_ref):
    _, _, _, taken = routing(near_ref, slot_ref)
    pick = jnp.where(taken, 1.0, 0.0).reshape(REACH * ROWS, NEAR).astype(BF16)
    tokens = near_ref[:, :, :D].reshape(NEAR, D)
    rows = jnp.dot(pick, tokens, preferred_element_type=F32)
    out_ref[...] = rows.astype(BF16).reshape(REACH, ROWS, D)


def mixing_kernel(near_ref, slot_ref, out_ref):
    hits, weights, here, taken = routing(near_ref, slot_ref)
    total = jnp.zeros((REACH, NEAR), F32)
    for part in weights:
        spread = jnp.zeros((SLOTS, NEAR), F32)
        for k in range(TOP):
            spread = spread + jnp.where(hits[k], part[k : k + 1], 0.0)
        total = total + jnp.dot(here, spread.astype(BF16), preferred_element_type=F32)
    mix = jnp.where(taken, total[:, None, :], 0.0).reshape(REACH * ROWS, NEAR).T
    high, low, _ = split(mix)
    out_ref[:NEAR] = high
    out_ref[NEAR:] = low


def combine_kernel(mix_ref, rows_ref, out_ref):
    rows = rows_ref[...].reshape(REACH * ROWS, D)
    both = jnp.dot(mix_ref[...], rows, preferred_element_type=F32)
    out_ref[...] = (both[:NEAR] + both[NEAR:]).astype(BF16).reshape(RING, TOK, D)


def total_kernel(parts_ref, out_ref):
    out_ref[...] = jnp.sum(parts_ref[...].astype(F32), axis=0).astype(BF16)


ROW_STEP = 256


def expert_kernel(rows_ref, gate_up_ref, other_gate_up_ref, down_ref, other_down_ref, out_ref):
    x = rows_ref[...]
    total = jnp.zeros((ROW_STEP, D), F32)
    for both_ref, back_ref in ((gate_up_ref, down_ref), (other_gate_up_ref, other_down_ref)):
        both = jnp.dot(x, both_ref[...], preferred_element_type=F32)
        gate, up = both[:, :HALF], both[:, HALF:]
        act = (gate / (1.0 + jnp.exp(-gate)) * up).astype(BF16)
        total = total + jnp.dot(act, back_ref[...], preferred_element_type=F32)
    out_ref[...] = total.astype(BF16)


def expert(rows, *weights):
    step = pl.BlockSpec((ROW_STEP, D), lambda i: (i, 0))
    fixed = [pl.BlockSpec(w.shape, lambda i: (0, 0)) for w in weights]
    return call(
        expert_kernel,
        "expert",
        shape(rows.shape),
        5,
        grid=(rows.shape[0] // ROW_STEP,),
        in_specs=[step] + fixed,
        out_specs=step,
    )(rows, *weights)


def write_states(ref, r, states):
    lane, row = iota((HEADS, HEAD), 1), iota((HEADS, HEAD), 0)
    line = iota((STAT, HEAD), 0)
    stats = jnp.zeros((STAT, HEAD), F32)
    for i, (top, total, mixed) in enumerate(states):
        ref[r, i * HEADS : (i + 1) * HEADS, :] = mixed.astype(BF16)
        flat = jnp.where(lane == row, top, 0.0) + jnp.where(lane == row + HEADS, total, 0.0)
        flat = jnp.sum(flat, axis=0, keepdims=True)
        for part, value in enumerate(split(flat)):
            stats = jnp.where(line == i * 3 + part, value.astype(F32), stats)
    ref[r, REQUESTS * HEADS :, :] = stats.astype(BF16)


def read_state(ref, r, i):
    lane, row = iota((HEADS, HEAD), 1), iota((HEADS, HEAD), 0)
    stats = ref[r, REQUESTS * HEADS :, :].astype(F32)
    flat = stats[i * 3 : i * 3 + 1] + stats[i * 3 + 1 : i * 3 + 2] + stats[i * 3 + 2 : i * 3 + 3]
    top = jnp.sum(jnp.where(lane == row, flat, 0.0), axis=1, keepdims=True)
    total = jnp.sum(jnp.where(lane == row + HEADS, flat, 0.0), axis=1, keepdims=True)
    return top, total, ref[r, i * HEADS : (i + 1) * HEADS, :].astype(F32)


def merged(states):
    best = states[0][0]
    for top, _, _ in states[1:]:
        best = jnp.maximum(best, top)
    sums, acc = 0.0, 0.0
    for top, total, mixed in states:
        factor = jnp.exp(top - best)
        sums = sums + factor * total
        acc = acc + factor * mixed
    return best, sums, acc


def merge_kernel(got0_ref, got1_ref, got2_ref, got3_ref, send_ref):
    refs = (got0_ref, got1_ref, got2_ref, got3_ref)
    for r in range(SIDE):
        write_states(
            send_ref,
            r,
            [merged([read_state(ref, r, i) for ref in refs]) for i in range(REQUESTS)],
        )


def partial_kernel(owner_ref, count_ref, query_ref, pool_ref, send_ref, top_ref, sum_ref, acc_ref):
    scale = 1.0 / math.sqrt(HEAD)
    top_ref[...] = jnp.full(top_ref.shape, NEG, F32)
    sum_ref[...] = jnp.zeros(sum_ref.shape, F32)
    acc_ref[...] = jnp.zeros(acc_ref.shape, F32)
    x, zl, _, _, _ = position(lax.axis_index(AXIS))
    per = HEADS // GROUPS
    own = iota((HEADS, KV), 1) // HEAD == iota((HEADS, KV), 0) // per
    slot = iota((HEADS, LEN), 1)
    for b in range(BLOCKS):
        owner = owner_ref[b]
        ax, az, request = owner >> 3, (owner >> 1) & 3, owner & 1
        asked = ((x - ax) & 3) * 8 + ((zl - az) & 3) * 2 + request
        state = ((ax - x) & 3) * 8 + ((az - zl) & 3) * 2 + request
        rows = pl.ds(pl.multiple_of(state * HEADS, HEADS), HEADS)
        query = query_ref[pl.ds(pl.multiple_of(asked * HEADS, HEADS), HEADS), :]
        wide = jnp.where(own, jnp.concatenate([query] * GROUPS, axis=1), jnp.zeros((), BF16))
        score = (
            lax.dot_general(
                wide, pool_ref[b, :, :KV], (((1,), (1,)), ((), ())), preferred_element_type=F32
            )
            * scale
        )
        keep = slot < count_ref[b]
        score = jnp.where(keep, score, NEG)
        top = jnp.max(score, axis=1, keepdims=True)
        weight = jnp.where(keep, jnp.exp(score - top), 0.0)
        total = jnp.sum(weight, axis=1, keepdims=True)
        high, low, _ = split(weight)
        mixed = jnp.dot(
            jnp.concatenate([high, low], axis=0), pool_ref[b, :, KV:], preferred_element_type=F32
        )
        mixed = mixed[:HEADS] + mixed[HEADS:]
        mixed = jnp.concatenate(
            [mixed[g * per : (g + 1) * per, g * HEAD : (g + 1) * HEAD] for g in range(GROUPS)],
            axis=0,
        )
        old = top_ref[rows, :]
        best = jnp.maximum(old, top)
        keep_old, add_new = jnp.exp(old - best), jnp.exp(top - best)
        top_ref[rows, :] = best
        sum_ref[rows, :] = keep_old * sum_ref[rows, :] + add_new * total
        acc_ref[rows, :] = keep_old * acc_ref[rows, :] + add_new * mixed
    for r in range(SIDE * SIDE):
        states = []
        for i in range(REQUESTS):
            at = (r * REQUESTS + i) * HEADS
            rows = slice(at, at + HEADS)
            states.append((top_ref[rows, :], sum_ref[rows, :], acc_ref[rows, :]))
        write_states(send_ref, r, states)


def partial_attention(owner, count, queries, pool):
    smem = pl.BlockSpec(memory_space=pltpu.SMEM)
    return call(
        partial_kernel,
        "partial_attention",
        shape((SIDE * SIDE, MESSAGE, HEAD)),
        4,
        in_specs=[smem, smem] + whole(2),
        scratch_shapes=[pltpu.VMEM((SIDE * SIDE * REQUESTS * HEADS, HEAD), F32)] * 3,
    )(owner, count, queries, pool)


def finish_kernel(got0_ref, got1_ref, got2_ref, got3_ref, query_ref, new_ref, out_ref):
    scale = 1.0 / math.sqrt(HEAD)
    per = HEADS // GROUPS

    def by_head(line):
        return jnp.concatenate(
            [
                jnp.broadcast_to(line[:, g * HEAD : (g + 1) * HEAD], (per, HEAD))
                for g in range(GROUPS)
            ],
            axis=0,
        )

    answers = []
    for i in range(REQUESTS):
        query = query_ref[i * HEADS : (i + 1) * HEADS, :].astype(F32)
        key = by_head(new_ref[i : i + 1, :KV].astype(F32))
        value = by_head(new_ref[i : i + 1, KV:].astype(F32))
        own = jnp.sum(query * key, axis=1, keepdims=True) * scale
        states = [(own, jnp.ones((HEADS, 1), F32), value)]
        states += [read_state(ref, 0, i) for ref in (got0_ref, got1_ref, got2_ref, got3_ref)]
        _, total, mixed = merged(states)
        answers.append(mixed / total)
    for h in range(HEADS):
        pair = jnp.concatenate([part[h : h + 1] for part in answers], axis=0)
        out_ref[:, h * HEAD : (h + 1) * HEAD] = pair.astype(BF16)


def along(array, axis):
    return [array] + [moved(array, **{axis: k}) for k in range(1, SIDE)]


def shards(
    moe_input,
    expert_ids,
    route_weight,
    expert_slot,
    w_gate_up,
    w_down,
    queries,
    incoming_key_value,
    key_value_pool,
    block_owner,
    block_tokens,
):
    slot_row = expert_slot.reshape(1, SLOTS)
    packed = call(pack_kernel, "pack", shape((RING, TOK, D + EXTRA)), 3)(
        moe_input, expert_ids.T, route_weight.T
    )
    own_queries = queries.reshape(REQUESTS * HEADS, HEAD)
    line = jnp.concatenate(along(own_queries, "dz"), axis=0)
    near = exchange(packed, RING_GROUPS)
    near, line = lax.optimization_barrier((near, line))
    send = call(dispatch_kernel, "dispatch", shape((REACH, ROWS, D)), 2)(near, slot_row)
    received = exchange(send, REACH_GROUPS)

    other_gate_up, other_down = moved(w_gate_up, dc=1), moved(w_down, dc=1)
    all_queries = jnp.concatenate(along(line, "dx"), axis=0)
    received, all_queries = lax.optimization_barrier((received, all_queries))
    rows = expert(
        received.reshape(REACH * ROWS, D), w_gate_up, other_gate_up, w_down, other_down
    )
    rows, block_owner = lax.optimization_barrier((rows, block_owner))
    returned = exchange(rows.reshape(REACH, ROWS, D), REACH_GROUPS)
    partials = partial_attention(block_owner, block_tokens, all_queries, key_value_pool)
    partials = partials.reshape(SIDE, SIDE, MESSAGE, HEAD)
    got = [partials[0]] + [moved(partials[k], dx=k) for k in range(1, SIDE)]
    mix = call(mixing_kernel, "mixing", shape((2 * NEAR, REACH * ROWS)), 2)(near, slot_row)
    returned, got = lax.optimization_barrier((returned, got))

    parts = call(combine_kernel, "combine", shape((RING, TOK, D)), 2)(mix, returned)
    parts = exchange(parts, RING_GROUPS)
    send = call(merge_kernel, "merge", shape((SIDE, MESSAGE, HEAD)), 4)(*got)
    got = [send[:1]] + [moved(send[k : k + 1], dz=k) for k in range(1, SIDE)]
    attn_out = call(finish_kernel, "finish", shape((REQUESTS, HEADS * HEAD)), 6)(
        *got, own_queries, incoming_key_value
    )
    moe_out = call(total_kernel, "total", shape((TOK, D)), 1)(parts)
    return (moe_out, attn_out)


def solution(mesh):
    flat = Mesh(mesh.devices.reshape(-1), (AXIS,))
    rows = P(AXIS, None)
    placed = (
        rows,
        rows,
        rows,
        P(),
        P(None, AXIS),
        rows,
        rows,
        rows,
        P(AXIS, None, None),
        P(AXIS),
        P(AXIS),
    )
    return jax.shard_map(
        shards, mesh=flat, in_specs=placed, out_specs=(rows, rows), check_vma=False
    )
```

```python
import math

import jax
import jax.numpy as jnp
from jax import lax
from jax.experimental import pallas as pl
from jax.experimental.pallas import tpu as pltpu
from jax.sharding import Mesh
from jax.sharding import PartitionSpec as P

D = 2048
TOK = 16
TOP = 8
SLOTS = 128
RING = 8
REACH = 32
ROWS = 16
NEAR = RING * TOK
EXTRA = 256
HALF = 192
HEADS = 64
GROUPS = 4
HEAD = 128
REQUESTS = 2
SIDE = 4
BLOCKS = 16
LEN = 64
KV = GROUPS * HEAD
NEG = -1e30
STAT = 16
MESSAGE = REQUESTS * HEADS + STAT

F32 = jnp.float32
BF16 = jnp.bfloat16
VMEM_LIMIT = 56 * 1024 * 1024
AXIS = "d"


def number(x, zl, y, zh, c):
    return (x * 4 + zl) * 32 + y * 4 + zh * 2 + c


def position(device):
    return device >> 7, (device >> 5) & 3, (device >> 2) & 7, (device >> 1) & 1, device & 1


RING_GROUPS = [
    [number(x, z % 4, y, z // 4, 0) for z in range(8)] for x in range(4) for y in range(8)
] + [
    [number(x, z % 4, y, z // 4, 1) for y in range(8)] for x in range(4) for z in range(8)
]
REACH_GROUPS = [
    [number(x, z % 4, y, z // 4, 0) for x in range(4) for y in range(8)] for z in range(8)
] + [
    [number(x, z % 4, y, z // 4, 1) for x in range(4) for z in range(8)] for y in range(8)
]


def exchange(array, groups):
    return lax.all_to_all(
        array, AXIS, split_axis=0, concat_axis=0, axis_index_groups=groups, tiled=True
    )


def moved(array, dx=0, dz=0, dc=0):
    pairs = []
    for device in range(512):
        x, zl, y, zh, c = position(device)
        pairs.append((device, number((x + dx) % 4, (zl + dz) % 4, y, zh, (c + dc) % 2)))
    return lax.ppermute(array, AXIS, pairs)


def doubled(array, fx=0, fz=0):
    pairs = []
    for device in range(512):
        x, zl, y, zh, c = position(device)
        pairs.append((device, number(x ^ fx, zl ^ fz, y, zh, c)))
    return jnp.concatenate([array, lax.ppermute(array, AXIS, pairs)], axis=0)


def iota(shape, dim):
    return lax.broadcasted_iota(jnp.int32, shape, dim)


def whole(count):
    return [pl.BlockSpec(memory_space=pltpu.VMEM)] * count


def one(condition):
    return jnp.where(condition, 1.0, 0.0).astype(BF16)


def split(value):
    high = value.astype(BF16)
    rest = value - high.astype(F32)
    middle = rest.astype(BF16)
    return high, middle, (rest - middle.astype(F32)).astype(BF16)


def call(kernel, name, shapes, inputs, **more):
    return pl.pallas_call(
        kernel,
        name=name,
        out_shape=shapes,
        in_specs=more.pop("in_specs", whole(inputs)),
        out_specs=more.pop("out_specs", whole(1)[0]),
        compiler_params=pltpu.CompilerParams(vmem_limit_bytes=VMEM_LIMIT),
        **more,
    )


def shape(dims, kind=BF16):
    return jax.ShapeDtypeStruct(dims, kind)


def pack_kernel(token_ref, ids_ref, weight_ref, out_ref):
    x, zl, y, zh, c = position(lax.axis_index(AXIS))
    mine = jnp.where(c == 0, zh * 4 + zl, y)
    put = one(iota((TOK, NEAR), 1) == iota((TOK, NEAR), 0) + mine * TOK)
    ids = ids_ref[...].astype(F32).astype(BF16)
    parts = [jnp.dot(p, put, preferred_element_type=F32) for p in (ids,) + split(weight_ref[...])]
    left = jnp.concatenate(parts[:2], axis=0).astype(BF16)
    right = jnp.concatenate(parts[2:], axis=0).astype(BF16)
    for u in range(RING):
        out_ref[u, :, :D] = token_ref[...]
        out_ref[u, :, D : D + NEAR] = left
        out_ref[u, :, D + NEAR :] = right


def reached(slot_ref):
    x, zl, y, zh, c = position(lax.axis_index(AXIS))
    d = iota((REACH, SLOTS), 0)
    across, along = d >> 3, d & 7
    at_zl = jnp.where(c == 0, zl, along & 3)
    at_y = jnp.where(c == 0, along, y)
    return one(slot_ref[...] == (across * 4 + at_zl) * 8 + at_y)


def routing(near_ref, slot_ref):
    head = jnp.sum(near_ref[:, :, D:].astype(F32), axis=0)
    ids, weights = head[:TOP, :NEAR], (head[TOP:, :NEAR], head[:TOP, NEAR:], head[TOP:, NEAR:])
    expert = iota((SLOTS, NEAR), 0).astype(F32)
    hits = [ids[k : k + 1] == expert for k in range(TOP)]
    chosen = jnp.zeros((SLOTS, NEAR), F32)
    for hit in hits:
        chosen = chosen + jnp.where(hit, 1.0, 0.0)
    here = reached(slot_ref)
    mine = jnp.dot(here, chosen.astype(BF16), preferred_element_type=F32)
    earlier = one(iota((NEAR, NEAR), 0) < iota((NEAR, NEAR), 1))
    rank = jnp.dot(mine.astype(BF16), earlier, preferred_element_type=F32)
    place = jnp.where(mine > 0.5, rank, -1.0)
    taken = place[:, None, :] == iota((1, ROWS, NEAR), 1).astype(F32)
    return hits, weights, here, taken


def dispatch_kernel(near_ref, slot_ref, out_ref):
    _, _, _, taken = routing(near_ref, slot_ref)
    pick = jnp.where(taken, 1.0, 0.0).reshape(REACH * ROWS, NEAR).astype(BF16)
    tokens = near_ref[:, :, :D].reshape(NEAR, D)
    rows = jnp.dot(pick, tokens, preferred_element_type=F32)
    out_ref[...] = rows.astype(BF16).reshape(REACH, ROWS, D)


def mixing_kernel(near_ref, slot_ref, out_ref):
    hits, weights, here, taken = routing(near_ref, slot_ref)
    total = jnp.zeros((REACH, NEAR), F32)
    for part in weights:
        spread = jnp.zeros((SLOTS, NEAR), F32)
        for k in range(TOP):
            spread = spread + jnp.where(hits[k], part[k : k + 1], 0.0)
        total = total + jnp.dot(here, spread.astype(BF16), preferred_element_type=F32)
    mix = jnp.where(taken, total[:, None, :], 0.0).reshape(REACH * ROWS, NEAR).T
    high, low, _ = split(mix)
    out_ref[:NEAR] = high
    out_ref[NEAR:] = low


def combine_kernel(mix_ref, rows_ref, out_ref):
    rows = rows_ref[...].reshape(REACH * ROWS, D)
    both = jnp.dot(mix_ref[...], rows, preferred_element_type=F32)
    out_ref[...] = (both[:NEAR] + both[NEAR:]).astype(BF16).reshape(RING, TOK, D)


def total_kernel(parts_ref, out_ref):
    out_ref[...] = jnp.sum(parts_ref[...].astype(F32), axis=0).astype(BF16)


ROW_STEP = 256


def expert_kernel(rows_ref, gate_up_ref, other_gate_up_ref, down_ref, other_down_ref, out_ref):
    x = rows_ref[...]
    total = jnp.zeros((ROW_STEP, D), F32)
    for both_ref, back_ref in ((gate_up_ref, down_ref), (other_gate_up_ref, other_down_ref)):
        both = jnp.dot(x, both_ref[...], preferred_element_type=F32)
        gate, up = both[:, :HALF], both[:, HALF:]
        act = (gate / (1.0 + jnp.exp(-gate)) * up).astype(BF16)
        total = total + jnp.dot(act, back_ref[...], preferred_element_type=F32)
    out_ref[...] = total.astype(BF16)


def expert(rows, *weights):
    step = pl.BlockSpec((ROW_STEP, D), lambda i: (i, 0))
    fixed = [pl.BlockSpec(w.shape, lambda i: (0, 0)) for w in weights]
    return call(
        expert_kernel,
        "expert",
        shape(rows.shape),
        5,
        grid=(rows.shape[0] // ROW_STEP,),
        in_specs=[step] + fixed,
        out_specs=step,
    )(rows, *weights)


def write_states(ref, r, states):
    lane, row = iota((HEADS, HEAD), 1), iota((HEADS, HEAD), 0)
    line = iota((STAT, HEAD), 0)
    stats = jnp.zeros((STAT, HEAD), F32)
    for i, (top, total, mixed) in enumerate(states):
        ref[r, i * HEADS : (i + 1) * HEADS, :] = mixed.astype(BF16)
        flat = jnp.where(lane == row, top, 0.0) + jnp.where(lane == row + HEADS, total, 0.0)
        flat = jnp.sum(flat, axis=0, keepdims=True)
        for part, value in enumerate(split(flat)):
            stats = jnp.where(line == i * 3 + part, value.astype(F32), stats)
    ref[r, REQUESTS * HEADS :, :] = stats.astype(BF16)


def read_state(ref, r, i):
    lane, row = iota((HEADS, HEAD), 1), iota((HEADS, HEAD), 0)
    stats = ref[r, REQUESTS * HEADS :, :].astype(F32)
    flat = stats[i * 3 : i * 3 + 1] + stats[i * 3 + 1 : i * 3 + 2] + stats[i * 3 + 2 : i * 3 + 3]
    top = jnp.sum(jnp.where(lane == row, flat, 0.0), axis=1, keepdims=True)
    total = jnp.sum(jnp.where(lane == row + HEADS, flat, 0.0), axis=1, keepdims=True)
    return top, total, ref[r, i * HEADS : (i + 1) * HEADS, :].astype(F32)


def merged(states):
    best = states[0][0]
    for top, _, _ in states[1:]:
        best = jnp.maximum(best, top)
    sums, acc = 0.0, 0.0
    for top, total, mixed in states:
        factor = jnp.exp(top - best)
        sums = sums + factor * total
        acc = acc + factor * mixed
    return best, sums, acc


def merge_kernel(got0_ref, got1_ref, got2_ref, got3_ref, *sends):
    refs = (got0_ref, got1_ref, got2_ref, got3_ref)
    for r in range(SIDE):
        write_states(
            sends[r],
            0,
            [merged([read_state(ref, r, i) for ref in refs]) for i in range(REQUESTS)],
        )


def partial_kernel(owner_ref, count_ref, query_ref, pool_ref, *refs):
    sends, (top_ref, sum_ref, acc_ref) = refs[:SIDE], refs[SIDE:]
    scale = 1.0 / math.sqrt(HEAD)
    top_ref[...] = jnp.full(top_ref.shape, NEG, F32)
    sum_ref[...] = jnp.zeros(sum_ref.shape, F32)
    acc_ref[...] = jnp.zeros(acc_ref.shape, F32)
    x, zl, _, _, _ = position(lax.axis_index(AXIS))
    per = HEADS // GROUPS
    own = iota((HEADS, KV), 1) // HEAD == iota((HEADS, KV), 0) // per
    slot = iota((HEADS, LEN), 1)
    for b in range(BLOCKS):
        owner = owner_ref[b]
        ax, az, request = owner >> 3, (owner >> 1) & 3, owner & 1
        fx, fz = ax ^ x, az ^ zl
        asked = (fz & 1) * 16 + (fz >> 1) * 8 + (fx & 1) * 4 + (fx >> 1) * 2 + request
        state = ((ax - x) & 3) * 8 + ((az - zl) & 3) * 2 + request
        rows = pl.ds(pl.multiple_of(state * HEADS, HEADS), HEADS)
        query = query_ref[pl.ds(pl.multiple_of(asked * HEADS, HEADS), HEADS), :]
        wide = jnp.where(own, jnp.concatenate([query] * GROUPS, axis=1), jnp.zeros((), BF16))
        score = (
            lax.dot_general(
                wide, pool_ref[b, :, :KV], (((1,), (1,)), ((), ())), preferred_element_type=F32
            )
            * scale
        )
        keep = slot < count_ref[b]
        score = jnp.where(keep, score, NEG)
        top = jnp.max(score, axis=1, keepdims=True)
        weight = jnp.where(keep, jnp.exp(score - top), 0.0)
        total = jnp.sum(weight, axis=1, keepdims=True)
        high, low, _ = split(weight)
        mixed = jnp.dot(
            jnp.concatenate([high, low], axis=0), pool_ref[b, :, KV:], preferred_element_type=F32
        )
        mixed = mixed[:HEADS] + mixed[HEADS:]
        mixed = jnp.concatenate(
            [mixed[g * per : (g + 1) * per, g * HEAD : (g + 1) * HEAD] for g in range(GROUPS)],
            axis=0,
        )
        old = top_ref[rows, :]
        best = jnp.maximum(old, top)
        keep_old, add_new = jnp.exp(old - best), jnp.exp(top - best)
        top_ref[rows, :] = best
        sum_ref[rows, :] = keep_old * sum_ref[rows, :] + add_new * total
        acc_ref[rows, :] = keep_old * acc_ref[rows, :] + add_new * mixed
    for r in range(SIDE * SIDE):
        states = []
        for i in range(REQUESTS):
            at = (r * REQUESTS + i) * HEADS
            rows = slice(at, at + HEADS)
            states.append((top_ref[rows, :], sum_ref[rows, :], acc_ref[rows, :]))
        write_states(sends[r // SIDE], r % SIDE, states)


def partial_attention(owner, count, queries, pool):
    smem = pl.BlockSpec(memory_space=pltpu.SMEM)
    return call(
        partial_kernel,
        "partial_attention",
        [shape((SIDE, MESSAGE, HEAD))] * SIDE,
        4,
        in_specs=[smem, smem] + whole(2),
        out_specs=whole(SIDE),
        scratch_shapes=[pltpu.VMEM((SIDE * SIDE * REQUESTS * HEADS, HEAD), F32)] * 3,
    )(owner, count, queries, pool)


def finish_kernel(got0_ref, got1_ref, got2_ref, got3_ref, query_ref, new_ref, out_ref):
    scale = 1.0 / math.sqrt(HEAD)
    per = HEADS // GROUPS

    def by_head(line):
        return jnp.concatenate(
            [
                jnp.broadcast_to(line[:, g * HEAD : (g + 1) * HEAD], (per, HEAD))
                for g in range(GROUPS)
            ],
            axis=0,
        )

    answers = []
    for i in range(REQUESTS):
        query = query_ref[i * HEADS : (i + 1) * HEADS, :].astype(F32)
        key = by_head(new_ref[i : i + 1, :KV].astype(F32))
        value = by_head(new_ref[i : i + 1, KV:].astype(F32))
        own = jnp.sum(query * key, axis=1, keepdims=True) * scale
        states = [(own, jnp.ones((HEADS, 1), F32), value)]
        states += [read_state(ref, 0, i) for ref in (got0_ref, got1_ref, got2_ref, got3_ref)]
        _, total, mixed = merged(states)
        answers.append(mixed / total)
    for h in range(HEADS):
        pair = jnp.concatenate([part[h : h + 1] for part in answers], axis=0)
        out_ref[:, h * HEAD : (h + 1) * HEAD] = pair.astype(BF16)


def spread(arrays, axis):
    return [moved(array, **{axis: k}) if k else array for k, array in enumerate(arrays)]


def shards(
    moe_input,
    expert_ids,
    route_weight,
    expert_slot,
    w_gate_up,
    w_down,
    queries,
    incoming_key_value,
    key_value_pool,
    block_owner,
    block_tokens,
):
    slot_row = expert_slot.reshape(1, SLOTS)
    packed = call(pack_kernel, "pack", shape((RING, TOK, D + EXTRA)), 3)(
        moe_input, expert_ids.T, route_weight.T
    )
    own_queries = queries.reshape(REQUESTS * HEADS, HEAD)
    near = exchange(packed, RING_GROUPS)
    all_queries = doubled(doubled(own_queries, fx=2), fx=1)
    all_queries = doubled(doubled(all_queries, fz=2), fz=1)
    near, all_queries = lax.optimization_barrier((near, all_queries))
    send = call(dispatch_kernel, "dispatch", shape((REACH, ROWS, D)), 2)(near, slot_row)
    received = exchange(send, REACH_GROUPS)

    other_gate_up, other_down = moved(w_gate_up, dc=1), moved(w_down, dc=1)
    partials = partial_attention(block_owner, block_tokens, all_queries, key_value_pool)
    across = spread(partials, "dx")
    rows = expert(
        received.reshape(REACH * ROWS, D), w_gate_up, other_gate_up, w_down, other_down
    )
    rows, across = lax.optimization_barrier((rows, across))
    returned = exchange(rows.reshape(REACH, ROWS, D), REACH_GROUPS)

    mix = call(mixing_kernel, "mixing", shape((2 * NEAR, REACH * ROWS)), 2)(near, slot_row)
    met = call(
        merge_kernel,
        "merge",
        [shape((1, MESSAGE, HEAD))] * SIDE,
        4,
        out_specs=whole(SIDE),
    )(*across)
    met = spread(met, "dz")
    parts = call(combine_kernel, "combine", shape((RING, TOK, D)), 2)(mix, returned)
    parts, met = lax.optimization_barrier((parts, met))
    parts = exchange(parts, RING_GROUPS)
    attn_out = call(finish_kernel, "finish", shape((REQUESTS, HEADS * HEAD)), 6)(
        *met, own_queries, incoming_key_value
    )
    moe_out = call(total_kernel, "total", shape((TOK, D)), 1)(parts)
    return (moe_out, attn_out)


def solution(mesh):
    flat = Mesh(mesh.devices.reshape(-1), (AXIS,))
    rows = P(AXIS, None)
    placed = (
        rows,
        rows,
        rows,
        P(),
        P(None, AXIS),
        rows,
        rows,
        rows,
        P(AXIS, None, None),
        P(AXIS),
        P(AXIS),
    )
    return jax.shard_map(
        shards, mesh=flat, in_specs=placed, out_specs=(rows, rows), check_vma=False
    )
```

```python
import math

import jax
import jax.numpy as jnp
from jax import lax
from jax.experimental import pallas as pl
from jax.experimental.pallas import tpu as pltpu
from jax.sharding import Mesh
from jax.sharding import PartitionSpec as P

D = 2048
TOK = 16
TOP = 8
SLOTS = 128
RING = 8
REACH = 32
ROWS = 16
NEAR = RING * TOK
EXTRA = 256
HALF = 192
HEADS = 64
GROUPS = 4
HEAD = 128
REQUESTS = 2
SIDE = 4
BLOCKS = 16
LEN = 64
KV = GROUPS * HEAD
NEG = -1e30
STAT = 16
MESSAGE = REQUESTS * HEADS + STAT

F32 = jnp.float32
BF16 = jnp.bfloat16
VMEM_LIMIT = 62 * 1024 * 1024
AXIS = "d"


def number(x, zl, y, zh, c):
    return (x * 4 + zl) * 32 + y * 4 + zh * 2 + c


def position(device):
    return device >> 7, (device >> 5) & 3, (device >> 2) & 7, (device >> 1) & 1, device & 1


RING_GROUPS = [
    [number(x, z % 4, y, z // 4, 0) for z in range(8)] for x in range(4) for y in range(8)
] + [
    [number(x, z % 4, y, z // 4, 1) for y in range(8)] for x in range(4) for z in range(8)
]
REACH_GROUPS = [
    [number(x, z % 4, y, z // 4, 0) for x in range(4) for y in range(8)] for z in range(8)
] + [
    [number(x, z % 4, y, z // 4, 1) for x in range(4) for z in range(8)] for y in range(8)
]


def exchange(array, groups):
    return lax.all_to_all(
        array, AXIS, split_axis=0, concat_axis=0, axis_index_groups=groups, tiled=True
    )


def moved(array, dx=0, dz=0, dc=0):
    pairs = []
    for device in range(512):
        x, zl, y, zh, c = position(device)
        pairs.append((device, number((x + dx) % 4, (zl + dz) % 4, y, zh, (c + dc) % 2)))
    return lax.ppermute(array, AXIS, pairs)


def iota(shape, dim):
    return lax.broadcasted_iota(jnp.int32, shape, dim)


def whole(count):
    return [pl.BlockSpec(memory_space=pltpu.VMEM)] * count


def one(condition):
    return jnp.where(condition, 1.0, 0.0).astype(BF16)


def split(value):
    high = value.astype(BF16)
    rest = value - high.astype(F32)
    middle = rest.astype(BF16)
    return high, middle, (rest - middle.astype(F32)).astype(BF16)


def call(kernel, name, shapes, inputs, **more):
    return pl.pallas_call(
        kernel,
        name=name,
        out_shape=shapes,
        in_specs=more.pop("in_specs", whole(inputs)),
        out_specs=more.pop("out_specs", whole(1)[0]),
        compiler_params=pltpu.CompilerParams(vmem_limit_bytes=VMEM_LIMIT),
        **more,
    )


def shape(dims, kind=BF16):
    return jax.ShapeDtypeStruct(dims, kind)


def pack_kernel(token_ref, ids_ref, weight_ref, out_ref):
    x, zl, y, zh, c = position(lax.axis_index(AXIS))
    mine = jnp.where(c == 0, zh * 4 + zl, y)
    put = one(iota((TOK, NEAR), 1) == iota((TOK, NEAR), 0) + mine * TOK)
    ids = ids_ref[...].astype(F32).astype(BF16)
    parts = [jnp.dot(p, put, preferred_element_type=F32) for p in (ids,) + split(weight_ref[...])]
    left = jnp.concatenate(parts[:2], axis=0).astype(BF16)
    right = jnp.concatenate(parts[2:], axis=0).astype(BF16)
    for u in range(RING):
        out_ref[u, :, :D] = token_ref[...]
        out_ref[u, :, D : D + NEAR] = left
        out_ref[u, :, D + NEAR :] = right


def reached(slot_ref):
    x, zl, y, zh, c = position(lax.axis_index(AXIS))
    d = iota((REACH, SLOTS), 0)
    across, along = d >> 3, d & 7
    at_zl = jnp.where(c == 0, zl, along & 3)
    at_y = jnp.where(c == 0, along, y)
    return one(slot_ref[...] == (across * 4 + at_zl) * 8 + at_y)


def routing(near_ref, slot_ref):
    head = jnp.sum(near_ref[:, :, D:].astype(F32), axis=0)
    ids, weights = head[:TOP, :NEAR], (head[TOP:, :NEAR], head[:TOP, NEAR:], head[TOP:, NEAR:])
    expert = iota((SLOTS, NEAR), 0).astype(F32)
    hits = [ids[k : k + 1] == expert for k in range(TOP)]
    chosen = jnp.zeros((SLOTS, NEAR), F32)
    for hit in hits:
        chosen = chosen + jnp.where(hit, 1.0, 0.0)
    here = reached(slot_ref)
    mine = jnp.dot(here, chosen.astype(BF16), preferred_element_type=F32)
    earlier = one(iota((NEAR, NEAR), 0) < iota((NEAR, NEAR), 1))
    rank = jnp.dot(mine.astype(BF16), earlier, preferred_element_type=F32)
    place = jnp.where(mine > 0.5, rank, -1.0)
    taken = place[:, None, :] == iota((1, ROWS, NEAR), 1).astype(F32)
    return hits, weights, here, taken


def dispatch_kernel(near_ref, slot_ref, out_ref):
    _, _, _, taken = routing(near_ref, slot_ref)
    pick = jnp.where(taken, 1.0, 0.0).reshape(REACH * ROWS, NEAR).astype(BF16)
    tokens = near_ref[:, :, :D].reshape(NEAR, D)
    rows = jnp.dot(pick, tokens, preferred_element_type=F32)
    out_ref[...] = rows.astype(BF16).reshape(REACH, ROWS, D)


def mixing_kernel(near_ref, slot_ref, out_ref):
    hits, weights, here, taken = routing(near_ref, slot_ref)
    total = jnp.zeros((REACH, NEAR), F32)
    for part in weights:
        spread = jnp.zeros((SLOTS, NEAR), F32)
        for k in range(TOP):
            spread = spread + jnp.where(hits[k], part[k : k + 1], 0.0)
        total = total + jnp.dot(here, spread.astype(BF16), preferred_element_type=F32)
    mix = jnp.where(taken, total[:, None, :], 0.0).reshape(REACH * ROWS, NEAR).T
    high, low, _ = split(mix)
    out_ref[:NEAR] = high
    out_ref[NEAR:] = low


def combine_kernel(mix_ref, rows_ref, out_ref):
    rows = rows_ref[...].reshape(REACH * ROWS, D)
    both = jnp.dot(mix_ref[...], rows, preferred_element_type=F32)
    out_ref[...] = (both[:NEAR] + both[NEAR:]).astype(BF16).reshape(RING, TOK, D)


def total_kernel(parts_ref, out_ref):
    out_ref[...] = jnp.sum(parts_ref[...].astype(F32), axis=0).astype(BF16)


ROW_STEP = 256


def expert_kernel(rows_ref, gate_up_ref, other_gate_up_ref, down_ref, other_down_ref, out_ref):
    x = rows_ref[...]
    total = jnp.zeros((ROW_STEP, D), F32)
    for both_ref, back_ref in ((gate_up_ref, down_ref), (other_gate_up_ref, other_down_ref)):
        both = jnp.dot(x, both_ref[...], preferred_element_type=F32)
        gate, up = both[:, :HALF], both[:, HALF:]
        act = (gate / (1.0 + jnp.exp(-gate)) * up).astype(BF16)
        total = total + jnp.dot(act, back_ref[...], preferred_element_type=F32)
    out_ref[...] = total.astype(BF16)


def expert(rows, *weights):
    step = pl.BlockSpec((ROW_STEP, D), lambda i: (i, 0))
    fixed = [pl.BlockSpec(w.shape, lambda i: (0, 0)) for w in weights]
    return call(
        expert_kernel,
        "expert",
        shape(rows.shape),
        5,
        grid=(rows.shape[0] // ROW_STEP,),
        in_specs=[step] + fixed,
        out_specs=step,
    )(rows, *weights)


def write_states(ref, r, states):
    lane, row = iota((HEADS, HEAD), 1), iota((HEADS, HEAD), 0)
    line = iota((STAT, HEAD), 0)
    stats = jnp.zeros((STAT, HEAD), F32)
    for i, (top, total, mixed) in enumerate(states):
        ref[r, i * HEADS : (i + 1) * HEADS, :] = mixed.astype(BF16)
        flat = jnp.where(lane == row, top, 0.0) + jnp.where(lane == row + HEADS, total, 0.0)
        flat = jnp.sum(flat, axis=0, keepdims=True)
        for part, value in enumerate(split(flat)):
            stats = jnp.where(line == i * 3 + part, value.astype(F32), stats)
    ref[r, REQUESTS * HEADS :, :] = stats.astype(BF16)


def read_state(ref, r, i):
    lane, row = iota((HEADS, HEAD), 1), iota((HEADS, HEAD), 0)
    stats = ref[r, REQUESTS * HEADS :, :].astype(F32)
    flat = stats[i * 3 : i * 3 + 1] + stats[i * 3 + 1 : i * 3 + 2] + stats[i * 3 + 2 : i * 3 + 3]
    top = jnp.sum(jnp.where(lane == row, flat, 0.0), axis=1, keepdims=True)
    total = jnp.sum(jnp.where(lane == row + HEADS, flat, 0.0), axis=1, keepdims=True)
    return top, total, ref[r, i * HEADS : (i + 1) * HEADS, :].astype(F32)


def merged(states):
    best = states[0][0]
    for top, _, _ in states[1:]:
        best = jnp.maximum(best, top)
    sums, acc = 0.0, 0.0
    for top, total, mixed in states:
        factor = jnp.exp(top - best)
        sums = sums + factor * total
        acc = acc + factor * mixed
    return best, sums, acc


def merge_kernel(got0_ref, got1_ref, got2_ref, got3_ref, *sends):
    refs = (got0_ref, got1_ref, got2_ref, got3_ref)
    for r in range(SIDE):
        write_states(
            sends[r],
            0,
            [merged([read_state(ref, r, i) for ref in refs]) for i in range(REQUESTS)],
        )


def partial_kernel(owner_ref, count_ref, query_ref, pool_ref, *refs):
    sends, (top_ref, sum_ref, acc_ref) = refs[:SIDE], refs[SIDE:]
    scale = 1.0 / math.sqrt(HEAD)
    top_ref[...] = jnp.full(top_ref.shape, NEG, F32)
    sum_ref[...] = jnp.zeros(sum_ref.shape, F32)
    acc_ref[...] = jnp.zeros(acc_ref.shape, F32)
    x, zl, _, _, _ = position(lax.axis_index(AXIS))
    per = HEADS // GROUPS
    own = iota((HEADS, KV), 1) // HEAD == iota((HEADS, KV), 0) // per
    slot = iota((HEADS, LEN), 1)
    for b in range(BLOCKS):
        owner = owner_ref[b]
        ax, az, request = owner >> 3, (owner >> 1) & 3, owner & 1
        asked = ((x - ax) & 3) * 8 + ((zl - az) & 3) * 2 + request
        state = ((ax - x) & 3) * 8 + ((az - zl) & 3) * 2 + request
        rows = pl.ds(pl.multiple_of(state * HEADS, HEADS), HEADS)
        query = query_ref[pl.ds(pl.multiple_of(asked * HEADS, HEADS), HEADS), :]
        wide = jnp.where(own, jnp.concatenate([query] * GROUPS, axis=1), jnp.zeros((), BF16))
        score = (
            lax.dot_general(
                wide, pool_ref[b, :, :KV], (((1,), (1,)), ((), ())), preferred_element_type=F32
            )
            * scale
        )
        keep = slot < count_ref[b]
        score = jnp.where(keep, score, NEG)
        top = jnp.max(score, axis=1, keepdims=True)
        weight = jnp.where(keep, jnp.exp(score - top), 0.0)
        total = jnp.sum(weight, axis=1, keepdims=True)
        high, low, _ = split(weight)
        mixed = jnp.dot(
            jnp.concatenate([high, low], axis=0), pool_ref[b, :, KV:], preferred_element_type=F32
        )
        mixed = mixed[:HEADS] + mixed[HEADS:]
        mixed = jnp.concatenate(
            [mixed[g * per : (g + 1) * per, g * HEAD : (g + 1) * HEAD] for g in range(GROUPS)],
            axis=0,
        )
        old = top_ref[rows, :]
        best = jnp.maximum(old, top)
        keep_old, add_new = jnp.exp(old - best), jnp.exp(top - best)
        top_ref[rows, :] = best
        sum_ref[rows, :] = keep_old * sum_ref[rows, :] + add_new * total
        acc_ref[rows, :] = keep_old * acc_ref[rows, :] + add_new * mixed
    for r in range(SIDE * SIDE):
        states = []
        for i in range(REQUESTS):
            at = (r * REQUESTS + i) * HEADS
            rows = slice(at, at + HEADS)
            states.append((top_ref[rows, :], sum_ref[rows, :], acc_ref[rows, :]))
        write_states(sends[r // SIDE], r % SIDE, states)


def partial_attention(owner, count, queries, pool):
    smem = pl.BlockSpec(memory_space=pltpu.SMEM)
    return call(
        partial_kernel,
        "partial_attention",
        [shape((SIDE, MESSAGE, HEAD))] * SIDE,
        4,
        in_specs=[smem, smem] + whole(2),
        out_specs=whole(SIDE),
        scratch_shapes=[pltpu.VMEM((SIDE * SIDE * REQUESTS * HEADS, HEAD), F32)] * 3,
    )(owner, count, queries, pool)


def finish_kernel(got0_ref, got1_ref, got2_ref, got3_ref, query_ref, new_ref, out_ref):
    scale = 1.0 / math.sqrt(HEAD)
    per = HEADS // GROUPS

    def by_head(line):
        return jnp.concatenate(
            [
                jnp.broadcast_to(line[:, g * HEAD : (g + 1) * HEAD], (per, HEAD))
                for g in range(GROUPS)
            ],
            axis=0,
        )

    answers = []
    for i in range(REQUESTS):
        query = query_ref[i * HEADS : (i + 1) * HEADS, :].astype(F32)
        key = by_head(new_ref[i : i + 1, :KV].astype(F32))
        value = by_head(new_ref[i : i + 1, KV:].astype(F32))
        own = jnp.sum(query * key, axis=1, keepdims=True) * scale
        states = [(own, jnp.ones((HEADS, 1), F32), value)]
        states += [read_state(ref, 0, i) for ref in (got0_ref, got1_ref, got2_ref, got3_ref)]
        _, total, mixed = merged(states)
        answers.append(mixed / total)
    for h in range(HEADS):
        pair = jnp.concatenate([part[h : h + 1] for part in answers], axis=0)
        out_ref[:, h * HEAD : (h + 1) * HEAD] = pair.astype(BF16)


def along(array, axis):
    return [array] + [moved(array, **{axis: k}) for k in range(1, SIDE)]


def spread(arrays, axis):
    return [moved(array, **{axis: k}) if k else array for k, array in enumerate(arrays)]


def shards(
    moe_input,
    expert_ids,
    route_weight,
    expert_slot,
    w_gate_up,
    w_down,
    queries,
    incoming_key_value,
    key_value_pool,
    block_owner,
    block_tokens,
):
    slot_row = expert_slot.reshape(1, SLOTS)
    packed = call(pack_kernel, "pack", shape((RING, TOK, D + EXTRA)), 3)(
        moe_input, expert_ids.T, route_weight.T
    )
    own_queries = queries.reshape(REQUESTS * HEADS, HEAD)
    near = exchange(packed, RING_GROUPS)
    line = jnp.concatenate(along(own_queries, "dz"), axis=0)
    near, line = lax.optimization_barrier((near, line))
    send = call(dispatch_kernel, "dispatch", shape((REACH, ROWS, D)), 2)(near, slot_row)
    received = exchange(send, REACH_GROUPS)

    other_gate_up, other_down = moved(w_gate_up, dc=1), moved(w_down, dc=1)
    square = along(line, "dx")
    rows = expert(
        received.reshape(REACH * ROWS, D), w_gate_up, other_gate_up, w_down, other_down
    )
    rows, square = lax.optimization_barrier((rows, square))
    returned = exchange(rows.reshape(REACH, ROWS, D), REACH_GROUPS)

    partials = partial_attention(
        block_owner, block_tokens, jnp.concatenate(square, axis=0), key_value_pool
    )
    across = spread(partials, "dx")
    mix = call(mixing_kernel, "mixing", shape((2 * NEAR, REACH * ROWS)), 2)(near, slot_row)
    parts = call(combine_kernel, "combine", shape((RING, TOK, D)), 2)(mix, returned)
    parts, across = lax.optimization_barrier((parts, across))
    parts = exchange(parts, RING_GROUPS)

    met = call(
        merge_kernel,
        "merge",
        [shape((1, MESSAGE, HEAD))] * SIDE,
        4,
        out_specs=whole(SIDE),
    )(*across)
    attn_out = call(finish_kernel, "finish", shape((REQUESTS, HEADS * HEAD)), 6)(
        *spread(met, "dz"), own_queries, incoming_key_value
    )
    moe_out = call(total_kernel, "total", shape((TOK, D)), 1)(parts)
    return (moe_out, attn_out)


def solution(mesh):
    flat = Mesh(mesh.devices.reshape(-1), (AXIS,))
    rows = P(AXIS, None)
    placed = (
        rows,
        rows,
        rows,
        P(),
        P(None, AXIS),
        rows,
        rows,
        rows,
        P(AXIS, None, None),
        P(AXIS),
        P(AXIS),
    )
    return jax.shard_map(
        shards, mesh=flat, in_specs=placed, out_specs=(rows, rows), check_vma=False
    )
```

```python
import math

import jax
import jax.numpy as jnp
from jax import lax
from jax.experimental import pallas as pl
from jax.experimental.pallas import tpu as pltpu
from jax.sharding import Mesh
from jax.sharding import PartitionSpec as P

D = 2048
TOK = 16
TOP = 8
SLOTS = 128
RING = 8
REACH = 32
ROWS = 16
NEAR = RING * TOK
EXTRA = 256
HALF = 192
HEADS = 64
GROUPS = 4
HEAD = 128
REQUESTS = 2
SIDE = 4
BLOCKS = 16
LEN = 64
KV = GROUPS * HEAD
NEG = -1e30
STAT = 16
MESSAGE = REQUESTS * HEADS + STAT

F32 = jnp.float32
BF16 = jnp.bfloat16
VMEM_LIMIT = 32 * 1024 * 1024
VMEM_MOST = 60 * 1024 * 1024
VMEM_ALL = 62 * 1024 * 1024
AXIS = "d"


def number(x, zl, y, zh, c):
    return (x * 4 + zl) * 32 + y * 4 + zh * 2 + c


def position(device):
    return device >> 7, (device >> 5) & 3, (device >> 2) & 7, (device >> 1) & 1, device & 1


RING_GROUPS = [
    [number(x, z % 4, y, z // 4, 0) for z in range(8)] for x in range(4) for y in range(8)
] + [
    [number(x, z % 4, y, z // 4, 1) for y in range(8)] for x in range(4) for z in range(8)
]
REACH_GROUPS = [
    [number(x, z % 4, y, z // 4, 0) for x in range(4) for y in range(8)] for z in range(8)
] + [
    [number(x, z % 4, y, z // 4, 1) for x in range(4) for z in range(8)] for y in range(8)
]


def exchange(array, groups):
    return lax.all_to_all(
        array, AXIS, split_axis=0, concat_axis=0, axis_index_groups=groups, tiled=True
    )


def moved(array, dx=0, dz=0, dc=0):
    pairs = []
    for device in range(512):
        x, zl, y, zh, c = position(device)
        pairs.append((device, number((x + dx) % 4, (zl + dz) % 4, y, zh, (c + dc) % 2)))
    return lax.ppermute(array, AXIS, pairs)


def iota(shape, dim):
    return lax.broadcasted_iota(jnp.int32, shape, dim)


def whole(count):
    return [pl.BlockSpec(memory_space=pltpu.VMEM)] * count


def one(condition):
    return jnp.where(condition, 1.0, 0.0).astype(BF16)


def split(value):
    high = value.astype(BF16)
    rest = value - high.astype(F32)
    middle = rest.astype(BF16)
    return high, middle, (rest - middle.astype(F32)).astype(BF16)


def call(kernel, name, shapes, inputs, **more):
    return pl.pallas_call(
        kernel,
        name=name,
        out_shape=shapes,
        in_specs=more.pop("in_specs", whole(inputs)),
        out_specs=more.pop("out_specs", whole(1)[0]),
        compiler_params=pltpu.CompilerParams(vmem_limit_bytes=more.pop("limit", VMEM_LIMIT)),
        **more,
    )


def shape(dims, kind=BF16):
    return jax.ShapeDtypeStruct(dims, kind)


def pack_kernel(token_ref, ids_ref, weight_ref, out_ref):
    x, zl, y, zh, c = position(lax.axis_index(AXIS))
    mine = jnp.where(c == 0, zh * 4 + zl, y)
    put = one(iota((TOK, NEAR), 1) == iota((TOK, NEAR), 0) + mine * TOK)
    ids = ids_ref[...].astype(F32).astype(BF16)
    parts = [jnp.dot(p, put, preferred_element_type=F32) for p in (ids,) + split(weight_ref[...])]
    left = jnp.concatenate(parts[:2], axis=0).astype(BF16)
    right = jnp.concatenate(parts[2:], axis=0).astype(BF16)
    for u in range(RING):
        out_ref[u, :, :D] = token_ref[...]
        out_ref[u, :, D : D + NEAR] = left
        out_ref[u, :, D + NEAR :] = right


def reached(slot_ref):
    x, zl, y, zh, c = position(lax.axis_index(AXIS))
    d = iota((REACH, SLOTS), 0)
    across, along = d >> 3, d & 7
    at_zl = jnp.where(c == 0, zl, along & 3)
    at_y = jnp.where(c == 0, along, y)
    return one(slot_ref[...] == (across * 4 + at_zl) * 8 + at_y)


def routing(near_ref, slot_ref):
    head = jnp.sum(near_ref[:, :, D:].astype(F32), axis=0)
    ids, weights = head[:TOP, :NEAR], (head[TOP:, :NEAR], head[:TOP, NEAR:], head[TOP:, NEAR:])
    expert = iota((SLOTS, NEAR), 0).astype(F32)
    hits = [ids[k : k + 1] == expert for k in range(TOP)]
    chosen = jnp.zeros((SLOTS, NEAR), F32)
    for hit in hits:
        chosen = chosen + jnp.where(hit, 1.0, 0.0)
    here = reached(slot_ref)
    mine = jnp.dot(here, chosen.astype(BF16), preferred_element_type=F32)
    earlier = one(iota((NEAR, NEAR), 0) < iota((NEAR, NEAR), 1))
    rank = jnp.dot(mine.astype(BF16), earlier, preferred_element_type=F32)
    place = jnp.where(mine > 0.5, rank, -1.0)
    taken = place[:, None, :] == iota((1, ROWS, NEAR), 1).astype(F32)
    return hits, weights, here, taken


def dispatch_kernel(near_ref, slot_ref, out_ref):
    _, _, _, taken = routing(near_ref, slot_ref)
    pick = jnp.where(taken, 1.0, 0.0).reshape(REACH * ROWS, NEAR).astype(BF16)
    tokens = near_ref[:, :, :D].reshape(NEAR, D)
    rows = jnp.dot(pick, tokens, preferred_element_type=F32)
    out_ref[...] = rows.astype(BF16).reshape(REACH, ROWS, D)


def mixing_kernel(near_ref, slot_ref, out_ref):
    hits, weights, here, taken = routing(near_ref, slot_ref)
    total = jnp.zeros((REACH, NEAR), F32)
    for part in weights:
        spread = jnp.zeros((SLOTS, NEAR), F32)
        for k in range(TOP):
            spread = spread + jnp.where(hits[k], part[k : k + 1], 0.0)
        total = total + jnp.dot(here, spread.astype(BF16), preferred_element_type=F32)
    mix = jnp.where(taken, total[:, None, :], 0.0).reshape(REACH * ROWS, NEAR).T
    high, low, _ = split(mix)
    out_ref[:NEAR] = high
    out_ref[NEAR:] = low


def combine_kernel(mix_ref, rows_ref, out_ref):
    rows = rows_ref[...].reshape(REACH * ROWS, D)
    both = jnp.dot(mix_ref[...], rows, preferred_element_type=F32)
    out_ref[...] = (both[:NEAR] + both[NEAR:]).astype(BF16).reshape(RING, TOK, D)


def total_kernel(parts_ref, out_ref):
    out_ref[...] = jnp.sum(parts_ref[...].astype(F32), axis=0).astype(BF16)


EXPERT_STEPS = 2


def expert_kernel(rows_ref, *refs):
    sources, out_ref, held, made_ref, came_sem, left_sem = refs[:4], refs[4], refs[5:9], *refs[9:]
    come = [
        pltpu.make_async_copy(source, kept, came_sem.at[i])
        for i, (source, kept) in enumerate(zip(sources, held))
    ]
    for copy in come:
        copy.start()
    step = REACH // EXPERT_STEPS
    leave = []
    for s in range(EXPERT_STEPS):
        x = rows_ref[s * step : (s + 1) * step].reshape(step * ROWS, D)
        total = jnp.zeros((step * ROWS, D), F32)
        for pair in range(2):
            if s == 0:
                come[2 * pair].wait()
            both = jnp.dot(x, held[2 * pair][...], preferred_element_type=F32)
            gate, up = both[:, :HALF], both[:, HALF:]
            act = (gate / (1.0 + jnp.exp(-gate)) * up).astype(BF16)
            if s == 0:
                come[2 * pair + 1].wait()
            total = total + jnp.dot(act, held[2 * pair + 1][...], preferred_element_type=F32)
        made_ref[s] = total.astype(BF16).reshape(step, ROWS, D)
        leave.append(
            pltpu.make_async_copy(
                made_ref.at[s], out_ref.at[s * step : (s + 1) * step], left_sem.at[s]
            )
        )
        leave[-1].start()
    for copy in leave:
        copy.wait()


def on_core(array):
    return pltpu.with_memory_space_constraint(array, pltpu.VMEM)


def expert(rows, *weights):
    apart = pl.BlockSpec(memory_space=pltpu.HBM)
    return call(
        expert_kernel,
        "expert",
        shape(rows.shape),
        5,
        in_specs=whole(1) + [apart] * 4,
        out_specs=apart,
        limit=VMEM_MOST,
        scratch_shapes=[pltpu.VMEM(w.shape, BF16) for w in weights]
        + [
            pltpu.VMEM((EXPERT_STEPS, REACH // EXPERT_STEPS, ROWS, D), BF16),
            pltpu.SemaphoreType.DMA((4,)),
            pltpu.SemaphoreType.DMA((EXPERT_STEPS,)),
        ],
    )(on_core(rows), *weights)


def write_states(ref, r, states):
    lane, row = iota((HEADS, HEAD), 1), iota((HEADS, HEAD), 0)
    line = iota((STAT, HEAD), 0)
    stats = jnp.zeros((STAT, HEAD), F32)
    for i, (top, total, mixed) in enumerate(states):
        ref[r, i * HEADS : (i + 1) * HEADS, :] = mixed.astype(BF16)
        flat = jnp.where(lane == row, top, 0.0) + jnp.where(lane == row + HEADS, total, 0.0)
        flat = jnp.sum(flat, axis=0, keepdims=True)
        for part, value in enumerate(split(flat)):
            stats = jnp.where(line == i * 3 + part, value.astype(F32), stats)
    ref[r, REQUESTS * HEADS :, :] = stats.astype(BF16)


def read_state(ref, r, i):
    lane, row = iota((HEADS, HEAD), 1), iota((HEADS, HEAD), 0)
    stats = ref[r, REQUESTS * HEADS :, :].astype(F32)
    flat = stats[i * 3 : i * 3 + 1] + stats[i * 3 + 1 : i * 3 + 2] + stats[i * 3 + 2 : i * 3 + 3]
    top = jnp.sum(jnp.where(lane == row, flat, 0.0), axis=1, keepdims=True)
    total = jnp.sum(jnp.where(lane == row + HEADS, flat, 0.0), axis=1, keepdims=True)
    return top, total, ref[r, i * HEADS : (i + 1) * HEADS, :].astype(F32)


def merged(states):
    best = states[0][0]
    for top, _, _ in states[1:]:
        best = jnp.maximum(best, top)
    sums, acc = 0.0, 0.0
    for top, total, mixed in states:
        factor = jnp.exp(top - best)
        sums = sums + factor * total
        acc = acc + factor * mixed
    return best, sums, acc


def merge_kernel(got0_ref, got1_ref, got2_ref, got3_ref, *sends):
    refs = (got0_ref, got1_ref, got2_ref, got3_ref)
    for r in range(SIDE):
        write_states(
            sends[r],
            0,
            [merged([read_state(ref, r, i) for ref in refs]) for i in range(REQUESTS)],
        )


def partial_kernel(owner_ref, count_ref, query_ref, pool_ref, *refs):
    sends, (top_ref, sum_ref, acc_ref) = refs[:SIDE], refs[SIDE:]
    scale = 1.0 / math.sqrt(HEAD)
    top_ref[...] = jnp.full(top_ref.shape, NEG, F32)
    sum_ref[...] = jnp.zeros(sum_ref.shape, F32)
    acc_ref[...] = jnp.zeros(acc_ref.shape, F32)
    x, zl, _, _, _ = position(lax.axis_index(AXIS))
    per = HEADS // GROUPS
    own = iota((HEADS, KV), 1) // HEAD == iota((HEADS, KV), 0) // per
    slot = iota((HEADS, LEN), 1)
    for b in range(BLOCKS):
        owner = owner_ref[b]
        ax, az, request = owner >> 3, (owner >> 1) & 3, owner & 1
        asked = ((x - ax) & 3) * 8 + ((zl - az) & 3) * 2 + request
        state = ((ax - x) & 3) * 8 + ((az - zl) & 3) * 2 + request
        rows = pl.ds(pl.multiple_of(state * HEADS, HEADS), HEADS)
        query = query_ref[pl.ds(pl.multiple_of(asked * HEADS, HEADS), HEADS), :]
        wide = jnp.where(own, jnp.concatenate([query] * GROUPS, axis=1), jnp.zeros((), BF16))
        score = (
            lax.dot_general(
                wide, pool_ref[b, :, :KV], (((1,), (1,)), ((), ())), preferred_element_type=F32
            )
            * scale
        )
        keep = slot < count_ref[b]
        score = jnp.where(keep, score, NEG)
        top = jnp.max(score, axis=1, keepdims=True)
        weight = jnp.where(keep, jnp.exp(score - top), 0.0)
        total = jnp.sum(weight, axis=1, keepdims=True)
        high, low, _ = split(weight)
        mixed = jnp.dot(
            jnp.concatenate([high, low], axis=0), pool_ref[b, :, KV:], preferred_element_type=F32
        )
        mixed = mixed[:HEADS] + mixed[HEADS:]
        mixed = jnp.concatenate(
            [mixed[g * per : (g + 1) * per, g * HEAD : (g + 1) * HEAD] for g in range(GROUPS)],
            axis=0,
        )
        old = top_ref[rows, :]
        best = jnp.maximum(old, top)
        keep_old, add_new = jnp.exp(old - best), jnp.exp(top - best)
        top_ref[rows, :] = best
        sum_ref[rows, :] = keep_old * sum_ref[rows, :] + add_new * total
        acc_ref[rows, :] = keep_old * acc_ref[rows, :] + add_new * mixed
    for r in range(SIDE * SIDE):
        states = []
        for i in range(REQUESTS):
            at = (r * REQUESTS + i) * HEADS
            rows = slice(at, at + HEADS)
            states.append((top_ref[rows, :], sum_ref[rows, :], acc_ref[rows, :]))
        write_states(sends[r // SIDE], r % SIDE, states)


def partial_attention(owner, count, queries, pool):
    smem = pl.BlockSpec(memory_space=pltpu.SMEM)
    return call(
        partial_kernel,
        "partial_attention",
        [shape((SIDE, MESSAGE, HEAD))] * SIDE,
        4,
        in_specs=[smem, smem] + whole(2),
        out_specs=whole(SIDE),
        scratch_shapes=[pltpu.VMEM((SIDE * SIDE * REQUESTS * HEADS, HEAD), F32)] * 3,
    )(owner, count, queries, pool)


def finish_kernel(got0_ref, got1_ref, got2_ref, got3_ref, query_ref, new_ref, out_ref):
    scale = 1.0 / math.sqrt(HEAD)
    per = HEADS // GROUPS

    def by_head(line):
        return jnp.concatenate(
            [
                jnp.broadcast_to(line[:, g * HEAD : (g + 1) * HEAD], (per, HEAD))
                for g in range(GROUPS)
            ],
            axis=0,
        )

    answers = []
    for i in range(REQUESTS):
        query = query_ref[i * HEADS : (i + 1) * HEADS, :].astype(F32)
        key = by_head(new_ref[i : i + 1, :KV].astype(F32))
        value = by_head(new_ref[i : i + 1, KV:].astype(F32))
        own = jnp.sum(query * key, axis=1, keepdims=True) * scale
        states = [(own, jnp.ones((HEADS, 1), F32), value)]
        states += [read_state(ref, 0, i) for ref in (got0_ref, got1_ref, got2_ref, got3_ref)]
        _, total, mixed = merged(states)
        answers.append(mixed / total)
    for h in range(HEADS):
        pair = jnp.concatenate([part[h : h + 1] for part in answers], axis=0)
        out_ref[:, h * HEAD : (h + 1) * HEAD] = pair.astype(BF16)


def along(array, axis):
    return [array] + [moved(array, **{axis: k}) for k in range(1, SIDE)]


def spread(arrays, axis):
    return [moved(array, **{axis: k}) if k else array for k, array in enumerate(arrays)]


def shards(
    moe_input,
    expert_ids,
    route_weight,
    expert_slot,
    w_gate_up,
    w_down,
    queries,
    incoming_key_value,
    key_value_pool,
    block_owner,
    block_tokens,
):
    slot_row = expert_slot.reshape(1, SLOTS)
    packed = call(pack_kernel, "pack", shape((RING, TOK, D + EXTRA)), 3, limit=VMEM_ALL)(
        moe_input, expert_ids.T, route_weight.T
    )
    own_queries = queries.reshape(REQUESTS * HEADS, HEAD)
    near = exchange(packed, RING_GROUPS)
    line = along(own_queries, "dz")
    send = call(dispatch_kernel, "dispatch", shape((REACH, ROWS, D)), 2, limit=VMEM_ALL)(
        near, slot_row
    )
    send, line = lax.optimization_barrier((send, line))
    line = jnp.concatenate(line, axis=0)
    received = exchange(send, REACH_GROUPS)

    other_gate_up, other_down = moved(w_gate_up, dc=1), moved(w_down, dc=1)
    square = along(line, "dx")
    rows = expert(
        received, w_gate_up, w_down, other_gate_up, other_down
    )
    rows, square = lax.optimization_barrier((rows, square))
    returned = exchange(rows, REACH_GROUPS)

    partials = partial_attention(
        block_owner, block_tokens, jnp.concatenate(square, axis=0), key_value_pool
    )
    across = spread(partials, "dx")
    mix = call(mixing_kernel, "mixing", shape((2 * NEAR, REACH * ROWS)), 2)(near, slot_row)
    parts = call(combine_kernel, "combine", shape((RING, TOK, D)), 2)(mix, on_core(returned))
    parts, across = lax.optimization_barrier((parts, across))
    parts = exchange(parts, RING_GROUPS)

    met = call(
        merge_kernel,
        "merge",
        [shape((1, MESSAGE, HEAD))] * SIDE,
        4,
        out_specs=whole(SIDE),
    )(*across)
    attn_out = call(finish_kernel, "finish", shape((REQUESTS, HEADS * HEAD)), 6)(
        *spread(met, "dz"), own_queries, incoming_key_value
    )
    moe_out = call(total_kernel, "total", shape((TOK, D)), 1)(parts)
    return (moe_out, attn_out)


def solution(mesh):
    flat = Mesh(mesh.devices.reshape(-1), (AXIS,))
    rows = P(AXIS, None)
    placed = (
        rows,
        rows,
        rows,
        P(),
        P(None, AXIS),
        rows,
        rows,
        rows,
        P(AXIS, None, None),
        P(AXIS),
        P(AXIS),
    )
    return jax.shard_map(
        shards, mesh=flat, in_specs=placed, out_specs=(rows, rows), check_vma=False
    )
```

```python
import math

import jax
import jax.numpy as jnp
from jax import lax
from jax.experimental import pallas as pl
from jax.experimental.pallas import tpu as pltpu
from jax.sharding import Mesh
from jax.sharding import PartitionSpec as P

D = 2048
TOK = 16
TOP = 8
SLOTS = 128
RING = 8
REACH = 32
ROWS = 16
NEAR = RING * TOK
EXTRA = 256
HALF = 192
HEADS = 64
GROUPS = 4
HEAD = 128
REQUESTS = 2
SIDE = 4
BLOCKS = 16
LEN = 64
KV = GROUPS * HEAD
NEG = -1e30
STAT = 16
MESSAGE = REQUESTS * HEADS + STAT

F32 = jnp.float32
BF16 = jnp.bfloat16
VMEM_LIMIT = 32 * 1024 * 1024
VMEM_MOST = 60 * 1024 * 1024
VMEM_ALL = 62 * 1024 * 1024
AXIS = "d"


def number(x, zl, y, zh, c):
    return (x * 4 + zl) * 32 + y * 4 + zh * 2 + c


def position(device):
    return device >> 7, (device >> 5) & 3, (device >> 2) & 7, (device >> 1) & 1, device & 1


RING_GROUPS = [
    [number(x, z % 4, y, z // 4, 0) for z in range(8)] for x in range(4) for y in range(8)
] + [
    [number(x, z % 4, y, z // 4, 1) for y in range(8)] for x in range(4) for z in range(8)
]
REACH_GROUPS = [
    [number(x, z % 4, y, z // 4, 0) for x in range(4) for y in range(8)] for z in range(8)
] + [
    [number(x, z % 4, y, z // 4, 1) for x in range(4) for z in range(8)] for y in range(8)
]


def exchange(array, groups):
    return lax.all_to_all(
        array, AXIS, split_axis=0, concat_axis=0, axis_index_groups=groups, tiled=True
    )


def moved(array, first=0, second=0, core=0):
    pairs = []
    for device in range(512):
        x, zl, y, zh, c = position(device)
        dx, dz = (first, second) if c else (second, first)
        pairs.append((device, number((x + dx) % 4, (zl + dz) % 4, y, zh, (c + core) % 2)))
    return lax.ppermute(array, AXIS, pairs)


def iota(shape, dim):
    return lax.broadcasted_iota(jnp.int32, shape, dim)


def whole(count):
    return [pl.BlockSpec(memory_space=pltpu.VMEM)] * count


def one(condition):
    return jnp.where(condition, 1.0, 0.0).astype(BF16)


def split(value):
    high = value.astype(BF16)
    rest = value - high.astype(F32)
    middle = rest.astype(BF16)
    return high, middle, (rest - middle.astype(F32)).astype(BF16)


def call(kernel, name, shapes, inputs, **more):
    return pl.pallas_call(
        kernel,
        name=name,
        out_shape=shapes,
        in_specs=more.pop("in_specs", whole(inputs)),
        out_specs=more.pop("out_specs", whole(1)[0]),
        compiler_params=pltpu.CompilerParams(vmem_limit_bytes=more.pop("limit", VMEM_LIMIT)),
        **more,
    )


def shape(dims, kind=BF16):
    return jax.ShapeDtypeStruct(dims, kind)


def pack_kernel(token_ref, ids_ref, weight_ref, out_ref):
    x, zl, y, zh, c = position(lax.axis_index(AXIS))
    mine = jnp.where(c == 0, zh * 4 + zl, y)
    put = one(iota((TOK, NEAR), 1) == iota((TOK, NEAR), 0) + mine * TOK)
    ids = ids_ref[...].astype(F32).astype(BF16)
    parts = [jnp.dot(p, put, preferred_element_type=F32) for p in (ids,) + split(weight_ref[...])]
    left = jnp.concatenate(parts[:2], axis=0).astype(BF16)
    right = jnp.concatenate(parts[2:], axis=0).astype(BF16)
    for u in range(RING):
        out_ref[u, :, :D] = token_ref[...]
        out_ref[u, :, D : D + NEAR] = left
        out_ref[u, :, D + NEAR :] = right


def reached(slot_ref):
    x, zl, y, zh, c = position(lax.axis_index(AXIS))
    d = iota((REACH, SLOTS), 0)
    across, along = d >> 3, d & 7
    at_zl = jnp.where(c == 0, zl, along & 3)
    at_y = jnp.where(c == 0, along, y)
    return one(slot_ref[...] == (across * 4 + at_zl) * 8 + at_y)


def routing(near_ref, slot_ref):
    head = jnp.sum(near_ref[:, :, D:].astype(F32), axis=0)
    ids, weights = head[:TOP, :NEAR], (head[TOP:, :NEAR], head[:TOP, NEAR:], head[TOP:, NEAR:])
    expert = iota((SLOTS, NEAR), 0).astype(F32)
    hits = [ids[k : k + 1] == expert for k in range(TOP)]
    chosen = jnp.zeros((SLOTS, NEAR), F32)
    for hit in hits:
        chosen = chosen + jnp.where(hit, 1.0, 0.0)
    here = reached(slot_ref)
    mine = jnp.dot(here, chosen.astype(BF16), preferred_element_type=F32)
    earlier = one(iota((NEAR, NEAR), 0) < iota((NEAR, NEAR), 1))
    rank = jnp.dot(mine.astype(BF16), earlier, preferred_element_type=F32)
    place = jnp.where(mine > 0.5, rank, -1.0)
    taken = place[:, None, :] == iota((1, ROWS, NEAR), 1).astype(F32)
    return hits, weights, here, taken


def dispatch_kernel(near_ref, slot_ref, out_ref):
    _, _, _, taken = routing(near_ref, slot_ref)
    pick = jnp.where(taken, 1.0, 0.0).reshape(REACH * ROWS, NEAR).astype(BF16)
    tokens = near_ref[:, :, :D].reshape(NEAR, D)
    rows = jnp.dot(pick, tokens, preferred_element_type=F32)
    out_ref[...] = rows.astype(BF16).reshape(REACH, ROWS, D)


def mixing_kernel(near_ref, slot_ref, out_ref):
    hits, weights, here, taken = routing(near_ref, slot_ref)
    total = jnp.zeros((REACH, NEAR), F32)
    for part in weights:
        spread = jnp.zeros((SLOTS, NEAR), F32)
        for k in range(TOP):
            spread = spread + jnp.where(hits[k], part[k : k + 1], 0.0)
        total = total + jnp.dot(here, spread.astype(BF16), preferred_element_type=F32)
    mix = jnp.where(taken, total[:, None, :], 0.0).reshape(REACH * ROWS, NEAR).T
    high, low, _ = split(mix)
    out_ref[:NEAR] = high
    out_ref[NEAR:] = low


def combine_kernel(mix_ref, rows_ref, out_ref):
    rows = rows_ref[...].reshape(REACH * ROWS, D)
    both = jnp.dot(mix_ref[...], rows, preferred_element_type=F32)
    out_ref[...] = (both[:NEAR] + both[NEAR:]).astype(BF16).reshape(RING, TOK, D)


def total_kernel(parts_ref, out_ref):
    out_ref[...] = jnp.sum(parts_ref[...].astype(F32), axis=0).astype(BF16)


EXPERT_STEPS = 2


def expert_kernel(rows_ref, *refs):
    sources, out_ref, wide_ref, tall_ref, made_ref, came_sem, left_sem = refs[:4], *refs[4:]
    both, quarter = 2 * HALF, HALF
    places = (
        wide_ref.at[:, :both],
        wide_ref.at[:, both:],
        tall_ref.at[:quarter],
        tall_ref.at[quarter:],
    )
    come = [
        pltpu.make_async_copy(source, place, came_sem.at[i])
        for i, (source, place) in enumerate(zip(sources, places))
    ]
    for copy in come:
        copy.start()
    step = REACH // EXPERT_STEPS
    leave = []
    for s in range(EXPERT_STEPS):
        x = rows_ref[s * step : (s + 1) * step].reshape(step * ROWS, D)
        if s == 0:
            come[0].wait()
            come[1].wait()
        wide = jnp.dot(x, wide_ref[...], preferred_element_type=F32)
        acts = []
        for at in (0, both):
            gate, up = wide[:, at : at + HALF], wide[:, at + HALF : at + both]
            acts.append((gate / (1.0 + jnp.exp(-gate)) * up).astype(BF16))
        act = jnp.concatenate(acts, axis=1)
        if s == 0:
            come[2].wait()
            come[3].wait()
        total = jnp.dot(act, tall_ref[...], preferred_element_type=F32)
        made_ref[s] = total.astype(BF16).reshape(step, ROWS, D)
        leave.append(
            pltpu.make_async_copy(
                made_ref.at[s], out_ref.at[s * step : (s + 1) * step], left_sem.at[s]
            )
        )
        leave[-1].start()
    for copy in leave:
        copy.wait()


def on_core(array):
    return pltpu.with_memory_space_constraint(array, pltpu.VMEM)


def expert(rows, *weights):
    apart = pl.BlockSpec(memory_space=pltpu.HBM)
    return call(
        expert_kernel,
        "expert",
        shape(rows.shape),
        5,
        in_specs=whole(1) + [apart] * 4,
        out_specs=apart,
        limit=VMEM_MOST,
        scratch_shapes=[
            pltpu.VMEM((D, 4 * HALF), BF16),
            pltpu.VMEM((2 * HALF, D), BF16),
            pltpu.VMEM((EXPERT_STEPS, REACH // EXPERT_STEPS, ROWS, D), BF16),
            pltpu.SemaphoreType.DMA((4,)),
            pltpu.SemaphoreType.DMA((EXPERT_STEPS,)),
        ],
    )(on_core(rows), *weights)


def write_states(ref, r, states):
    lane, row = iota((HEADS, HEAD), 1), iota((HEADS, HEAD), 0)
    line = iota((STAT, HEAD), 0)
    stats = jnp.zeros((STAT, HEAD), F32)
    for i, (top, total, mixed) in enumerate(states):
        ref[r, i * HEADS : (i + 1) * HEADS, :] = mixed.astype(BF16)
        flat = jnp.where(lane == row, top, 0.0) + jnp.where(lane == row + HEADS, total, 0.0)
        flat = jnp.sum(flat, axis=0, keepdims=True)
        for part, value in enumerate(split(flat)):
            stats = jnp.where(line == i * 3 + part, value.astype(F32), stats)
    ref[r, REQUESTS * HEADS :, :] = stats.astype(BF16)


def read_state(ref, r, i):
    lane, row = iota((HEADS, HEAD), 1), iota((HEADS, HEAD), 0)
    stats = ref[r, REQUESTS * HEADS :, :].astype(F32)
    flat = stats[i * 3 : i * 3 + 1] + stats[i * 3 + 1 : i * 3 + 2] + stats[i * 3 + 2 : i * 3 + 3]
    top = jnp.sum(jnp.where(lane == row, flat, 0.0), axis=1, keepdims=True)
    total = jnp.sum(jnp.where(lane == row + HEADS, flat, 0.0), axis=1, keepdims=True)
    return top, total, ref[r, i * HEADS : (i + 1) * HEADS, :].astype(F32)


def merged(states):
    best = states[0][0]
    for top, _, _ in states[1:]:
        best = jnp.maximum(best, top)
    sums, acc = 0.0, 0.0
    for top, total, mixed in states:
        factor = jnp.exp(top - best)
        sums = sums + factor * total
        acc = acc + factor * mixed
    return best, sums, acc


def merge_kernel(got0_ref, got1_ref, got2_ref, got3_ref, *sends):
    refs = (got0_ref, got1_ref, got2_ref, got3_ref)
    for r in range(SIDE):
        write_states(
            sends[r],
            0,
            [merged([read_state(ref, r, i) for ref in refs]) for i in range(REQUESTS)],
        )


def pair(x_first, dz, dx):
    return jnp.where(x_first, dz * 4 + dx, dx * 4 + dz)


def partial_kernel(owner_ref, count_ref, query_ref, pool_ref, *refs):
    sends, (top_ref, sum_ref, acc_ref) = refs[:SIDE], refs[SIDE:]
    scale = 1.0 / math.sqrt(HEAD)
    top_ref[...] = jnp.full(top_ref.shape, NEG, F32)
    sum_ref[...] = jnp.zeros(sum_ref.shape, F32)
    acc_ref[...] = jnp.zeros(acc_ref.shape, F32)
    x, zl, _, _, c = position(lax.axis_index(AXIS))
    x_first = c == 1
    per = HEADS // GROUPS
    own = iota((HEADS, KV), 1) // HEAD == iota((HEADS, KV), 0) // per
    slot = iota((HEADS, LEN), 1)
    for b in range(BLOCKS):
        owner = owner_ref[b]
        ax, az, request = owner >> 3, (owner >> 1) & 3, owner & 1
        asked = pair(x_first, (zl - az) & 3, (x - ax) & 3) * 2 + request
        state = pair(x_first, (az - zl) & 3, (ax - x) & 3) * 2 + request
        rows = pl.ds(pl.multiple_of(state * HEADS, HEADS), HEADS)
        query = query_ref[pl.ds(pl.multiple_of(asked * HEADS, HEADS), HEADS), :]
        wide = jnp.where(own, jnp.concatenate([query] * GROUPS, axis=1), jnp.zeros((), BF16))
        score = (
            lax.dot_general(
                wide, pool_ref[b, :, :KV], (((1,), (1,)), ((), ())), preferred_element_type=F32
            )
            * scale
        )
        keep = slot < count_ref[b]
        score = jnp.where(keep, score, NEG)
        top = jnp.max(score, axis=1, keepdims=True)
        weight = jnp.where(keep, jnp.exp(score - top), 0.0)
        total = jnp.sum(weight, axis=1, keepdims=True)
        high, low, _ = split(weight)
        mixed = jnp.dot(
            jnp.concatenate([high, low], axis=0), pool_ref[b, :, KV:], preferred_element_type=F32
        )
        mixed = mixed[:HEADS] + mixed[HEADS:]
        mixed = jnp.concatenate(
            [mixed[g * per : (g + 1) * per, g * HEAD : (g + 1) * HEAD] for g in range(GROUPS)],
            axis=0,
        )
        old = top_ref[rows, :]
        best = jnp.maximum(old, top)
        keep_old, add_new = jnp.exp(old - best), jnp.exp(top - best)
        top_ref[rows, :] = best
        sum_ref[rows, :] = keep_old * sum_ref[rows, :] + add_new * total
        acc_ref[rows, :] = keep_old * acc_ref[rows, :] + add_new * mixed
    for r in range(SIDE * SIDE):
        states = []
        for i in range(REQUESTS):
            at = (r * REQUESTS + i) * HEADS
            rows = slice(at, at + HEADS)
            states.append((top_ref[rows, :], sum_ref[rows, :], acc_ref[rows, :]))
        write_states(sends[r // SIDE], r % SIDE, states)


def partial_attention(owner, count, queries, pool):
    smem = pl.BlockSpec(memory_space=pltpu.SMEM)
    return call(
        partial_kernel,
        "partial_attention",
        [shape((SIDE, MESSAGE, HEAD))] * SIDE,
        4,
        in_specs=[smem, smem] + whole(2),
        out_specs=whole(SIDE),
        scratch_shapes=[pltpu.VMEM((SIDE * SIDE * REQUESTS * HEADS, HEAD), F32)] * 3,
    )(owner, count, queries, pool)


def finish_kernel(got0_ref, got1_ref, got2_ref, got3_ref, query_ref, new_ref, out_ref):
    scale = 1.0 / math.sqrt(HEAD)
    per = HEADS // GROUPS

    def by_head(line):
        return jnp.concatenate(
            [
                jnp.broadcast_to(line[:, g * HEAD : (g + 1) * HEAD], (per, HEAD))
                for g in range(GROUPS)
            ],
            axis=0,
        )

    answers = []
    for i in range(REQUESTS):
        query = query_ref[i * HEADS : (i + 1) * HEADS, :].astype(F32)
        key = by_head(new_ref[i : i + 1, :KV].astype(F32))
        value = by_head(new_ref[i : i + 1, KV:].astype(F32))
        own = jnp.sum(query * key, axis=1, keepdims=True) * scale
        states = [(own, jnp.ones((HEADS, 1), F32), value)]
        states += [read_state(ref, 0, i) for ref in (got0_ref, got1_ref, got2_ref, got3_ref)]
        _, total, mixed = merged(states)
        answers.append(mixed / total)
    for h in range(HEADS):
        pair = jnp.concatenate([part[h : h + 1] for part in answers], axis=0)
        out_ref[:, h * HEAD : (h + 1) * HEAD] = pair.astype(BF16)


def along(array, axis):
    return [array] + [moved(array, **{axis: k}) for k in range(1, SIDE)]


def spread(arrays, axis):
    return [moved(array, **{axis: k}) if k else array for k, array in enumerate(arrays)]


def shards(
    moe_input,
    expert_ids,
    route_weight,
    expert_slot,
    w_gate_up,
    w_down,
    queries,
    incoming_key_value,
    key_value_pool,
    block_owner,
    block_tokens,
):
    slot_row = expert_slot.reshape(1, SLOTS)
    packed = call(pack_kernel, "pack", shape((RING, TOK, D + EXTRA)), 3, limit=VMEM_ALL)(
        moe_input, expert_ids.T, route_weight.T
    )
    own_queries = queries.reshape(REQUESTS * HEADS, HEAD)
    near = exchange(packed, RING_GROUPS)
    line = along(own_queries, "first")
    send = call(dispatch_kernel, "dispatch", shape((REACH, ROWS, D)), 2, limit=VMEM_ALL)(
        near, slot_row
    )
    send, line = lax.optimization_barrier((send, line))
    line = jnp.concatenate(line, axis=0)
    received = exchange(send, REACH_GROUPS)

    other_gate_up, other_down = moved(w_gate_up, core=1), moved(w_down, core=1)
    square = along(line, "second")
    rows = expert(
        received, w_gate_up, other_gate_up, w_down, other_down
    )
    rows, square = lax.optimization_barrier((rows, square))
    returned = exchange(rows, REACH_GROUPS)

    partials = partial_attention(
        block_owner, block_tokens, jnp.concatenate(square, axis=0), key_value_pool
    )
    across = spread(partials, "second")
    mix = call(mixing_kernel, "mixing", shape((2 * NEAR, REACH * ROWS)), 2)(near, slot_row)
    parts = call(combine_kernel, "combine", shape((RING, TOK, D)), 2)(mix, on_core(returned))
    parts, across = lax.optimization_barrier((parts, across))
    parts = exchange(parts, RING_GROUPS)

    met = call(
        merge_kernel,
        "merge",
        [shape((1, MESSAGE, HEAD))] * SIDE,
        4,
        out_specs=whole(SIDE),
    )(*across)
    attn_out = call(finish_kernel, "finish", shape((REQUESTS, HEADS * HEAD)), 6)(
        *spread(met, "first"), own_queries, incoming_key_value
    )
    moe_out = call(total_kernel, "total", shape((TOK, D)), 1)(parts)
    return (moe_out, attn_out)


def solution(mesh):
    flat = Mesh(mesh.devices.reshape(-1), (AXIS,))
    rows = P(AXIS, None)
    placed = (
        rows,
        rows,
        rows,
        P(),
        P(None, AXIS),
        rows,
        rows,
        rows,
        P(AXIS, None, None),
        P(AXIS),
        P(AXIS),
    )
    return jax.shard_map(
        shards, mesh=flat, in_specs=placed, out_specs=(rows, rows), check_vma=False
    )
```

```python
import math

import jax
import jax.numpy as jnp
from jax import lax
from jax.experimental import pallas as pl
from jax.experimental.pallas import tpu as pltpu
from jax.sharding import Mesh
from jax.sharding import PartitionSpec as P

D = 2048
TOK = 16
TOP = 8
SLOTS = 128
RING = 8
REACH = 32
ROWS = 16
NEAR = RING * TOK
EXTRA = 256
HALF = 192
HEADS = 64
GROUPS = 4
HEAD = 128
REQUESTS = 2
SIDE = 4
BLOCKS = 16
LEN = 64
KV = GROUPS * HEAD
NEG = -1e30
STAT = 16
MESSAGE = REQUESTS * HEADS + STAT

F32 = jnp.float32
BF16 = jnp.bfloat16
VMEM_LIMIT = 32 * 1024 * 1024
VMEM_MOST = 60 * 1024 * 1024
VMEM_ALL = 62 * 1024 * 1024
AXIS = "d"


def number(x, zl, y, zh, c):
    return (x * 4 + zl) * 32 + y * 4 + zh * 2 + c


def position(device):
    return device >> 7, (device >> 5) & 3, (device >> 2) & 7, (device >> 1) & 1, device & 1


RING_GROUPS = [
    [number(x, z % 4, y, z // 4, 0) for z in range(8)] for x in range(4) for y in range(8)
] + [
    [number(x, z % 4, y, z // 4, 1) for y in range(8)] for x in range(4) for z in range(8)
]
REACH_GROUPS = [
    [number(x, z % 4, y, z // 4, 0) for x in range(4) for y in range(8)] for z in range(8)
] + [
    [number(x, z % 4, y, z // 4, 1) for x in range(4) for z in range(8)] for y in range(8)
]


def exchange(array, groups):
    return lax.all_to_all(
        array, AXIS, split_axis=0, concat_axis=0, axis_index_groups=groups, tiled=True
    )


def moved(array, first=0, second=0, core=0):
    pairs = []
    for device in range(512):
        x, zl, y, zh, c = position(device)
        dx, dz = (first, second) if c else (second, first)
        pairs.append((device, number((x + dx) % 4, (zl + dz) % 4, y, zh, (c + core) % 2)))
    return lax.ppermute(array, AXIS, pairs)


def iota(shape, dim):
    return lax.broadcasted_iota(jnp.int32, shape, dim)


def whole(count):
    return [pl.BlockSpec(memory_space=pltpu.VMEM)] * count


def one(condition):
    return jnp.where(condition, 1.0, 0.0).astype(BF16)


def split(value):
    high = value.astype(BF16)
    rest = value - high.astype(F32)
    middle = rest.astype(BF16)
    return high, middle, (rest - middle.astype(F32)).astype(BF16)


def call(kernel, name, shapes, inputs, **more):
    return pl.pallas_call(
        kernel,
        name=name,
        out_shape=shapes,
        in_specs=more.pop("in_specs", whole(inputs)),
        out_specs=more.pop("out_specs", whole(1)[0]),
        compiler_params=pltpu.CompilerParams(vmem_limit_bytes=more.pop("limit", VMEM_LIMIT)),
        **more,
    )


def shape(dims, kind=BF16):
    return jax.ShapeDtypeStruct(dims, kind)


def pack_kernel(token_ref, ids_ref, weight_ref, out_ref):
    x, zl, y, zh, c = position(lax.axis_index(AXIS))
    mine = jnp.where(c == 0, zh * 4 + zl, y)
    put = one(iota((TOK, NEAR), 1) == iota((TOK, NEAR), 0) + mine * TOK)
    ids = ids_ref[...].astype(F32).astype(BF16)
    parts = [jnp.dot(p, put, preferred_element_type=F32) for p in (ids,) + split(weight_ref[...])]
    left = jnp.concatenate(parts[:2], axis=0).astype(BF16)
    right = jnp.concatenate(parts[2:], axis=0).astype(BF16)
    for u in range(RING):
        out_ref[u, :, :D] = token_ref[...]
        out_ref[u, :, D : D + NEAR] = left
        out_ref[u, :, D + NEAR :] = right


def reached(slot_ref):
    x, zl, y, zh, c = position(lax.axis_index(AXIS))
    d = iota((REACH, SLOTS), 0)
    across, along = d >> 3, d & 7
    at_zl = jnp.where(c == 0, zl, along & 3)
    at_y = jnp.where(c == 0, along, y)
    return one(slot_ref[...] == (across * 4 + at_zl) * 8 + at_y)


def routing(near_ref, slot_ref):
    head = jnp.sum(near_ref[:, :, D:].astype(F32), axis=0)
    ids, weights = head[:TOP, :NEAR], (head[TOP:, :NEAR], head[:TOP, NEAR:], head[TOP:, NEAR:])
    expert = iota((SLOTS, NEAR), 0).astype(F32)
    hits = [ids[k : k + 1] == expert for k in range(TOP)]
    chosen = jnp.zeros((SLOTS, NEAR), F32)
    for hit in hits:
        chosen = chosen + jnp.where(hit, 1.0, 0.0)
    here = reached(slot_ref)
    mine = jnp.dot(here, chosen.astype(BF16), preferred_element_type=F32)
    earlier = one(iota((NEAR, NEAR), 0) < iota((NEAR, NEAR), 1))
    rank = jnp.dot(mine.astype(BF16), earlier, preferred_element_type=F32)
    place = jnp.where(mine > 0.5, rank, -1.0)
    taken = place[:, None, :] == iota((1, ROWS, NEAR), 1).astype(F32)
    return hits, weights, here, taken


CHUNKS = 4


def dispatch_kernel(near_ref, slot_ref, out_ref, made_ref, left_sem):
    _, _, _, taken = routing(near_ref, slot_ref)
    pick = jnp.where(taken, 1.0, 0.0).reshape(REACH * ROWS, NEAR).astype(BF16)
    width = D // CHUNKS
    leave = []
    for s in range(CHUNKS):
        columns = slice(s * width, (s + 1) * width)
        tokens = near_ref[:, :, columns].reshape(NEAR, width)
        rows = jnp.dot(pick, tokens, preferred_element_type=F32)
        made_ref[s] = rows.astype(BF16).reshape(REACH, ROWS, width)
        leave.append(
            pltpu.make_async_copy(made_ref.at[s], out_ref.at[:, :, columns], left_sem.at[s])
        )
        leave[-1].start()
    for copy in leave:
        copy.wait()


def dispatch(near, slot_row):
    return call(
        dispatch_kernel,
        "dispatch",
        shape((REACH, ROWS, D)),
        2,
        out_specs=pl.BlockSpec(memory_space=pltpu.HBM),
        scratch_shapes=[
            pltpu.VMEM((CHUNKS, REACH, ROWS, D // CHUNKS), BF16),
            pltpu.SemaphoreType.DMA((CHUNKS,)),
        ],
        limit=VMEM_ALL,
    )(on_core(near), slot_row)


def mixing_kernel(near_ref, slot_ref, out_ref):
    hits, weights, here, taken = routing(near_ref, slot_ref)
    total = jnp.zeros((REACH, NEAR), F32)
    for part in weights:
        spread = jnp.zeros((SLOTS, NEAR), F32)
        for k in range(TOP):
            spread = spread + jnp.where(hits[k], part[k : k + 1], 0.0)
        total = total + jnp.dot(here, spread.astype(BF16), preferred_element_type=F32)
    mix = jnp.where(taken, total[:, None, :], 0.0).reshape(REACH * ROWS, NEAR).T
    high, low, _ = split(mix)
    out_ref[:NEAR] = high
    out_ref[NEAR:] = low


def combine_kernel(mix_ref, rows_ref, out_ref):
    rows = rows_ref[...].reshape(REACH * ROWS, D)
    both = jnp.dot(mix_ref[...], rows, preferred_element_type=F32)
    out_ref[...] = (both[:NEAR] + both[NEAR:]).astype(BF16).reshape(RING, TOK, D)


def total_kernel(parts_ref, out_ref):
    out_ref[...] = jnp.sum(parts_ref[...].astype(F32), axis=0).astype(BF16)


EXPERT_STEPS = 2


def expert_kernel(rows_ref, *refs):
    sources, out_ref, wide_ref, tall_ref, made_ref, came_sem, left_sem = refs[:4], *refs[4:]
    both, quarter = 2 * HALF, HALF
    places = (
        wide_ref.at[:, :both],
        wide_ref.at[:, both:],
        tall_ref.at[:quarter],
        tall_ref.at[quarter:],
    )
    come = [
        pltpu.make_async_copy(source, place, came_sem.at[i])
        for i, (source, place) in enumerate(zip(sources, places))
    ]
    for copy in come:
        copy.start()
    step = REACH // EXPERT_STEPS
    leave = []
    for s in range(EXPERT_STEPS):
        x = rows_ref[s * step : (s + 1) * step].reshape(step * ROWS, D)
        if s == 0:
            come[0].wait()
            left = jnp.dot(x, wide_ref[:, :both], preferred_element_type=F32)
            come[1].wait()
            right = jnp.dot(x, wide_ref[:, both:], preferred_element_type=F32)
            wide = jnp.concatenate([left, right], axis=1)
        else:
            wide = jnp.dot(x, wide_ref[...], preferred_element_type=F32)
        acts = []
        for at in (0, both):
            gate, up = wide[:, at : at + HALF], wide[:, at + HALF : at + both]
            acts.append((gate / (1.0 + jnp.exp(-gate)) * up).astype(BF16))
        act = jnp.concatenate(acts, axis=1)
        if s == 0:
            come[2].wait()
            come[3].wait()
        total = jnp.dot(act, tall_ref[...], preferred_element_type=F32)
        made_ref[s] = total.astype(BF16).reshape(step, ROWS, D)
        leave.append(
            pltpu.make_async_copy(
                made_ref.at[s], out_ref.at[s * step : (s + 1) * step], left_sem.at[s]
            )
        )
        leave[-1].start()
    for copy in leave:
        copy.wait()


def on_core(array):
    return pltpu.with_memory_space_constraint(array, pltpu.VMEM)


def expert(rows, *weights):
    apart = pl.BlockSpec(memory_space=pltpu.HBM)
    return call(
        expert_kernel,
        "expert",
        shape(rows.shape),
        5,
        in_specs=whole(1) + [apart] * 4,
        out_specs=apart,
        limit=VMEM_MOST,
        scratch_shapes=[
            pltpu.VMEM((D, 4 * HALF), BF16),
            pltpu.VMEM((2 * HALF, D), BF16),
            pltpu.VMEM((EXPERT_STEPS, REACH // EXPERT_STEPS, ROWS, D), BF16),
            pltpu.SemaphoreType.DMA((4,)),
            pltpu.SemaphoreType.DMA((EXPERT_STEPS,)),
        ],
    )(on_core(rows), *weights)


def write_states(ref, r, states):
    lane, row = iota((HEADS, HEAD), 1), iota((HEADS, HEAD), 0)
    line = iota((STAT, HEAD), 0)
    stats = jnp.zeros((STAT, HEAD), F32)
    for i, (top, total, mixed) in enumerate(states):
        ref[r, i * HEADS : (i + 1) * HEADS, :] = mixed.astype(BF16)
        flat = jnp.where(lane == row, top, 0.0) + jnp.where(lane == row + HEADS, total, 0.0)
        flat = jnp.sum(flat, axis=0, keepdims=True)
        for part, value in enumerate(split(flat)):
            stats = jnp.where(line == i * 3 + part, value.astype(F32), stats)
    ref[r, REQUESTS * HEADS :, :] = stats.astype(BF16)


def read_state(ref, r, i):
    lane, row = iota((HEADS, HEAD), 1), iota((HEADS, HEAD), 0)
    stats = ref[r, REQUESTS * HEADS :, :].astype(F32)
    flat = stats[i * 3 : i * 3 + 1] + stats[i * 3 + 1 : i * 3 + 2] + stats[i * 3 + 2 : i * 3 + 3]
    top = jnp.sum(jnp.where(lane == row, flat, 0.0), axis=1, keepdims=True)
    total = jnp.sum(jnp.where(lane == row + HEADS, flat, 0.0), axis=1, keepdims=True)
    return top, total, ref[r, i * HEADS : (i + 1) * HEADS, :].astype(F32)


def merged(states):
    best = states[0][0]
    for top, _, _ in states[1:]:
        best = jnp.maximum(best, top)
    sums, acc = 0.0, 0.0
    for top, total, mixed in states:
        factor = jnp.exp(top - best)
        sums = sums + factor * total
        acc = acc + factor * mixed
    return best, sums, acc


def merge_kernel(got0_ref, got1_ref, got2_ref, got3_ref, *sends):
    refs = (got0_ref, got1_ref, got2_ref, got3_ref)
    for r in range(SIDE):
        write_states(
            sends[r],
            0,
            [merged([read_state(ref, r, i) for ref in refs]) for i in range(REQUESTS)],
        )


def pair(x_first, dz, dx):
    return jnp.where(x_first, dz * 4 + dx, dx * 4 + dz)


def partial_kernel(owner_ref, count_ref, query_ref, pool_ref, *refs):
    sends, (top_ref, sum_ref, acc_ref) = refs[:SIDE], refs[SIDE:]
    scale = 1.0 / math.sqrt(HEAD)
    top_ref[...] = jnp.full(top_ref.shape, NEG, F32)
    sum_ref[...] = jnp.zeros(sum_ref.shape, F32)
    acc_ref[...] = jnp.zeros(acc_ref.shape, F32)
    x, zl, _, _, c = position(lax.axis_index(AXIS))
    x_first = c == 1
    per = HEADS // GROUPS
    own = iota((HEADS, KV), 1) // HEAD == iota((HEADS, KV), 0) // per
    slot = iota((HEADS, LEN), 1)
    for b in range(BLOCKS):
        owner = owner_ref[b]
        ax, az, request = owner >> 3, (owner >> 1) & 3, owner & 1
        asked = pair(x_first, (zl - az) & 3, (x - ax) & 3) * 2 + request
        state = pair(x_first, (az - zl) & 3, (ax - x) & 3) * 2 + request
        rows = pl.ds(pl.multiple_of(state * HEADS, HEADS), HEADS)
        query = query_ref[pl.ds(pl.multiple_of(asked * HEADS, HEADS), HEADS), :]
        wide = jnp.where(own, jnp.concatenate([query] * GROUPS, axis=1), jnp.zeros((), BF16))
        score = (
            lax.dot_general(
                wide, pool_ref[b, :, :KV], (((1,), (1,)), ((), ())), preferred_element_type=F32
            )
            * scale
        )
        keep = slot < count_ref[b]
        score = jnp.where(keep, score, NEG)
        top = jnp.max(score, axis=1, keepdims=True)
        weight = jnp.where(keep, jnp.exp(score - top), 0.0)
        total = jnp.sum(weight, axis=1, keepdims=True)
        high, low, _ = split(weight)
        mixed = jnp.dot(
            jnp.concatenate([high, low], axis=0), pool_ref[b, :, KV:], preferred_element_type=F32
        )
        mixed = mixed[:HEADS] + mixed[HEADS:]
        mixed = jnp.concatenate(
            [mixed[g * per : (g + 1) * per, g * HEAD : (g + 1) * HEAD] for g in range(GROUPS)],
            axis=0,
        )
        old = top_ref[rows, :]
        best = jnp.maximum(old, top)
        keep_old, add_new = jnp.exp(old - best), jnp.exp(top - best)
        top_ref[rows, :] = best
        sum_ref[rows, :] = keep_old * sum_ref[rows, :] + add_new * total
        acc_ref[rows, :] = keep_old * acc_ref[rows, :] + add_new * mixed
    for r in range(SIDE * SIDE):
        states = []
        for i in range(REQUESTS):
            at = (r * REQUESTS + i) * HEADS
            rows = slice(at, at + HEADS)
            states.append((top_ref[rows, :], sum_ref[rows, :], acc_ref[rows, :]))
        write_states(sends[r // SIDE], r % SIDE, states)


def partial_attention(owner, count, queries, pool):
    smem = pl.BlockSpec(memory_space=pltpu.SMEM)
    return call(
        partial_kernel,
        "partial_attention",
        [shape((SIDE, MESSAGE, HEAD))] * SIDE,
        4,
        in_specs=[smem, smem] + whole(2),
        out_specs=whole(SIDE),
        scratch_shapes=[pltpu.VMEM((SIDE * SIDE * REQUESTS * HEADS, HEAD), F32)] * 3,
    )(owner, count, queries, pool)


def finish_kernel(got0_ref, got1_ref, got2_ref, got3_ref, query_ref, new_ref, out_ref):
    scale = 1.0 / math.sqrt(HEAD)
    per = HEADS // GROUPS

    def by_head(line):
        return jnp.concatenate(
            [
                jnp.broadcast_to(line[:, g * HEAD : (g + 1) * HEAD], (per, HEAD))
                for g in range(GROUPS)
            ],
            axis=0,
        )

    answers = []
    for i in range(REQUESTS):
        query = query_ref[i * HEADS : (i + 1) * HEADS, :].astype(F32)
        key = by_head(new_ref[i : i + 1, :KV].astype(F32))
        value = by_head(new_ref[i : i + 1, KV:].astype(F32))
        own = jnp.sum(query * key, axis=1, keepdims=True) * scale
        states = [(own, jnp.ones((HEADS, 1), F32), value)]
        states += [read_state(ref, 0, i) for ref in (got0_ref, got1_ref, got2_ref, got3_ref)]
        _, total, mixed = merged(states)
        answers.append(mixed / total)
    for h in range(HEADS):
        pair = jnp.concatenate([part[h : h + 1] for part in answers], axis=0)
        out_ref[:, h * HEAD : (h + 1) * HEAD] = pair.astype(BF16)


def along(array, axis):
    return [array] + [moved(array, **{axis: k}) for k in range(1, SIDE)]


def spread(arrays, axis):
    return [moved(array, **{axis: k}) if k else array for k, array in enumerate(arrays)]


def shards(
    moe_input,
    expert_ids,
    route_weight,
    expert_slot,
    w_gate_up,
    w_down,
    queries,
    incoming_key_value,
    key_value_pool,
    block_owner,
    block_tokens,
):
    slot_row = expert_slot.reshape(1, SLOTS)
    packed = call(pack_kernel, "pack", shape((RING, TOK, D + EXTRA)), 3, limit=VMEM_ALL)(
        moe_input, expert_ids.T, route_weight.T
    )
    own_queries = queries.reshape(REQUESTS * HEADS, HEAD)
    near = exchange(packed, RING_GROUPS)
    line = along(own_queries, "first")
    send = dispatch(near, slot_row)
    send, line = lax.optimization_barrier((send, line))
    line = jnp.concatenate(line, axis=0)
    received = exchange(send, REACH_GROUPS)

    other_gate_up, other_down = moved(w_gate_up, core=1), moved(w_down, core=1)
    square = along(line, "second")
    rows = expert(
        received, w_gate_up, other_gate_up, w_down, other_down
    )
    rows, square = lax.optimization_barrier((rows, square))
    returned = exchange(rows, REACH_GROUPS)

    partials = partial_attention(
        block_owner, block_tokens, jnp.concatenate(square, axis=0), key_value_pool
    )
    across = spread(partials, "second")
    mix = call(mixing_kernel, "mixing", shape((2 * NEAR, REACH * ROWS)), 2)(near, slot_row)
    parts = call(combine_kernel, "combine", shape((RING, TOK, D)), 2)(mix, on_core(returned))
    parts, across = lax.optimization_barrier((parts, across))
    parts = exchange(parts, RING_GROUPS)

    met = call(
        merge_kernel,
        "merge",
        [shape((1, MESSAGE, HEAD))] * SIDE,
        4,
        out_specs=whole(SIDE),
    )(*across)
    attn_out = call(finish_kernel, "finish", shape((REQUESTS, HEADS * HEAD)), 6)(
        *spread(met, "first"), own_queries, incoming_key_value
    )
    moe_out = call(total_kernel, "total", shape((TOK, D)), 1)(parts)
    return (moe_out, attn_out)


def solution(mesh):
    flat = Mesh(mesh.devices.reshape(-1), (AXIS,))
    rows = P(AXIS, None)
    placed = (
        rows,
        rows,
        rows,
        P(),
        P(None, AXIS),
        rows,
        rows,
        rows,
        P(AXIS, None, None),
        P(AXIS),
        P(AXIS),
    )
    return jax.shard_map(
        shards, mesh=flat, in_specs=placed, out_specs=(rows, rows), check_vma=False
    )
```

```python
import math

import jax
import jax.numpy as jnp
from jax import lax
from jax.experimental import pallas as pl
from jax.experimental.pallas import tpu as pltpu
from jax.sharding import Mesh
from jax.sharding import PartitionSpec as P

D = 2048
TOK = 16
TOP = 8
SLOTS = 128
RING = 8
REACH = 32
ROWS = 16
NEAR = RING * TOK
EXTRA = 256
HALF = 192
HEADS = 64
GROUPS = 4
HEAD = 128
REQUESTS = 2
SIDE = 4
BLOCKS = 16
LEN = 64
KV = GROUPS * HEAD
NEG = -1e30
STAT = 16
MESSAGE = REQUESTS * HEADS + STAT

F32 = jnp.float32
BF16 = jnp.bfloat16
VMEM_LIMIT = 32 * 1024 * 1024
VMEM_MOST = 60 * 1024 * 1024
VMEM_ALL = 62 * 1024 * 1024
AXIS = "d"


def number(x, zl, y, zh, c):
    return (x * 4 + zl) * 32 + y * 4 + zh * 2 + c


def position(device):
    return device >> 7, (device >> 5) & 3, (device >> 2) & 7, (device >> 1) & 1, device & 1


RING_GROUPS = [
    [number(x, z % 4, y, z // 4, 0) for z in range(8)] for x in range(4) for y in range(8)
] + [
    [number(x, z % 4, y, z // 4, 1) for y in range(8)] for x in range(4) for z in range(8)
]
REACH_GROUPS = [
    [number(x, z % 4, y, z // 4, 0) for x in range(4) for y in range(8)] for z in range(8)
] + [
    [number(x, z % 4, y, z // 4, 1) for x in range(4) for z in range(8)] for y in range(8)
]


def exchange(array, groups):
    return lax.all_to_all(
        array, AXIS, split_axis=0, concat_axis=0, axis_index_groups=groups, tiled=True
    )


def moved(array, first=0, second=0, core=0):
    pairs = []
    for device in range(512):
        x, zl, y, zh, c = position(device)
        dx, dz = (first, second) if c else (second, first)
        pairs.append((device, number((x + dx) % 4, (zl + dz) % 4, y, zh, (c + core) % 2)))
    return lax.ppermute(array, AXIS, pairs)


def swapped(array, flip):
    pairs = []
    for device in range(512):
        x, zl, y, zh, c = position(device)
        pairs.append((device, number(x ^ (flip * c), zl ^ (flip * (1 - c)), y, zh, c)))
    return lax.ppermute(array, AXIS, pairs)


def iota(shape, dim):
    return lax.broadcasted_iota(jnp.int32, shape, dim)


def whole(count):
    return [pl.BlockSpec(memory_space=pltpu.VMEM)] * count


def one(condition):
    return jnp.where(condition, 1.0, 0.0).astype(BF16)


def split(value):
    high = value.astype(BF16)
    rest = value - high.astype(F32)
    middle = rest.astype(BF16)
    return high, middle, (rest - middle.astype(F32)).astype(BF16)


def call(kernel, name, shapes, inputs, **more):
    return pl.pallas_call(
        kernel,
        name=name,
        out_shape=shapes,
        in_specs=more.pop("in_specs", whole(inputs)),
        out_specs=more.pop("out_specs", whole(1)[0]),
        compiler_params=pltpu.CompilerParams(vmem_limit_bytes=more.pop("limit", VMEM_LIMIT)),
        **more,
    )


def shape(dims, kind=BF16):
    return jax.ShapeDtypeStruct(dims, kind)


def pack_kernel(token_ref, ids_ref, weight_ref, out_ref):
    x, zl, y, zh, c = position(lax.axis_index(AXIS))
    mine = jnp.where(c == 0, zh * 4 + zl, y)
    put = one(iota((TOK, NEAR), 1) == iota((TOK, NEAR), 0) + mine * TOK)
    ids = ids_ref[...].astype(F32).astype(BF16)
    parts = [jnp.dot(p, put, preferred_element_type=F32) for p in (ids,) + split(weight_ref[...])]
    left = jnp.concatenate(parts[:2], axis=0).astype(BF16)
    right = jnp.concatenate(parts[2:], axis=0).astype(BF16)
    for u in range(RING):
        out_ref[u, :, :D] = token_ref[...]
        out_ref[u, :, D : D + NEAR] = left
        out_ref[u, :, D + NEAR :] = right


def reached(slot_ref):
    x, zl, y, zh, c = position(lax.axis_index(AXIS))
    d = iota((REACH, SLOTS), 0)
    across, along = d >> 3, d & 7
    at_zl = jnp.where(c == 0, zl, along & 3)
    at_y = jnp.where(c == 0, along, y)
    return one(slot_ref[...] == (across * 4 + at_zl) * 8 + at_y)


def routing(near_ref, slot_ref):
    head = jnp.sum(near_ref[:, :, D:].astype(F32), axis=0)
    ids, weights = head[:TOP, :NEAR], (head[TOP:, :NEAR], head[:TOP, NEAR:], head[TOP:, NEAR:])
    expert = iota((SLOTS, NEAR), 0).astype(F32)
    hits = [ids[k : k + 1] == expert for k in range(TOP)]
    chosen = jnp.zeros((SLOTS, NEAR), F32)
    for hit in hits:
        chosen = chosen + jnp.where(hit, 1.0, 0.0)
    here = reached(slot_ref)
    mine = jnp.dot(here, chosen.astype(BF16), preferred_element_type=F32)
    earlier = one(iota((NEAR, NEAR), 0) < iota((NEAR, NEAR), 1))
    rank = jnp.dot(mine.astype(BF16), earlier, preferred_element_type=F32)
    place = jnp.where(mine > 0.5, rank, -1.0)
    taken = place[:, None, :] == iota((1, ROWS, NEAR), 1).astype(F32)
    return hits, weights, here, taken


CHUNKS = 4


def dispatch_kernel(near_ref, slot_ref, out_ref, made_ref, left_sem):
    _, _, _, taken = routing(near_ref, slot_ref)
    pick = jnp.where(taken, 1.0, 0.0).reshape(REACH * ROWS, NEAR).astype(BF16)
    width = D // CHUNKS
    leave = []
    for s in range(CHUNKS):
        columns = slice(s * width, (s + 1) * width)
        tokens = near_ref[:, :, columns].reshape(NEAR, width)
        rows = jnp.dot(pick, tokens, preferred_element_type=F32)
        made_ref[s] = rows.astype(BF16).reshape(REACH, ROWS, width)
        leave.append(
            pltpu.make_async_copy(made_ref.at[s], out_ref.at[:, :, columns], left_sem.at[s])
        )
        leave[-1].start()
    for copy in leave:
        copy.wait()


def dispatch(near, slot_row):
    return call(
        dispatch_kernel,
        "dispatch",
        shape((REACH, ROWS, D)),
        2,
        out_specs=pl.BlockSpec(memory_space=pltpu.HBM),
        scratch_shapes=[
            pltpu.VMEM((CHUNKS, REACH, ROWS, D // CHUNKS), BF16),
            pltpu.SemaphoreType.DMA((CHUNKS,)),
        ],
        limit=VMEM_ALL,
    )(on_core(near), slot_row)


def mixing_kernel(near_ref, slot_ref, out_ref):
    hits, weights, here, taken = routing(near_ref, slot_ref)
    total = jnp.zeros((REACH, NEAR), F32)
    for part in weights:
        spread = jnp.zeros((SLOTS, NEAR), F32)
        for k in range(TOP):
            spread = spread + jnp.where(hits[k], part[k : k + 1], 0.0)
        total = total + jnp.dot(here, spread.astype(BF16), preferred_element_type=F32)
    mix = jnp.where(taken, total[:, None, :], 0.0).reshape(REACH * ROWS, NEAR).T
    high, low, _ = split(mix)
    out_ref[:NEAR] = high
    out_ref[NEAR:] = low


def combine_kernel(mix_ref, rows_ref, out_ref):
    rows = rows_ref[...].reshape(REACH * ROWS, D)
    both = jnp.dot(mix_ref[...], rows, preferred_element_type=F32)
    out_ref[...] = (both[:NEAR] + both[NEAR:]).astype(BF16).reshape(RING, TOK, D)


def total_kernel(parts_ref, out_ref):
    out_ref[...] = jnp.sum(parts_ref[...].astype(F32), axis=0).astype(BF16)


EXPERT_STEPS = 2


def expert_kernel(rows_ref, *refs):
    sources, out_ref, wide_ref, tall_ref, made_ref, came_sem, left_sem = refs[:4], *refs[4:]
    both, quarter = 2 * HALF, HALF
    places = (
        wide_ref.at[:, :both],
        wide_ref.at[:, both:],
        tall_ref.at[:quarter],
        tall_ref.at[quarter:],
    )
    come = [
        pltpu.make_async_copy(source, place, came_sem.at[i])
        for i, (source, place) in enumerate(zip(sources, places))
    ]
    for copy in come:
        copy.start()
    step = REACH // EXPERT_STEPS
    leave = []
    for s in range(EXPERT_STEPS):
        x = rows_ref[s * step : (s + 1) * step].reshape(step * ROWS, D)
        if s == 0:
            come[0].wait()
            left = jnp.dot(x, wide_ref[:, :both], preferred_element_type=F32)
            come[1].wait()
            right = jnp.dot(x, wide_ref[:, both:], preferred_element_type=F32)
            wide = jnp.concatenate([left, right], axis=1)
        else:
            wide = jnp.dot(x, wide_ref[...], preferred_element_type=F32)
        acts = []
        for at in (0, both):
            gate, up = wide[:, at : at + HALF], wide[:, at + HALF : at + both]
            acts.append((gate / (1.0 + jnp.exp(-gate)) * up).astype(BF16))
        act = jnp.concatenate(acts, axis=1)
        if s == 0:
            come[2].wait()
            come[3].wait()
        total = jnp.dot(act, tall_ref[...], preferred_element_type=F32)
        made_ref[s] = total.astype(BF16).reshape(step, ROWS, D)
        leave.append(
            pltpu.make_async_copy(
                made_ref.at[s], out_ref.at[s * step : (s + 1) * step], left_sem.at[s]
            )
        )
        leave[-1].start()
    for copy in leave:
        copy.wait()


def on_core(array):
    return pltpu.with_memory_space_constraint(array, pltpu.VMEM)


def expert(rows, *weights):
    apart = pl.BlockSpec(memory_space=pltpu.HBM)
    return call(
        expert_kernel,
        "expert",
        shape(rows.shape),
        5,
        in_specs=whole(1) + [apart] * 4,
        out_specs=apart,
        limit=VMEM_MOST,
        scratch_shapes=[
            pltpu.VMEM((D, 4 * HALF), BF16),
            pltpu.VMEM((2 * HALF, D), BF16),
            pltpu.VMEM((EXPERT_STEPS, REACH // EXPERT_STEPS, ROWS, D), BF16),
            pltpu.SemaphoreType.DMA((4,)),
            pltpu.SemaphoreType.DMA((EXPERT_STEPS,)),
        ],
    )(on_core(rows), *weights)


def write_states(ref, r, states):
    lane, row = iota((HEADS, HEAD), 1), iota((HEADS, HEAD), 0)
    line = iota((STAT, HEAD), 0)
    stats = jnp.zeros((STAT, HEAD), F32)
    for i, (top, total, mixed) in enumerate(states):
        ref[r, i * HEADS : (i + 1) * HEADS, :] = mixed.astype(BF16)
        flat = jnp.where(lane == row, top, 0.0) + jnp.where(lane == row + HEADS, total, 0.0)
        flat = jnp.sum(flat, axis=0, keepdims=True)
        for part, value in enumerate(split(flat)):
            stats = jnp.where(line == i * 3 + part, value.astype(F32), stats)
    ref[r, REQUESTS * HEADS :, :] = stats.astype(BF16)


def read_state(ref, r, i):
    lane, row = iota((HEADS, HEAD), 1), iota((HEADS, HEAD), 0)
    stats = ref[r, REQUESTS * HEADS :, :].astype(F32)
    flat = stats[i * 3 : i * 3 + 1] + stats[i * 3 + 1 : i * 3 + 2] + stats[i * 3 + 2 : i * 3 + 3]
    top = jnp.sum(jnp.where(lane == row, flat, 0.0), axis=1, keepdims=True)
    total = jnp.sum(jnp.where(lane == row + HEADS, flat, 0.0), axis=1, keepdims=True)
    return top, total, ref[r, i * HEADS : (i + 1) * HEADS, :].astype(F32)


def merged(states):
    best = states[0][0]
    for top, _, _ in states[1:]:
        best = jnp.maximum(best, top)
    sums, acc = 0.0, 0.0
    for top, total, mixed in states:
        factor = jnp.exp(top - best)
        sums = sums + factor * total
        acc = acc + factor * mixed
    return best, sums, acc


def merge_kernel(got0_ref, got1_ref, got2_ref, got3_ref, *sends):
    refs = (got0_ref, got1_ref, got2_ref, got3_ref)
    for r in range(SIDE):
        write_states(
            sends[r],
            0,
            [merged([read_state(ref, r, i) for ref in refs]) for i in range(REQUESTS)],
        )


def pair(x_first, dz, dx):
    return jnp.where(x_first, dz * 4 + dx, dx * 4 + dz)


def partial_kernel(owner_ref, count_ref, query_ref, pool_ref, *refs):
    sends, (top_ref, sum_ref, acc_ref) = refs[:SIDE], refs[SIDE:]
    scale = 1.0 / math.sqrt(HEAD)
    top_ref[...] = jnp.full(top_ref.shape, NEG, F32)
    sum_ref[...] = jnp.zeros(sum_ref.shape, F32)
    acc_ref[...] = jnp.zeros(acc_ref.shape, F32)
    x, zl, _, _, c = position(lax.axis_index(AXIS))
    x_first = c == 1
    per = HEADS // GROUPS
    own = iota((HEADS, KV), 1) // HEAD == iota((HEADS, KV), 0) // per
    slot = iota((HEADS, LEN), 1)
    for b in range(BLOCKS):
        owner = owner_ref[b]
        ax, az, request = owner >> 3, (owner >> 1) & 3, owner & 1
        first = jnp.where(x_first, ax ^ x, az ^ zl)
        second = jnp.where(x_first, (zl - az) & 3, (x - ax) & 3)
        asked = (second * 4 + (first & 1) * 2 + (first >> 1)) * 2 + request
        state = pair(x_first, (az - zl) & 3, (ax - x) & 3) * 2 + request
        rows = pl.ds(pl.multiple_of(state * HEADS, HEADS), HEADS)
        query = query_ref[pl.ds(pl.multiple_of(asked * HEADS, HEADS), HEADS), :]
        wide = jnp.where(own, jnp.concatenate([query] * GROUPS, axis=1), jnp.zeros((), BF16))
        score = (
            lax.dot_general(
                wide, pool_ref[b, :, :KV], (((1,), (1,)), ((), ())), preferred_element_type=F32
            )
            * scale
        )
        keep = slot < count_ref[b]
        score = jnp.where(keep, score, NEG)
        top = jnp.max(score, axis=1, keepdims=True)
        weight = jnp.where(keep, jnp.exp(score - top), 0.0)
        total = jnp.sum(weight, axis=1, keepdims=True)
        high, low, _ = split(weight)
        mixed = jnp.dot(
            jnp.concatenate([high, low], axis=0), pool_ref[b, :, KV:], preferred_element_type=F32
        )
        mixed = mixed[:HEADS] + mixed[HEADS:]
        mixed = jnp.concatenate(
            [mixed[g * per : (g + 1) * per, g * HEAD : (g + 1) * HEAD] for g in range(GROUPS)],
            axis=0,
        )
        old = top_ref[rows, :]
        best = jnp.maximum(old, top)
        keep_old, add_new = jnp.exp(old - best), jnp.exp(top - best)
        top_ref[rows, :] = best
        sum_ref[rows, :] = keep_old * sum_ref[rows, :] + add_new * total
        acc_ref[rows, :] = keep_old * acc_ref[rows, :] + add_new * mixed
    for r in range(SIDE * SIDE):
        states = []
        for i in range(REQUESTS):
            at = (r * REQUESTS + i) * HEADS
            rows = slice(at, at + HEADS)
            states.append((top_ref[rows, :], sum_ref[rows, :], acc_ref[rows, :]))
        write_states(sends[r // SIDE], r % SIDE, states)


def partial_attention(owner, count, queries, pool):
    smem = pl.BlockSpec(memory_space=pltpu.SMEM)
    return call(
        partial_kernel,
        "partial_attention",
        [shape((SIDE, MESSAGE, HEAD))] * SIDE,
        4,
        in_specs=[smem, smem] + whole(2),
        out_specs=whole(SIDE),
        scratch_shapes=[pltpu.VMEM((SIDE * SIDE * REQUESTS * HEADS, HEAD), F32)] * 3,
    )(owner, count, queries, pool)


def finish_kernel(got0_ref, got1_ref, got2_ref, got3_ref, query_ref, new_ref, out_ref):
    scale = 1.0 / math.sqrt(HEAD)
    per = HEADS // GROUPS

    def by_head(line):
        return jnp.concatenate(
            [
                jnp.broadcast_to(line[:, g * HEAD : (g + 1) * HEAD], (per, HEAD))
                for g in range(GROUPS)
            ],
            axis=0,
        )

    answers = []
    for i in range(REQUESTS):
        query = query_ref[i * HEADS : (i + 1) * HEADS, :].astype(F32)
        key = by_head(new_ref[i : i + 1, :KV].astype(F32))
        value = by_head(new_ref[i : i + 1, KV:].astype(F32))
        own = jnp.sum(query * key, axis=1, keepdims=True) * scale
        states = [(own, jnp.ones((HEADS, 1), F32), value)]
        states += [read_state(ref, 0, i) for ref in (got0_ref, got1_ref, got2_ref, got3_ref)]
        _, total, mixed = merged(states)
        answers.append(mixed / total)
    for h in range(HEADS):
        pair = jnp.concatenate([part[h : h + 1] for part in answers], axis=0)
        out_ref[:, h * HEAD : (h + 1) * HEAD] = pair.astype(BF16)


def along(array, axis):
    return [array] + [moved(array, **{axis: k}) for k in range(1, SIDE)]


def spread(arrays, axis):
    return [moved(array, **{axis: k}) if k else array for k, array in enumerate(arrays)]


def shards(
    moe_input,
    expert_ids,
    route_weight,
    expert_slot,
    w_gate_up,
    w_down,
    queries,
    incoming_key_value,
    key_value_pool,
    block_owner,
    block_tokens,
):
    slot_row = expert_slot.reshape(1, SLOTS)
    packed = call(pack_kernel, "pack", shape((RING, TOK, D + EXTRA)), 3, limit=VMEM_ALL)(
        moe_input, expert_ids.T, route_weight.T
    )
    own_queries = queries.reshape(REQUESTS * HEADS, HEAD)
    near = exchange(packed, RING_GROUPS)
    half = jnp.concatenate([own_queries, swapped(own_queries, 2)], axis=0)
    rest = swapped(half, 1)
    send = dispatch(near, slot_row)
    send, rest = lax.optimization_barrier((send, rest))
    line = jnp.concatenate([half, rest], axis=0)
    received = exchange(send, REACH_GROUPS)

    other_gate_up, other_down = moved(w_gate_up, core=1), moved(w_down, core=1)
    square = along(line, "second")
    rows = expert(
        received, w_gate_up, other_gate_up, w_down, other_down
    )
    rows, square = lax.optimization_barrier((rows, square))
    returned = exchange(rows, REACH_GROUPS)

    partials = partial_attention(
        block_owner, block_tokens, jnp.concatenate(square, axis=0), key_value_pool
    )
    across = spread(partials, "second")
    mix = call(mixing_kernel, "mixing", shape((2 * NEAR, REACH * ROWS)), 2)(near, slot_row)
    parts = call(combine_kernel, "combine", shape((RING, TOK, D)), 2)(mix, on_core(returned))
    parts, across = lax.optimization_barrier((parts, across))
    parts = exchange(parts, RING_GROUPS)

    met = call(
        merge_kernel,
        "merge",
        [shape((1, MESSAGE, HEAD))] * SIDE,
        4,
        out_specs=whole(SIDE),
    )(*across)
    attn_out = call(finish_kernel, "finish", shape((REQUESTS, HEADS * HEAD)), 6)(
        *spread(met, "first"), own_queries, incoming_key_value
    )
    moe_out = call(total_kernel, "total", shape((TOK, D)), 1)(parts)
    return (moe_out, attn_out)


def solution(mesh):
    flat = Mesh(mesh.devices.reshape(-1), (AXIS,))
    rows = P(AXIS, None)
    placed = (
        rows,
        rows,
        rows,
        P(),
        P(None, AXIS),
        rows,
        rows,
        rows,
        P(AXIS, None, None),
        P(AXIS),
        P(AXIS),
    )
    return jax.shard_map(
        shards, mesh=flat, in_specs=placed, out_specs=(rows, rows), check_vma=False
    )
```

```python
import math

import jax
import jax.numpy as jnp
from jax import lax
from jax.experimental import pallas as pl
from jax.experimental.pallas import tpu as pltpu
from jax.sharding import Mesh
from jax.sharding import PartitionSpec as P

D = 2048
TOK = 16
TOP = 8
SLOTS = 128
RING = 8
REACH = 32
ROWS = 16
NEAR = RING * TOK
EXTRA = 256
HALF = 192
HEADS = 64
GROUPS = 4
HEAD = 128
REQUESTS = 2
SIDE = 4
BLOCKS = 16
LEN = 64
KV = GROUPS * HEAD
NEG = -1e30
STAT = 16
MESSAGE = REQUESTS * HEADS + STAT

F32 = jnp.float32
BF16 = jnp.bfloat16
VMEM_LIMIT = 32 * 1024 * 1024
VMEM_MOST = 60 * 1024 * 1024
VMEM_ALL = 62 * 1024 * 1024
AXIS = "d"


def number(x, zl, y, zh, c):
    return (x * 4 + zl) * 32 + y * 4 + zh * 2 + c


def position(device):
    return device >> 7, (device >> 5) & 3, (device >> 2) & 7, (device >> 1) & 1, device & 1


RING_GROUPS = [
    [number(x, z % 4, y, z // 4, 0) for z in range(8)] for x in range(4) for y in range(8)
] + [
    [number(x, z % 4, y, z // 4, 1) for y in range(8)] for x in range(4) for z in range(8)
]
REACH_GROUPS = [
    [number(x, z % 4, y, z // 4, 0) for x in range(4) for y in range(8)] for z in range(8)
] + [
    [number(x, z % 4, y, z // 4, 1) for x in range(4) for z in range(8)] for y in range(8)
]


def exchange(array, groups):
    return lax.all_to_all(
        array, AXIS, split_axis=0, concat_axis=0, axis_index_groups=groups, tiled=True
    )


def moved(array, first=0, second=0, core=0):
    pairs = []
    for device in range(512):
        x, zl, y, zh, c = position(device)
        dx, dz = (first, second) if c else (second, first)
        pairs.append((device, number((x + dx) % 4, (zl + dz) % 4, y, zh, (c + core) % 2)))
    return lax.ppermute(array, AXIS, pairs)


def swapped(array, flip):
    pairs = []
    for device in range(512):
        x, zl, y, zh, c = position(device)
        pairs.append((device, number(x ^ (flip * c), zl ^ (flip * (1 - c)), y, zh, c)))
    return lax.ppermute(array, AXIS, pairs)


def iota(shape, dim):
    return lax.broadcasted_iota(jnp.int32, shape, dim)


def whole(count):
    return [pl.BlockSpec(memory_space=pltpu.VMEM)] * count


def one(condition):
    return jnp.where(condition, 1.0, 0.0).astype(BF16)


def split(value):
    high = value.astype(BF16)
    rest = value - high.astype(F32)
    middle = rest.astype(BF16)
    return high, middle, (rest - middle.astype(F32)).astype(BF16)


def call(kernel, name, shapes, inputs, **more):
    return pl.pallas_call(
        kernel,
        name=name,
        out_shape=shapes,
        in_specs=more.pop("in_specs", whole(inputs)),
        out_specs=more.pop("out_specs", whole(1)[0]),
        compiler_params=pltpu.CompilerParams(vmem_limit_bytes=more.pop("limit", VMEM_LIMIT)),
        **more,
    )


def shape(dims, kind=BF16):
    return jax.ShapeDtypeStruct(dims, kind)


def pack_kernel(token_ref, ids_ref, weight_ref, out_ref):
    x, zl, y, zh, c = position(lax.axis_index(AXIS))
    mine = jnp.where(c == 0, zh * 4 + zl, y)
    put = one(iota((TOK, NEAR), 1) == iota((TOK, NEAR), 0) + mine * TOK)
    ids = ids_ref[...].astype(F32).astype(BF16)
    parts = [jnp.dot(p, put, preferred_element_type=F32) for p in (ids,) + split(weight_ref[...])]
    left = jnp.concatenate(parts[:2], axis=0).astype(BF16)
    right = jnp.concatenate(parts[2:], axis=0).astype(BF16)
    for u in range(RING):
        out_ref[u, :, :D] = token_ref[...]
        out_ref[u, :, D : D + NEAR] = left
        out_ref[u, :, D + NEAR :] = right


def reached(slot_ref):
    x, zl, y, zh, c = position(lax.axis_index(AXIS))
    d = iota((REACH, SLOTS), 0)
    across, along = d >> 3, d & 7
    at_zl = jnp.where(c == 0, zl, along & 3)
    at_y = jnp.where(c == 0, along, y)
    return one(slot_ref[...] == (across * 4 + at_zl) * 8 + at_y)


def routing(near_ref, slot_ref):
    head = jnp.sum(near_ref[:, :, D:].astype(F32), axis=0)
    ids, weights = head[:TOP, :NEAR], (head[TOP:, :NEAR], head[:TOP, NEAR:], head[TOP:, NEAR:])
    expert = iota((SLOTS, NEAR), 0).astype(F32)
    hits = [ids[k : k + 1] == expert for k in range(TOP)]
    chosen = jnp.zeros((SLOTS, NEAR), F32)
    for hit in hits:
        chosen = chosen + jnp.where(hit, 1.0, 0.0)
    here = reached(slot_ref)
    mine = jnp.dot(here, chosen.astype(BF16), preferred_element_type=F32)
    earlier = one(iota((NEAR, NEAR), 0) < iota((NEAR, NEAR), 1))
    rank = jnp.dot(mine.astype(BF16), earlier, preferred_element_type=F32)
    place = jnp.where(mine > 0.5, rank, -1.0)
    taken = place[:, None, :] == iota((1, ROWS, NEAR), 1).astype(F32)
    return hits, weights, here, taken


CHUNKS = 4


def dispatch_kernel(near_ref, slot_ref, out_ref, made_ref, left_sem):
    _, _, _, taken = routing(near_ref, slot_ref)
    pick = jnp.where(taken, 1.0, 0.0).reshape(REACH * ROWS, NEAR).astype(BF16)
    width = D // CHUNKS
    leave = []
    for s in range(CHUNKS):
        columns = slice(s * width, (s + 1) * width)
        tokens = near_ref[:, :, columns].reshape(NEAR, width)
        rows = jnp.dot(pick, tokens, preferred_element_type=F32)
        made_ref[s] = rows.astype(BF16).reshape(REACH, ROWS, width)
        leave.append(
            pltpu.make_async_copy(made_ref.at[s], out_ref.at[:, :, columns], left_sem.at[s])
        )
        leave[-1].start()
    for copy in leave:
        copy.wait()


def dispatch(near, slot_row):
    return call(
        dispatch_kernel,
        "dispatch",
        shape((REACH, ROWS, D)),
        2,
        out_specs=pl.BlockSpec(memory_space=pltpu.HBM),
        scratch_shapes=[
            pltpu.VMEM((CHUNKS, REACH, ROWS, D // CHUNKS), BF16),
            pltpu.SemaphoreType.DMA((CHUNKS,)),
        ],
        limit=VMEM_ALL,
    )(near, slot_row)


def mixing_kernel(near_ref, slot_ref, out_ref):
    hits, weights, here, taken = routing(near_ref, slot_ref)
    total = jnp.zeros((REACH, NEAR), F32)
    for part in weights:
        spread = jnp.zeros((SLOTS, NEAR), F32)
        for k in range(TOP):
            spread = spread + jnp.where(hits[k], part[k : k + 1], 0.0)
        total = total + jnp.dot(here, spread.astype(BF16), preferred_element_type=F32)
    mix = jnp.where(taken, total[:, None, :], 0.0).reshape(REACH * ROWS, NEAR).T
    high, low, _ = split(mix)
    out_ref[:NEAR] = high
    out_ref[NEAR:] = low


def combine_kernel(mix_ref, rows_ref, out_ref):
    rows = rows_ref[...].reshape(REACH * ROWS, D)
    both = jnp.dot(mix_ref[...], rows, preferred_element_type=F32)
    out_ref[...] = (both[:NEAR] + both[NEAR:]).astype(BF16).reshape(RING, TOK, D)


def total_kernel(parts_ref, out_ref):
    out_ref[...] = jnp.sum(parts_ref[...].astype(F32), axis=0).astype(BF16)


EXPERT_STEPS = 2


def expert_kernel(rows_ref, *refs):
    sources, out_ref, wide_ref, tall_ref, made_ref, came_sem, left_sem = refs[:4], *refs[4:]
    both, quarter = 2 * HALF, HALF
    places = (
        wide_ref.at[:, :both],
        wide_ref.at[:, both:],
        tall_ref.at[:quarter],
        tall_ref.at[quarter:],
    )
    come = [
        pltpu.make_async_copy(source, place, came_sem.at[i])
        for i, (source, place) in enumerate(zip(sources, places))
    ]
    for copy in come:
        copy.start()
    step = REACH // EXPERT_STEPS
    leave = []
    for s in range(EXPERT_STEPS):
        x = rows_ref[s * step : (s + 1) * step].reshape(step * ROWS, D)
        if s == 0:
            come[0].wait()
            left = jnp.dot(x, wide_ref[:, :both], preferred_element_type=F32)
            come[1].wait()
            right = jnp.dot(x, wide_ref[:, both:], preferred_element_type=F32)
            wide = jnp.concatenate([left, right], axis=1)
        else:
            wide = jnp.dot(x, wide_ref[...], preferred_element_type=F32)
        acts = []
        for at in (0, both):
            gate, up = wide[:, at : at + HALF], wide[:, at + HALF : at + both]
            acts.append((gate / (1.0 + jnp.exp(-gate)) * up).astype(BF16))
        act = jnp.concatenate(acts, axis=1)
        if s == 0:
            come[2].wait()
            come[3].wait()
        total = jnp.dot(act, tall_ref[...], preferred_element_type=F32)
        made_ref[s] = total.astype(BF16).reshape(step, ROWS, D)
        leave.append(
            pltpu.make_async_copy(
                made_ref.at[s], out_ref.at[s * step : (s + 1) * step], left_sem.at[s]
            )
        )
        leave[-1].start()
    for copy in leave:
        copy.wait()


def on_core(array):
    return pltpu.with_memory_space_constraint(array, pltpu.VMEM)


def expert(rows, *weights):
    apart = pl.BlockSpec(memory_space=pltpu.HBM)
    return call(
        expert_kernel,
        "expert",
        shape(rows.shape),
        5,
        in_specs=whole(1) + [apart] * 4,
        out_specs=apart,
        limit=VMEM_MOST,
        scratch_shapes=[
            pltpu.VMEM((D, 4 * HALF), BF16),
            pltpu.VMEM((2 * HALF, D), BF16),
            pltpu.VMEM((EXPERT_STEPS, REACH // EXPERT_STEPS, ROWS, D), BF16),
            pltpu.SemaphoreType.DMA((4,)),
            pltpu.SemaphoreType.DMA((EXPERT_STEPS,)),
        ],
    )(on_core(rows), *weights)


def write_states(ref, r, states):
    lane, row = iota((HEADS, HEAD), 1), iota((HEADS, HEAD), 0)
    line = iota((STAT, HEAD), 0)
    stats = jnp.zeros((STAT, HEAD), F32)
    for i, (top, total, mixed) in enumerate(states):
        ref[r, i * HEADS : (i + 1) * HEADS, :] = mixed.astype(BF16)
        flat = jnp.where(lane == row, top, 0.0) + jnp.where(lane == row + HEADS, total, 0.0)
        flat = jnp.sum(flat, axis=0, keepdims=True)
        for part, value in enumerate(split(flat)):
            stats = jnp.where(line == i * 3 + part, value.astype(F32), stats)
    ref[r, REQUESTS * HEADS :, :] = stats.astype(BF16)


def read_state(ref, r, i):
    lane, row = iota((HEADS, HEAD), 1), iota((HEADS, HEAD), 0)
    stats = ref[r, REQUESTS * HEADS :, :].astype(F32)
    flat = stats[i * 3 : i * 3 + 1] + stats[i * 3 + 1 : i * 3 + 2] + stats[i * 3 + 2 : i * 3 + 3]
    top = jnp.sum(jnp.where(lane == row, flat, 0.0), axis=1, keepdims=True)
    total = jnp.sum(jnp.where(lane == row + HEADS, flat, 0.0), axis=1, keepdims=True)
    return top, total, ref[r, i * HEADS : (i + 1) * HEADS, :].astype(F32)


def merged(states):
    best = states[0][0]
    for top, _, _ in states[1:]:
        best = jnp.maximum(best, top)
    sums, acc = 0.0, 0.0
    for top, total, mixed in states:
        factor = jnp.exp(top - best)
        sums = sums + factor * total
        acc = acc + factor * mixed
    return best, sums, acc


def merge_kernel(got0_ref, got1_ref, got2_ref, got3_ref, *sends):
    refs = (got0_ref, got1_ref, got2_ref, got3_ref)
    for r in range(SIDE):
        write_states(
            sends[r],
            0,
            [merged([read_state(ref, r, i) for ref in refs]) for i in range(REQUESTS)],
        )


def pair(x_first, dz, dx):
    return jnp.where(x_first, dz * 4 + dx, dx * 4 + dz)


def partial_kernel(owner_ref, count_ref, query_ref, pool_ref, *refs):
    sends, (top_ref, sum_ref, acc_ref) = refs[:SIDE], refs[SIDE:]
    scale = 1.0 / math.sqrt(HEAD)
    top_ref[...] = jnp.full(top_ref.shape, NEG, F32)
    sum_ref[...] = jnp.zeros(sum_ref.shape, F32)
    acc_ref[...] = jnp.zeros(acc_ref.shape, F32)
    x, zl, _, _, c = position(lax.axis_index(AXIS))
    x_first = c == 1
    per = HEADS // GROUPS
    own = iota((HEADS, KV), 1) // HEAD == iota((HEADS, KV), 0) // per
    slot = iota((HEADS, LEN), 1)
    for b in range(BLOCKS):
        owner = owner_ref[b]
        ax, az, request = owner >> 3, (owner >> 1) & 3, owner & 1
        first = jnp.where(x_first, ax ^ x, az ^ zl)
        second = jnp.where(x_first, (zl - az) & 3, (x - ax) & 3)
        asked = (second * 4 + (first & 1) * 2 + (first >> 1)) * 2 + request
        state = pair(x_first, (az - zl) & 3, (ax - x) & 3) * 2 + request
        rows = pl.ds(pl.multiple_of(state * HEADS, HEADS), HEADS)
        query = query_ref[pl.ds(pl.multiple_of(asked * HEADS, HEADS), HEADS), :]
        wide = jnp.where(own, jnp.concatenate([query] * GROUPS, axis=1), jnp.zeros((), BF16))
        score = (
            lax.dot_general(
                wide, pool_ref[b, :, :KV], (((1,), (1,)), ((), ())), preferred_element_type=F32
            )
            * scale
        )
        keep = slot < count_ref[b]
        score = jnp.where(keep, score, NEG)
        top = jnp.max(score, axis=1, keepdims=True)
        weight = jnp.where(keep, jnp.exp(score - top), 0.0)
        total = jnp.sum(weight, axis=1, keepdims=True)
        high, low, _ = split(weight)
        mixed = jnp.dot(
            jnp.concatenate([high, low], axis=0), pool_ref[b, :, KV:], preferred_element_type=F32
        )
        mixed = mixed[:HEADS] + mixed[HEADS:]
        mixed = jnp.concatenate(
            [mixed[g * per : (g + 1) * per, g * HEAD : (g + 1) * HEAD] for g in range(GROUPS)],
            axis=0,
        )
        old = top_ref[rows, :]
        best = jnp.maximum(old, top)
        keep_old, add_new = jnp.exp(old - best), jnp.exp(top - best)
        top_ref[rows, :] = best
        sum_ref[rows, :] = keep_old * sum_ref[rows, :] + add_new * total
        acc_ref[rows, :] = keep_old * acc_ref[rows, :] + add_new * mixed
    for r in range(SIDE * SIDE):
        states = []
        for i in range(REQUESTS):
            at = (r * REQUESTS + i) * HEADS
            rows = slice(at, at + HEADS)
            states.append((top_ref[rows, :], sum_ref[rows, :], acc_ref[rows, :]))
        write_states(sends[r // SIDE], r % SIDE, states)


def partial_attention(owner, count, queries, pool):
    smem = pl.BlockSpec(memory_space=pltpu.SMEM)
    return call(
        partial_kernel,
        "partial_attention",
        [shape((SIDE, MESSAGE, HEAD))] * SIDE,
        4,
        in_specs=[smem, smem] + whole(2),
        out_specs=whole(SIDE),
        scratch_shapes=[pltpu.VMEM((SIDE * SIDE * REQUESTS * HEADS, HEAD), F32)] * 3,
    )(owner, count, queries, pool)


def finish_kernel(got0_ref, got1_ref, got2_ref, got3_ref, query_ref, new_ref, out_ref):
    scale = 1.0 / math.sqrt(HEAD)
    per = HEADS // GROUPS

    def by_head(line):
        return jnp.concatenate(
            [
                jnp.broadcast_to(line[:, g * HEAD : (g + 1) * HEAD], (per, HEAD))
                for g in range(GROUPS)
            ],
            axis=0,
        )

    answers = []
    for i in range(REQUESTS):
        query = query_ref[i * HEADS : (i + 1) * HEADS, :].astype(F32)
        key = by_head(new_ref[i : i + 1, :KV].astype(F32))
        value = by_head(new_ref[i : i + 1, KV:].astype(F32))
        own = jnp.sum(query * key, axis=1, keepdims=True) * scale
        states = [(own, jnp.ones((HEADS, 1), F32), value)]
        states += [read_state(ref, 0, i) for ref in (got0_ref, got1_ref, got2_ref, got3_ref)]
        _, total, mixed = merged(states)
        answers.append(mixed / total)
    for h in range(HEADS):
        pair = jnp.concatenate([part[h : h + 1] for part in answers], axis=0)
        out_ref[:, h * HEAD : (h + 1) * HEAD] = pair.astype(BF16)


def along(array, axis):
    return [array] + [moved(array, **{axis: k}) for k in range(1, SIDE)]


def spread(arrays, axis):
    return [moved(array, **{axis: k}) if k else array for k, array in enumerate(arrays)]


def shards(
    moe_input,
    expert_ids,
    route_weight,
    expert_slot,
    w_gate_up,
    w_down,
    queries,
    incoming_key_value,
    key_value_pool,
    block_owner,
    block_tokens,
):
    slot_row = expert_slot.reshape(1, SLOTS)
    packed = call(pack_kernel, "pack", shape((RING, TOK, D + EXTRA)), 3, limit=VMEM_ALL)(
        moe_input, expert_ids.T, route_weight.T
    )
    own_queries = queries.reshape(REQUESTS * HEADS, HEAD)
    near = exchange(packed, RING_GROUPS)
    half = jnp.concatenate([own_queries, swapped(own_queries, 2)], axis=0)
    rest = swapped(half, 1)
    send = dispatch(near, slot_row)
    send, rest = lax.optimization_barrier((send, rest))
    line = jnp.concatenate([half, rest], axis=0)
    received = exchange(send, REACH_GROUPS)

    other_gate_up, other_down = moved(w_gate_up, core=1), moved(w_down, core=1)
    square = along(line, "second")
    rows = expert(
        received, w_gate_up, other_gate_up, w_down, other_down
    )
    rows, square = lax.optimization_barrier((rows, square))
    returned = exchange(rows, REACH_GROUPS)

    partials = partial_attention(
        block_owner, block_tokens, jnp.concatenate(square, axis=0), key_value_pool
    )
    across = spread(partials, "second")
    mix = call(mixing_kernel, "mixing", shape((2 * NEAR, REACH * ROWS)), 2)(near, slot_row)
    parts = call(combine_kernel, "combine", shape((RING, TOK, D)), 2)(mix, on_core(returned))
    parts, across = lax.optimization_barrier((parts, across))
    parts = exchange(parts, RING_GROUPS)

    met = call(
        merge_kernel,
        "merge",
        [shape((1, MESSAGE, HEAD))] * SIDE,
        4,
        out_specs=whole(SIDE),
    )(*across)
    attn_out = call(finish_kernel, "finish", shape((REQUESTS, HEADS * HEAD)), 6)(
        *spread(met, "first"), own_queries, incoming_key_value
    )
    moe_out = call(total_kernel, "total", shape((TOK, D)), 1)(parts)
    return (moe_out, attn_out)


def solution(mesh):
    flat = Mesh(mesh.devices.reshape(-1), (AXIS,))
    rows = P(AXIS, None)
    placed = (
        rows,
        rows,
        rows,
        P(),
        P(None, AXIS),
        rows,
        rows,
        rows,
        P(AXIS, None, None),
        P(AXIS),
        P(AXIS),
    )
    return jax.shard_map(
        shards, mesh=flat, in_specs=placed, out_specs=(rows, rows), check_vma=False
    )
```
